128 devices in a mesh: wide: 32 (over x, z, core), narrow: 4 (over y).
Axes of the slice: x: 4, y: 4, z: 4, core: 2. Of those that a mesh axis runs over, the one named last changes fastest.
Arguments:
- front: bfloat16 [4, 32, 128, 32, 4, 128], P(None, 'wide', None, None, 'narrow'), may hold values from -6 to 6
- pivot_inverse: bfloat16 [4, 128, 128], replicated, may hold values from -0.0105112052 to 0.17838107
- rhs: bfloat16 [4, 32, 128, 256], P(None, 'wide'), may hold values from -6 to 6
- trail_sol: bfloat16 [4, 32, 128, 256], P(None, 'wide'), may hold values from -1.1953125 to 1.1953125
- block_mask: int32 [4, 32, 32, 4], P(None, 'wide', None, 'narrow'), may hold values 0 or 1
- panel_order: int32 [4], replicated, may hold values from 0 to 3, each once
Outputs:
- front_out: bfloat16 [4, 32, 128, 32, 4, 128], P(None, 'wide', None, None, 'narrow')
- forward_rhs: bfloat16 [4, 32, 128, 256], P(None, 'wide')
- window_solution: bfloat16 [4, 128, 256], replicated
The draws below stay inside these ranges and needn't reach their ends.
Inputs may be any that keep to these rules, and one draw needn't show every extreme that they name: `panel_order`: each value 0 to 3 appears once.
All inputs are finite; a program needn't handle non-finite values. No bound on the sum of `block_mask` on one device may be relied on, other than what follows from the above.
Results may differ from the reference program's by a relative error of at most 0.0076.
Values may be sent and summed in bfloat16 or wider, within the bound.
No kernel may reach another device: no remote copies, remote signals or barrier semaphores. Data moves between devices by JAX's collectives and lax.ppermute only.
A program may use at most 64 MiB of HBM per device.

```python
import math
import jax
import jax.numpy as jnp
from jax import lax

BS = 128
NBLK = 128
NRHS = 256
PANELS = 4
RLOC = 4
CLOC = 32
N_WIDE = 32
N_NARROW = 4


def draw_pivot_inverse(key, part):
    inner = jax.random.fold_in(key, 7177)
    key_diag, key_off = jax.random.split(inner)
    scale = 0.5 * BS ** (-0.25)
    spread = 0.2 / math.sqrt(BS)
    diag = jax.random.uniform(key_diag, (PANELS, BS), jnp.float32, 0.9, 1.1)
    noise = jnp.clip(jax.random.normal(key_off, (PANELS, BS, BS), jnp.float32), -4.0, 4.0) * spread
    rows_index = lax_iota_rows()
    cols_index = lax_iota_cols()
    on_diag = (rows_index == cols_index)[None, :, :]
    matrix = jnp.where(on_diag, diag[:, :, None], noise)
    return (scale * matrix).astype(jnp.bfloat16)


def lax_iota_rows():
    return jnp.arange(BS, dtype=jnp.int32)[:, None] + jnp.zeros((1, BS), jnp.int32)


def lax_iota_cols():
    return jnp.arange(BS, dtype=jnp.int32)[None, :] + jnp.zeros((BS, 1), jnp.int32)


def set_ends(array, rng, least, high):
    index_at = [jax.random.randint(jax.random.fold_in(rng, axis), (), 0, length) for axis, length in enumerate(array.shape)]
    main_axis = array.shape.index(max(array.shape))
    neighbour = index_at[:main_axis] + [(index_at[main_axis] + 1) % array.shape[main_axis]] + index_at[main_axis + 1:]
    return array.at[tuple(index_at)].set(least).at[tuple(neighbour)].set(high)


def level_of(key, dims, cuts, least, largest):
    loudness, own = 1.0, jax.random.fold_in(key, 6)
    for axis_at, blocks in cuts:
        heights = jnp.exp(jax.random.uniform(jax.random.fold_in(own, axis_at), (blocks,), jnp.float32, least / len(cuts), largest / len(cuts)))
        loudness = loudness * jnp.repeat(heights, dims[axis_at] // blocks).reshape([-1 if axis == axis_at else 1 for axis in range(len(dims))])
    return loudness


def centred(stream_key, shape, scale, limit, pieces=(), kind=jnp.bfloat16):
    loudness = level_of(stream_key, shape, pieces, -0.22, 0.18) if pieces else 1.0
    array = jax.random.normal(stream_key, shape, jnp.float32) * scale * loudness
    return jnp.minimum(jnp.maximum(array, -limit), limit).astype(kind)


def setup_inputs(seed: int = 0) -> dict:
    key_of = jax.random.split(jax.random.key(seed), 7)
    front = centred(key_of[0], (RLOC, N_WIDE, BS, CLOC, N_NARROW, BS), 1.0, 6.0, ((1, 32), (4, 4)))
    pivot_inverse = draw_pivot_inverse(jax.random.fold_in(key_of[6], 71), 0)
    rhs = centred(key_of[2], (RLOC, N_WIDE, BS, NRHS), 1.0, 6.0, ((1, 32),))
    trail_sol = centred(key_of[3], (RLOC, N_WIDE, BS, NRHS), 0.2, 1.1953125, ((1, 32),))
    block_mask = set_ends((jax.random.randint(key_of[4], (RLOC, N_WIDE, CLOC, N_NARROW), 0, 5) < 4).astype(jnp.int32), jax.random.fold_in(key_of[4], 1), 0, 1)
    panel_order = jax.random.permutation(key_of[5], PANELS).astype(jnp.int32)
    return {"front": front, "pivot_inverse": pivot_inverse, "rhs": rhs, "trail_sol": trail_sol, "block_mask": block_mask, "panel_order": panel_order}


def reference(front, pivot_inverse, rhs, trail_sol, block_mask, panel_order):
    blocks = front.reshape(NBLK, BS, NBLK, BS)
    pattern = block_mask.reshape(NBLK, NBLK).astype(jnp.float32)
    right = rhs.reshape(NBLK, BS, NRHS)
    trailing = trail_sol.reshape(NBLK, BS, NRHS)
    ranks = jnp.full((NBLK,), PANELS, jnp.int32).at[panel_order].set(jnp.arange(PANELS, dtype=jnp.int32))
    saved_left = []
    saved_pivot = []
    for section in range(PANELS):
        target = panel_order[section]
        weight = lax.dynamic_index_in_dim(pivot_inverse, target, 0, keepdims=False).astype(jnp.float32)
        alive = ranks > section
        column = lax.dynamic_index_in_dim(blocks, target, 2, keepdims=False).astype(jnp.float32)
        left = jnp.einsum('iab,bc->iac', column, weight)
        left = jnp.where(alive[:, None, None], left, 0.0).astype(jnp.bfloat16)
        row_blocks = lax.dynamic_index_in_dim(blocks, target, 0, keepdims=False).astype(jnp.float32)
        upper = jnp.einsum('ac,ajb->cjb', weight, row_blocks)
        upper = jnp.where(alive[None, :, None], upper, 0.0).astype(jnp.bfloat16)
        upper_f = upper.astype(jnp.float32)

        def update_one(packed):
            a_row, l_row, m_row = packed
            product = jnp.einsum('ac,cjb->ajb', l_row.astype(jnp.float32), upper_f)
            return (a_row.astype(jnp.float32) - m_row[None, :, None] * product).astype(jnp.bfloat16)

        blocks = lax.map(update_one, (blocks, left, pattern))
        pivot_rhs = lax.dynamic_index_in_dim(right, target, 0, keepdims=False).astype(jnp.float32)
        solved = jnp.einsum('ac,an->cn', weight, pivot_rhs).astype(jnp.bfloat16)
        right = (right.astype(jnp.float32) - jnp.einsum('iac,cn->ian', left.astype(jnp.float32), solved.astype(jnp.float32))).astype(jnp.bfloat16)
        saved_left.append(left)
        saved_pivot.append(solved)
    current = trailing
    window = jnp.zeros((PANELS, BS, NRHS), jnp.bfloat16)
    for section in reversed(range(PANELS)):
        target = panel_order[section]
        weight = lax.dynamic_index_in_dim(pivot_inverse, target, 0, keepdims=False).astype(jnp.float32)
        total = jnp.einsum('iac,ian->cn', saved_left[section].astype(jnp.float32), current.astype(jnp.float32))
        corrected = (saved_pivot[section].astype(jnp.float32) - total).astype(jnp.bfloat16)
        result = jnp.einsum('ac,cn->an', weight, corrected.astype(jnp.float32)).astype(jnp.bfloat16)
        current = lax.dynamic_update_index_in_dim(current, result, target, 0)
        window = lax.dynamic_update_index_in_dim(window, result, target, 0)
    return blocks.reshape(front.shape), right.reshape(rhs.shape), window
```

```python
import jax
import jax.numpy as jnp
from jax import lax
from jax.experimental import pallas as pl
from jax.experimental.pallas import tpu as pltpu
from jax.sharding import PartitionSpec as P

BF = jnp.bfloat16
F32 = jnp.float32
BS = 128
NP = 4
NR = 4
NC = 32
NRHS = 256
NW = 32
PIECES = 8
CPP = NC // PIECES
SUB = 16
EXTRA = SUB + 8 + 8


def dot(a, b, ca=1, cb=0):
    return lax.dot_general(a, b, (((ca,), (cb,)), ((), ())), preferred_element_type=F32)


def ranks_of(order, w):
    rank = [sum(jnp.where(order[s] == i, s, 0) for s in range(NP)) for i in range(NP)]
    own = jnp.int32(NP)
    for i in range(NP):
        own = jnp.where(w == i, rank[i], own)
    return rank, own


def panel_kernel(order, meta, mpan, own, d1, d2, d3, got, w_ref, b_ref, y_ref,
                 lown, lpiv, zt, frhs, tpart, pan, bs, ztall):
    w, q = meta[0], meta[1]
    rank, own_rank = ranks_of(order, w)
    for d, ref in enumerate((own, d1, d2, d3)):
        pan[lax.rem(q - d + 4, 4), 0 : NR * BS] = ref[0 : NR * BS]
    for k in range(NP):
        for i in range(NP):
            for p in range(PIECES):
                pan[k, NR * BS + i * BS + p * SUB : NR * BS + i * BS + (p + 1) * SUB] = got[4 * p + i, k, 0:SUB]
    for r in range(NR):
        bs[r] = b_ref[r].astype(F32)
    for i in range(NP):
        for p in range(PIECES):
            for n in range(4):
                r0 = p * SUB + 8 * (n >> 1)
                c0 = 128 * (n & 1)
                bs[NR + i, r0 : r0 + 8, c0 : c0 + 128] = got[4 * p + i, n, SUB : SUB + 8].astype(F32)
    row_rank = [own_rank, None, None, None] + rank
    for s in range(NP):
        k = order[s]
        weight = w_ref[k]
        left = dot(pan[k], weight)
        parts = []
        for i in range(NR + NP):
            part = left[i * BS : (i + 1) * BS]
            if row_rank[i] is not None:
                part = jnp.where(row_rank[i] > s, part, 0.0)
            parts.append(part.astype(BF))
        lb = jnp.concatenate(parts, axis=0)
        lown[:, s * BS : (s + 1) * BS] = lb[: NR * BS]
        lpiv[s] = lb[NR * BS :]
        if s + 1 < NP:
            uppers = []
            for j in range(NP):
                akj = pan[j, pl.ds(pl.multiple_of(NR * BS + k * BS, BS), BS), :]
                upper = dot(weight, akj, 0, 0)
                uppers.append(jnp.where(rank[j] > s, upper, 0.0).astype(BF))
            for j in range(NP):
                prod = dot(lb, uppers[j])
                for i in range(NR + NP):
                    sl = slice(i * BS, (i + 1) * BS)
                    pan[j, sl] = (pan[j, sl].astype(F32) - mpan[i * NP + j] * prod[sl]).astype(BF)
        bk = bs[NR + k].astype(BF)
        z = dot(weight, bk, 0, 0).astype(BF)
        ztall[...] = dot(bk, weight, 0, 0).astype(BF).astype(F32)
        zt[s] = ztall[pl.ds(pl.multiple_of(w * 8, 8), 8), :]
        elim = dot(lb, z)
        for i in range(NR + NP):
            bs[i] = (bs[i] - elim[i * BS : (i + 1) * BS]).astype(BF).astype(F32)
    for r in range(NR):
        frhs[r] = bs[r].astype(BF)
    y0 = jnp.where(w < NP, jnp.zeros_like(y_ref[0]), y_ref[0])
    y = jnp.concatenate([y0] + [y_ref[r] for r in range(1, NR)], axis=0)
    tpart[...] = dot(y, lown[...], 0, 0)


def solve_kernel(order, parts, zt, lpiv, w_ref, out, xs):
    total = jnp.sum(parts[...], axis=0)
    xs[...] = jnp.zeros_like(xs)
    for s in reversed(range(NP)):
        k = order[s]
        acc = total[:, s * BS : (s + 1) * BS]
        if s + 1 < NP:
            for i in range(NP):
                acc = acc + dot(xs[i].astype(BF), lpiv[s, i * BS : (i + 1) * BS, :])
        c = (zt[s] - acc).astype(BF)
        xs[k] = dot(c, w_ref[k], 1, 1).astype(BF).astype(F32)
    x = jnp.concatenate([xs[i] for i in range(NP)], axis=1).astype(BF)
    for d in range(NW):
        out[d] = x


GC = 8


def update_kernel(order, meta, mown, mpiv, a_ref, u_ref, w_ref, lown, lpiv, out, aw, us):
    g = pl.program_id(0)
    q = meta[1]
    rank, _ = ranks_of(order, meta[0])
    qrank = jnp.int32(0)
    for i in range(NP):
        qrank = jnp.where(q == i, rank[i], qrank)
    for col in range(GC):
        for k in range(NP):
            aw[k, :, col * BS : (col + 1) * BS] = u_ref[col // CPP, k, col % CPP]
    for s in range(NP):
        k = order[s]
        upper = dot(w_ref[k], aw[k], 0, 0)
        first = jnp.where((g == 0) & (qrank <= s), 0.0, upper[:, :BS])
        ub = jnp.concatenate([first, upper[:, BS:]], axis=1).astype(BF)
        us[s * BS : (s + 1) * BS, :] = ub
        for t in range(s + 1, NP):
            k2 = order[t]
            prod = dot(lpiv[s, pl.ds(pl.multiple_of(k2 * BS, BS), BS), :], ub)
            for col in range(GC):
                sl = slice(col * BS, (col + 1) * BS)
                m = mpiv[k2 * NC + g * GC + col]
                aw[k2, :, sl] = (aw[k2, :, sl].astype(F32) - m * prod[:, sl]).astype(BF)
    rows = lax.broadcasted_iota(jnp.int32, (BS, BS), 0)
    cols = lax.broadcasted_iota(jnp.int32, (BS, BS), 1)
    perm = jnp.where((rows % GC) * SUB + rows // GC == cols, 1.0, 0.0).astype(BF)
    for r in range(NR):
        lu = dot(lown[r * BS : (r + 1) * BS, :], us[...])
        blocks = []
        for col in range(GC):
            m = mown[r * NC + g * GC + col]
            blocks.append((m * lu[:, col * BS : (col + 1) * BS]).astype(BF))
        for ag in range(BS // SUB):
            sl = slice(ag * SUB, (ag + 1) * SUB)
            stack = jnp.concatenate([b[sl] for b in blocks], axis=0)
            delta = dot(perm, stack).reshape(SUB, GC, BS)
            out[r, sl] = (a_ref[r, sl].astype(F32) - delta).astype(BF)


def vmem(n):
    return [pl.BlockSpec(memory_space=pltpu.VMEM)] * n


def smem(n):
    return [pl.BlockSpec(memory_space=pltpu.SMEM)] * n


def body(front, pivot_inverse, rhs, trail_sol, block_mask, panel_order):
    w, q = lax.axis_index("wide"), lax.axis_index("narrow")
    meta = jnp.stack([w, q]).astype(jnp.int32)
    blocks = front.reshape(NR, BS, NC, BS)
    mask = block_mask.reshape(NR, NC)
    b = rhs.reshape(NR, BS, NRHS)
    y = trail_sol.reshape(NR, BS, NRHS)

    mine = blocks[:, :, 0, :].reshape(NR * BS, BS)
    mrow = jnp.broadcast_to(jnp.pad(mask[:, :1], ((0, 4), (0, 0))).astype(BF), (8, BS))
    mine = jnp.concatenate([mine, mrow], axis=0)
    others = [lax.ppermute(mine, "narrow", [(i, (i + d) % 4) for i in range(4)]) for d in (1, 2, 3)]

    urows = blocks[0].reshape(BS, PIECES, CPP, BS).transpose(1, 2, 0, 3).reshape(PIECES, CPP * BS, BS)
    prow = blocks[0, :, 0, :].reshape(PIECES, SUB, BS)
    tiles = b[0].reshape(PIECES, 2, 8, 2, BS)
    tile = lax.dynamic_index_in_dim(tiles, q // 2, 1, keepdims=False)
    tile = lax.dynamic_index_in_dim(tile, q % 2, 2, keepdims=False)
    mline = jnp.pad(mask[0].astype(BF), (0, BS - NC))
    mline = jnp.broadcast_to(mline[None, None, :], (PIECES, 8, BS))
    groups = [[4 * p + i for p in range(PIECES)] for i in range(NP)]
    sent = jnp.concatenate([urows, prow, tile, mline], axis=1)
    got = lax.all_to_all(sent, "wide", 0, 0, axis_index_groups=groups)[0]

    ugath = lax.all_gather(got[: CPP * BS], "wide").reshape(PIECES, NP, CPP, BS, BS)

    small = jnp.broadcast_to(got[None, CPP * BS :], (NW * 4, EXTRA, BS))
    small = lax.all_to_all(small, ("wide", "narrow"), 0, 0).reshape(NW, 4, EXTRA, BS)

    mlines = small[:NP, :, SUB + 8, :NC].astype(F32)
    mpiv = lax.dynamic_index_in_dim(mlines, q, 1, keepdims=False).reshape(NP * NC)
    own_cols = jnp.stack([mine[NR * BS :, 0]] + [o[NR * BS :, 0] for o in others])[:, :NR]
    own_cols = own_cols[jnp.mod(q - jnp.arange(4), 4)]
    mpan = jnp.concatenate([own_cols.T.astype(F32), mlines[:, :, 0]], axis=0).reshape(-1)
    mown = mask.astype(F32).reshape(-1)

    lown, lpiv, zt, frhs, tpart = pl.pallas_call(
        panel_kernel,
        out_shape=(
            jax.ShapeDtypeStruct((NR * BS, NP * BS), BF),
            jax.ShapeDtypeStruct((NP, NP * BS, BS), BF),
            jax.ShapeDtypeStruct((NP, 8, BS), F32),
            jax.ShapeDtypeStruct((NR, BS, NRHS), BF),
            jax.ShapeDtypeStruct((NRHS, NP * BS), F32),
        ),
        in_specs=smem(3) + vmem(8),
        out_specs=tuple(vmem(5)),
        scratch_shapes=[
            pltpu.VMEM((NP, (NR + NP) * BS, BS), BF),
            pltpu.VMEM((NR + NP, BS, NRHS), F32),
            pltpu.VMEM((NRHS, BS), F32),
        ],
        name="panel",
    )(panel_order, meta, mpan, mine, *others, small, pivot_inverse, b, y)

    tparts = lax.all_to_all(tpart.reshape(NW, 8, NP * BS), "wide", 0, 0)
    xg = pl.pallas_call(
        solve_kernel,
        out_shape=jax.ShapeDtypeStruct((NW, 8, NP * BS), BF),
        in_specs=smem(1) + vmem(4),
        out_specs=vmem(1)[0],
        scratch_shapes=[pltpu.VMEM((NP, 8, BS), F32)],
        name="solve",
    )(panel_order, tparts, zt, lpiv, pivot_inverse)
    xall = lax.all_to_all(xg, "wide", 0, 0).reshape(NRHS, NP * BS)
    window = xall.T.reshape(NP, BS, NRHS)

    fixed2 = lambda shape: pl.BlockSpec(shape, lambda g: (0,) * len(shape))
    front_out = pl.pallas_call(
        update_kernel,
        out_shape=jax.ShapeDtypeStruct((NR, BS, NC, BS), BF),
        grid=(NC // GC,),
        in_specs=smem(4)
        + [
            pl.BlockSpec((NR, BS, GC, BS), lambda g: (0, 0, g, 0)),
            pl.BlockSpec((GC // CPP, NP, CPP, BS, BS), lambda g: (g, 0, 0, 0, 0)),
            fixed2((NP, BS, BS)),
            fixed2((NR * BS, NP * BS)),
            fixed2((NP, NP * BS, BS)),
        ],
        out_specs=pl.BlockSpec((NR, BS, GC, BS), lambda g: (0, 0, g, 0)),
        scratch_shapes=[
            pltpu.VMEM((NP, BS, GC * BS), BF),
            pltpu.VMEM((NP * BS, GC * BS), BF),
        ],
        name="update",
    )(panel_order, meta, mown, mpiv, blocks, ugath, pivot_inverse, lown, lpiv)
    return front_out.reshape(front.shape), frhs.reshape(rhs.shape), window


def solution(mesh):
    in_specs = (
        P(None, "wide", None, None, "narrow", None),
        P(),
        P(None, "wide", None, None),
        P(None, "wide", None, None),
        P(None, "wide", None, "narrow"),
        P(),
    )
    out_specs = (P(None, "wide", None, None, "narrow", None), P(None, "wide", None, None), P())
    return jax.shard_map(body, mesh=mesh, in_specs=in_specs, out_specs=out_specs, check_vma=False)
```

```python
import jax
import jax.numpy as jnp
from jax import lax
from jax.experimental import pallas as pl
from jax.experimental.pallas import tpu as pltpu
from jax.sharding import PartitionSpec as P

BF = jnp.bfloat16
F32 = jnp.float32
BS = 128
NP = 4
NR = 4
NC = 32
NRHS = 256
NW = 32
PIECES = 8
CPP = NC // PIECES
SUB = 16
EXTRA = SUB + 8 + 8


def holder(p, i):
    z = i >> 1 if p % 2 == 0 else 3 - (i >> 1)
    return (p >> 1) * 8 + z * 2 + (i & 1)


def dot(a, b, ca=1, cb=0):
    return lax.dot_general(a, b, (((ca,), (cb,)), ((), ())), preferred_element_type=F32)


def ranks_of(order, w):
    rank = [sum(jnp.where(order[s] == i, s, 0) for s in range(NP)) for i in range(NP)]
    own = jnp.int32(NP)
    for i in range(NP):
        own = jnp.where(w == i, rank[i], own)
    return rank, own


def panel_kernel(order, meta, mpan, own, d1, d2, d3, got, w_ref, b_ref, y_ref,
                 lown, lpiv, zt, frhs, tpart, delta, pan, bs, ztall):
    w, q = meta[0], meta[1]
    rank, own_rank = ranks_of(order, w)
    for d, ref in enumerate((own, d1, d2, d3)):
        pan[lax.rem(q - d + 4, 4), 0 : NR * BS] = ref[0 : NR * BS]
    for k in range(NP):
        for i in range(NP):
            for p in range(PIECES):
                pan[k, NR * BS + i * BS + p * SUB : NR * BS + i * BS + (p + 1) * SUB] = got[holder(p, i), k, 0:SUB]
    for r in range(NR):
        bs[r] = b_ref[r].astype(F32)
    for i in range(NP):
        for p in range(PIECES):
            for n in range(4):
                r0 = p * SUB + 8 * (n >> 1)
                c0 = 128 * (n & 1)
                bs[NR + i, r0 : r0 + 8, c0 : c0 + 128] = got[holder(p, i), n, SUB : SUB + 8].astype(F32)
    row_rank = [own_rank, None, None, None] + rank
    for s in range(NP):
        k = order[s]
        weight = w_ref[k]
        left = dot(pan[k], weight)
        parts = []
        for i in range(NR + NP):
            part = left[i * BS : (i + 1) * BS]
            if row_rank[i] is not None:
                part = jnp.where(row_rank[i] > s, part, 0.0)
            parts.append(part.astype(BF))
        lb = jnp.concatenate(parts, axis=0)
        lown[:, s * BS : (s + 1) * BS] = lb[: NR * BS]
        lpiv[s] = lb[NR * BS :]
        if s + 1 < NP:
            uppers = []
            for j in range(NP):
                akj = pan[j, pl.ds(pl.multiple_of(NR * BS + k * BS, BS), BS), :]
                upper = dot(weight, akj, 0, 0)
                uppers.append(jnp.where(rank[j] > s, upper, 0.0).astype(BF))
            for j in range(NP):
                prod = dot(lb, uppers[j])
                for i in range(NR + NP):
                    sl = slice(i * BS, (i + 1) * BS)
                    pan[j, sl] = (pan[j, sl].astype(F32) - mpan[i * NP + j] * prod[sl]).astype(BF)
        bk = bs[NR + k].astype(BF)
        z = dot(weight, bk, 0, 0).astype(BF)
        ztall[...] = dot(bk, weight, 0, 0).astype(BF).astype(F32)
        zt[s] = ztall[pl.ds(pl.multiple_of(w * 8, 8), 8), :]
        elim = dot(lb, z)
        for i in range(NR + NP):
            bs[i] = (bs[i] - elim[i * BS : (i + 1) * BS]).astype(BF).astype(F32)
    for r in range(NR):
        frhs[r] = bs[r].astype(BF)
    delta[...] = (own[0 : NR * BS].astype(F32) - pan[q, 0 : NR * BS].astype(F32)).astype(BF)
    y0 = jnp.where(w < NP, jnp.zeros_like(y_ref[0]), y_ref[0])
    y = jnp.concatenate([y0] + [y_ref[r] for r in range(1, NR)], axis=0)
    tpart[...] = dot(y, lown[...], 0, 0)


def solve_kernel(order, parts, zt, lpiv, w_ref, out, xs):
    total = jnp.sum(parts[...], axis=0)
    xs[...] = jnp.zeros_like(xs)
    for s in reversed(range(NP)):
        k = order[s]
        acc = total[:, s * BS : (s + 1) * BS]
        if s + 1 < NP:
            for i in range(NP):
                acc = acc + dot(xs[i].astype(BF), lpiv[s, i * BS : (i + 1) * BS, :])
        c = (zt[s] - acc).astype(BF)
        xs[k] = dot(c, w_ref[k], 1, 1).astype(BF).astype(F32)
    x = jnp.concatenate([xs[i] for i in range(NP)], axis=1).astype(BF)
    for d in range(NW):
        out[d] = x


def combine_kernel(order, lown, lpiv, w_ref, h):
    def low(t, s):
        return lpiv[s, pl.ds(pl.multiple_of(order[t] * BS, BS), BS), :]

    def right(coeff, s):
        return dot(coeff.astype(BF), w_ref[order[s]], 1, 1).astype(BF)

    base = [lown[:, s * BS : (s + 1) * BS].astype(F32) for s in range(NP)]
    r3 = right(base[3], 3)
    r3_low = [dot(r3, low(3, s)) for s in range(3)]
    for m3 in range(2):
        c3 = [base[s] - r3_low[s] if m3 else base[s] for s in range(3)]
        r2 = right(c3[2], 2)
        r2_low = [dot(r2, low(2, s)) for s in range(2)]
        for m2 in range(2):
            c2 = [c3[s] - r2_low[s] if m2 else c3[s] for s in range(2)]
            r1 = right(c2[1], 1)
            r1_low = dot(r1, low(1, 0))
            for m1 in range(2):
                r0 = right(c2[0] - r1_low if m1 else c2[0], 0)
                pat = m1 + 2 * m2 + 4 * m3
                for s, block in enumerate((r0, r1, r2, r3)):
                    h[pat, :, s * BS : (s + 1) * BS] = block


GC = 8


def update_kernel(order, meta, mown, mpiv, a_ref, near, far, h, delta, out, rows_of):
    g = pl.program_id(0)
    core = meta[0] & 1
    for zg in range(2):
        for fz in range(2):
            z = zg if fz == 0 else 3 - zg
            for cc in range(CPP):
                rows_of[2 * zg + core, fz * CPP + cc] = near[0, z, cc]
                rows_of[2 * zg + 1 - core, fz * CPP + cc] = far[0, z, cc]
    rows = lax.broadcasted_iota(jnp.int32, (BS, BS), 0)
    cols = lax.broadcasted_iota(jnp.int32, (BS, BS), 1)
    perm = jnp.where((rows % GC) * SUB + rows // GC == cols, 1.0, 0.0).astype(BF)
    cols_out = []
    for col in range(GC):
        c = g * GC + col
        pat = mpiv[order[1] * NC + c] + 2 * mpiv[order[2] * NC + c] + 4 * mpiv[order[3] * NC + c]
        raw = jnp.concatenate([rows_of[order[s], col] for s in range(NP)], axis=0)
        lu = dot(h[pat], raw)
        parts = []
        for r in range(NR):
            parts.append(jnp.where(mown[r * NC + c] != 0, lu[r * BS : (r + 1) * BS], 0.0).astype(BF))
        if col == 0:
            parts = [jnp.where(g == 0, delta[r * BS : (r + 1) * BS], parts[r]) for r in range(NR)]
        cols_out.append(parts)
    for r in range(NR):
        for ag in range(BS // SUB):
            sl = slice(ag * SUB, (ag + 1) * SUB)
            stack = jnp.concatenate([cols_out[col][r][sl] for col in range(GC)], axis=0)
            change = dot(perm, stack).reshape(SUB, GC, BS)
            out[r, sl] = (a_ref[r, sl].astype(F32) - change).astype(BF)


def vmem(n):
    return [pl.BlockSpec(memory_space=pltpu.VMEM)] * n


def smem(n):
    return [pl.BlockSpec(memory_space=pltpu.SMEM)] * n


def body(front, pivot_inverse, rhs, trail_sol, block_mask, panel_order):
    w, q = lax.axis_index("wide"), lax.axis_index("narrow")
    meta = jnp.stack([w, q]).astype(jnp.int32)
    blocks = front.reshape(NR, BS, NC, BS)
    mask = block_mask.reshape(NR, NC)
    b = rhs.reshape(NR, BS, NRHS)
    y = trail_sol.reshape(NR, BS, NRHS)

    mine = blocks[:, :, 0, :].reshape(NR * BS, BS)
    mrow = jnp.broadcast_to(jnp.pad(mask[:, :1], ((0, 4), (0, 0))).astype(BF), (8, BS))
    mine = jnp.concatenate([mine, mrow], axis=0)
    others = [lax.ppermute(mine, "narrow", [(i, (i + d) % 4) for i in range(4)]) for d in (1, 2, 3)]

    urows = blocks[0].reshape(BS, PIECES, CPP, BS).transpose(1, 2, 0, 3).reshape(PIECES, CPP * BS, BS)
    prow = blocks[0, :, 0, :].reshape(PIECES, SUB, BS)
    tiles = b[0].reshape(PIECES, 2, 8, 2, BS)
    tile = lax.dynamic_index_in_dim(tiles, q // 2, 1, keepdims=False)
    tile = lax.dynamic_index_in_dim(tile, q % 2, 2, keepdims=False)
    mline = jnp.pad(mask[0].astype(BF), (0, BS - NC))
    mline = jnp.broadcast_to(mline[None, None, :], (PIECES, 8, BS))
    groups = [[holder(p, i) for p in range(PIECES)] for i in range(NP)]
    sent = jnp.concatenate([urows, prow, tile, mline], axis=1)
    got = lax.all_to_all(sent, "wide", 0, 0, axis_index_groups=groups)[0]

    same_core = [[v for v in range(NW) if v % 2 == c] for c in range(2)]
    copies = jnp.broadcast_to(got[None, : CPP * BS], (NW // 2, CPP * BS, BS))
    near = lax.all_to_all(copies, "wide", 0, 0, axis_index_groups=same_core)
    near = near.reshape(4, 4, CPP, BS, BS)
    far = lax.ppermute(near, "wide", [(v, v ^ 1) for v in range(NW)])

    small = jnp.broadcast_to(got[None, CPP * BS :], (NW * 4, EXTRA, BS))
    small = lax.all_to_all(small, ("wide", "narrow"), 0, 0).reshape(NW, 4, EXTRA, BS)

    mlines = small[:NP, :, SUB + 8, :NC]
    mpiv = lax.dynamic_index_in_dim(mlines, q, 1, keepdims=False).reshape(NP * NC).astype(jnp.int32)
    own_cols = jnp.stack([mine[NR * BS :, 0]] + [o[NR * BS :, 0] for o in others])[:, :NR]
    own_cols = own_cols[jnp.mod(q - jnp.arange(4), 4)]
    mpan = jnp.concatenate([own_cols.T.astype(F32), mlines[:, :, 0].astype(F32)], axis=0).reshape(-1)
    mown = mask.reshape(-1)

    lown, lpiv, zt, frhs, tpart, delta = pl.pallas_call(
        panel_kernel,
        out_shape=(
            jax.ShapeDtypeStruct((NR * BS, NP * BS), BF),
            jax.ShapeDtypeStruct((NP, NP * BS, BS), BF),
            jax.ShapeDtypeStruct((NP, 8, BS), F32),
            jax.ShapeDtypeStruct((NR, BS, NRHS), BF),
            jax.ShapeDtypeStruct((NRHS, NP * BS), F32),
            jax.ShapeDtypeStruct((NR * BS, BS), BF),
        ),
        in_specs=smem(3) + vmem(8),
        out_specs=tuple(vmem(6)),
        scratch_shapes=[
            pltpu.VMEM((NP, (NR + NP) * BS, BS), BF),
            pltpu.VMEM((NR + NP, BS, NRHS), F32),
            pltpu.VMEM((NRHS, BS), F32),
        ],
        name="panel",
    )(panel_order, meta, mpan, mine, *others, small, pivot_inverse, b, y)

    tparts = lax.all_to_all(tpart.reshape(NW, 8, NP * BS), "wide", 0, 0)
    xg = pl.pallas_call(
        solve_kernel,
        out_shape=jax.ShapeDtypeStruct((NW, 8, NP * BS), BF),
        in_specs=smem(1) + vmem(4),
        out_specs=vmem(1)[0],
        scratch_shapes=[pltpu.VMEM((NP, 8, BS), F32)],
        name="solve",
    )(panel_order, tparts, zt, lpiv, pivot_inverse)
    xall = lax.all_to_all(xg, "wide", 0, 0).reshape(NRHS, NP * BS)
    window = xall.T.reshape(NP, BS, NRHS)

    h = pl.pallas_call(
        combine_kernel,
        out_shape=jax.ShapeDtypeStruct((8, NR * BS, NP * BS), BF),
        in_specs=smem(1) + vmem(3),
        out_specs=vmem(1)[0],
        name="combine",
    )(panel_order, lown, lpiv, pivot_inverse)

    fixed2 = lambda shape: pl.BlockSpec(shape, lambda g: (0,) * len(shape))
    front_out = pl.pallas_call(
        update_kernel,
        out_shape=jax.ShapeDtypeStruct((NR, BS, NC, BS), BF),
        grid=(NC // GC,),
        in_specs=smem(4)
        + [
            pl.BlockSpec((NR, BS, GC, BS), lambda g: (0, 0, g, 0)),
            pl.BlockSpec((1, 4, CPP, BS, BS), lambda g: (g, 0, 0, 0, 0)),
            pl.BlockSpec((1, 4, CPP, BS, BS), lambda g: (g, 0, 0, 0, 0)),
            fixed2((8, NR * BS, NP * BS)),
            fixed2((NR * BS, BS)),
        ],
        out_specs=pl.BlockSpec((NR, BS, GC, BS), lambda g: (0, 0, g, 0)),
        scratch_shapes=[pltpu.VMEM((NP, GC, BS, BS), BF)],
        name="update",
    )(panel_order, meta, mown, mpiv, blocks, near, far, h, delta)
    return front_out.reshape(front.shape), frhs.reshape(rhs.shape), window


def solution(mesh):
    in_specs = (
        P(None, "wide", None, None, "narrow", None),
        P(),
        P(None, "wide", None, None),
        P(None, "wide", None, None),
        P(None, "wide", None, "narrow"),
        P(),
    )
    out_specs = (P(None, "wide", None, None, "narrow", None), P(None, "wide", None, None), P())
    return jax.shard_map(body, mesh=mesh, in_specs=in_specs, out_specs=out_specs, check_vma=False)
```

```python
import jax
import jax.numpy as jnp
from jax import lax
from jax.experimental import pallas as pl
from jax.experimental.pallas import tpu as pltpu
from jax.sharding import PartitionSpec as P

BF = jnp.bfloat16
F32 = jnp.float32
BS = 128
NP = 4
NR = 4
NC = 32
NRHS = 256
NW = 32
PIECES = 8
CPP = NC // PIECES
SUB = 16
EXTRA = SUB + 8 + 8


def holder(p, i):
    z = i >> 1 if p % 2 == 0 else 3 - (i >> 1)
    return (p >> 1) * 8 + z * 2 + (i & 1)


def dot(a, b, ca=1, cb=0):
    return lax.dot_general(a, b, (((ca,), (cb,)), ((), ())), preferred_element_type=F32)


def ranks_of(order, w):
    rank = [sum(jnp.where(order[s] == i, s, 0) for s in range(NP)) for i in range(NP)]
    own = jnp.int32(NP)
    for i in range(NP):
        own = jnp.where(w == i, rank[i], own)
    return rank, own


TROWS = 128


def panel_kernel(order, meta, own, d1, d2, d3, got, piece, w_ref, b_ref, y_ref,
                 lown, lpiv, zt, frhs, send, delta, pan, bs, ztall, mk):
    w, q = meta[0], meta[1]
    rank, own_rank = ranks_of(order, w)
    for d, ref in enumerate((own, d1, d2, d3)):
        k = lax.rem(q - d + 4, 4)
        pan[k, 0 : NR * BS] = ref[0 : NR * BS]
        mk[k] = ref[NR * BS : NR * BS + 8].astype(F32)
    for k in range(NP):
        for i in range(NP):
            for p in range(PIECES):
                pan[k, NR * BS + i * BS + p * SUB : NR * BS + i * BS + (p + 1) * SUB] = got[holder(p, i), k, 0:SUB]
    for d in range(NW // 2):
        send[d, : CPP * BS] = piece[...]
    for r in range(NR):
        bs[r] = b_ref[r].astype(F32)
    for i in range(NP):
        for p in range(PIECES):
            for n in range(4):
                r0 = p * SUB + 8 * (n >> 1)
                c0 = 128 * (n & 1)
                bs[NR + i, r0 : r0 + 8, c0 : c0 + 128] = got[holder(p, i), n, SUB : SUB + 8].astype(F32)
    row_rank = [own_rank, None, None, None] + rank
    for s in range(NP):
        k = order[s]
        weight = w_ref[k]
        left = dot(pan[k], weight)
        parts = []
        for i in range(NR + NP):
            part = left[i * BS : (i + 1) * BS]
            if row_rank[i] is not None:
                part = jnp.where(row_rank[i] > s, part, 0.0)
            parts.append(part.astype(BF))
        lb = jnp.concatenate(parts, axis=0)
        lown[:, s * BS : (s + 1) * BS] = lb[: NR * BS]
        lpiv[s] = lb[NR * BS :]
        if s + 1 < NP:
            uppers = []
            for j in range(NP):
                akj = pan[j, pl.ds(pl.multiple_of(NR * BS + k * BS, BS), BS), :]
                upper = dot(weight, akj, 0, 0)
                uppers.append(jnp.where(rank[j] > s, upper, 0.0).astype(BF))
            for j in range(NP):
                prod = dot(lb, uppers[j])
                for i in range(NR + NP):
                    sl = slice(i * BS, (i + 1) * BS)
                    if i < NR:
                        m = mk[j, i : i + 1, :]
                    else:
                        m = got[holder(0, i - NR), j, SUB + 8 : SUB + 16].astype(F32)[0:1, 0:1]
                    pan[j, sl] = (pan[j, sl].astype(F32) - m * prod[sl]).astype(BF)
        bk = bs[NR + k].astype(BF)
        z = dot(weight, bk, 0, 0).astype(BF)
        ztall[...] = dot(bk, weight, 0, 0).astype(BF).astype(F32)
        zt[s] = ztall[pl.ds(pl.multiple_of(w * 8, 8), 8), :]
        elim = dot(lb, z)
        for i in range(NR + NP):
            bs[i] = (bs[i] - elim[i * BS : (i + 1) * BS]).astype(BF).astype(F32)
    for r in range(NR):
        frhs[r] = bs[r].astype(BF)
    delta[...] = (own[0 : NR * BS].astype(F32) - pan[q, 0 : NR * BS].astype(F32)).astype(BF)
    y0 = jnp.where(w < NP, jnp.zeros_like(y_ref[0]), y_ref[0])
    y = jnp.concatenate([y0] + [y_ref[r] for r in range(1, NR)], axis=0)
    t = dot(y, lown[...], 0, 0)
    hi = t.astype(BF)
    lo = (t - hi.astype(F32)).astype(BF)
    for half, part in enumerate((hi, lo)):
        for s in range(NP):
            for d in range(NW // 2):
                row = CPP * BS + half * 64 + s * 16
                send[d, row : row + 16] = part[d * 16 : (d + 1) * 16, s * BS : (s + 1) * BS]


def solve_kernel(order, meta, near, far, zt, lpiv, w_ref, out, xs, both):
    tsum = jnp.sum(near[...].astype(F32), axis=0) + jnp.sum(far[...].astype(F32), axis=0)
    both[...] = tsum[:64] + tsum[64:]
    core = meta[0] & 1
    xs[...] = jnp.zeros_like(xs)
    for s in reversed(range(NP)):
        k = order[s]
        acc = both[pl.ds(pl.multiple_of(s * 16 + core * 8, 8), 8), :]
        if s + 1 < NP:
            for i in range(NP):
                acc = acc + dot(xs[i].astype(BF), lpiv[s, i * BS : (i + 1) * BS, :])
        c = (zt[s] - acc).astype(BF)
        xs[k] = dot(c, w_ref[k], 1, 1).astype(BF).astype(F32)
    x = jnp.concatenate([xs[i] for i in range(NP)], axis=1).astype(BF)
    for d in range(NW):
        out[d] = x


def combine_kernel(order, lown, lpiv, w_ref, h):
    def low(t, s):
        return lpiv[s, pl.ds(pl.multiple_of(order[t] * BS, BS), BS), :]

    def right(coeff, s):
        return dot(coeff.astype(BF), w_ref[order[s]], 1, 1).astype(BF)

    base = [lown[:, s * BS : (s + 1) * BS].astype(F32) for s in range(NP)]
    r3 = right(base[3], 3)
    r3_low = [dot(r3, low(3, s)) for s in range(3)]
    for m3 in range(2):
        c3 = [base[s] - r3_low[s] if m3 else base[s] for s in range(3)]
        r2 = right(c3[2], 2)
        r2_low = [dot(r2, low(2, s)) for s in range(2)]
        for m2 in range(2):
            c2 = [c3[s] - r2_low[s] if m2 else c3[s] for s in range(2)]
            r1 = right(c2[1], 1)
            r1_low = dot(r1, low(1, 0))
            for m1 in range(2):
                r0 = right(c2[0] - r1_low if m1 else c2[0], 0)
                pat = m1 + 2 * m2 + 4 * m3
                for s, block in enumerate((r0, r1, r2, r3)):
                    h[pat, :, s * BS : (s + 1) * BS] = block


GC = 8


def update_kernel(order, meta, mown, mpiv, a_ref, near, far, h, delta, out, rows_of):
    g = pl.program_id(0)
    core = meta[0] & 1
    for zg in range(2):
        for fz in range(2):
            z = zg if fz == 0 else 3 - zg
            for cc in range(CPP):
                rows_of[2 * zg + core, fz * CPP + cc] = near[z, cc * BS : (cc + 1) * BS]
                rows_of[2 * zg + 1 - core, fz * CPP + cc] = far[z, cc * BS : (cc + 1) * BS]
    rows = lax.broadcasted_iota(jnp.int32, (BS, BS), 0)
    cols = lax.broadcasted_iota(jnp.int32, (BS, BS), 1)
    perm = jnp.where((rows % GC) * SUB + rows // GC == cols, 1.0, 0.0).astype(BF)
    cols_out = []
    for col in range(GC):
        c = g * GC + col
        pat = mpiv[order[1] * NC + c] + 2 * mpiv[order[2] * NC + c] + 4 * mpiv[order[3] * NC + c]
        raw = jnp.concatenate([rows_of[order[s], col] for s in range(NP)], axis=0)
        lu = dot(h[pat], raw)
        parts = []
        for r in range(NR):
            parts.append(jnp.where(mown[r * NC + c] != 0, lu[r * BS : (r + 1) * BS], 0.0).astype(BF))
        if col == 0:
            parts = [jnp.where(g == 0, delta[r * BS : (r + 1) * BS], parts[r]) for r in range(NR)]
        cols_out.append(parts)
    for r in range(NR):
        for ag in range(BS // SUB):
            sl = slice(ag * SUB, (ag + 1) * SUB)
            stack = jnp.concatenate([cols_out[col][r][sl] for col in range(GC)], axis=0)
            change = dot(perm, stack).reshape(SUB, GC, BS)
            out[r, sl] = (a_ref[r, sl].astype(F32) - change).astype(BF)


def vmem(n):
    return [pl.BlockSpec(memory_space=pltpu.VMEM)] * n


def smem(n):
    return [pl.BlockSpec(memory_space=pltpu.SMEM)] * n


def body(front, pivot_inverse, rhs, trail_sol, block_mask, panel_order):
    w, q = lax.axis_index("wide"), lax.axis_index("narrow")
    meta = jnp.stack([w, q]).astype(jnp.int32)
    blocks = front.reshape(NR, BS, NC, BS)
    mask = block_mask.reshape(NR, NC)
    b = rhs.reshape(NR, BS, NRHS)
    y = trail_sol.reshape(NR, BS, NRHS)

    mine = blocks[:, :, 0, :].reshape(NR * BS, BS)
    mrow = jnp.broadcast_to(jnp.pad(mask[:, :1], ((0, 4), (0, 0))).astype(BF), (8, BS))
    mine = jnp.concatenate([mine, mrow], axis=0)
    others = [lax.ppermute(mine, "narrow", [(i, (i + d) % 4) for i in range(4)]) for d in (1, 2, 3)]

    urows = blocks[0].reshape(BS, PIECES, CPP, BS).transpose(1, 2, 0, 3).reshape(PIECES, CPP * BS, BS)
    prow = blocks[0, :, 0, :].reshape(PIECES, SUB, BS)
    tiles = b[0].reshape(PIECES, 2, 8, 2, BS)
    tile = lax.dynamic_index_in_dim(tiles, q // 2, 1, keepdims=False)
    tile = lax.dynamic_index_in_dim(tile, q % 2, 2, keepdims=False)
    mline = jnp.pad(mask[0].astype(BF), (0, BS - NC))
    mline = jnp.broadcast_to(mline[None, None, :], (PIECES, 8, BS))
    sent = jnp.concatenate([prow, tile, mline], axis=1)

    def scatter(pieces):
        got = jnp.where(w < NP, pieces[0], jnp.zeros_like(pieces[0]))
        for p in range(1, PIECES):
            got = got + lax.ppermute(pieces[p], "wide", [(i, holder(p, i)) for i in range(NP)])
        return got

    small = scatter(sent)
    piece = scatter(urows)

    small = jnp.broadcast_to(small[None], (NW * 4, EXTRA, BS))
    small = lax.all_to_all(small, ("wide", "narrow"), 0, 0).reshape(NW, 4, EXTRA, BS)

    mlines = small[:NP, :, SUB + 8, :NC]
    mpiv = lax.dynamic_index_in_dim(mlines, q, 1, keepdims=False).reshape(NP * NC).astype(jnp.int32)
    mown = mask.reshape(-1)

    lown, lpiv, zt, frhs, send, delta = pl.pallas_call(
        panel_kernel,
        out_shape=(
            jax.ShapeDtypeStruct((NR * BS, NP * BS), BF),
            jax.ShapeDtypeStruct((NP, NP * BS, BS), BF),
            jax.ShapeDtypeStruct((NP, 8, BS), F32),
            jax.ShapeDtypeStruct((NR, BS, NRHS), BF),
            jax.ShapeDtypeStruct((NW // 2, CPP * BS + TROWS, BS), BF),
            jax.ShapeDtypeStruct((NR * BS, BS), BF),
        ),
        in_specs=smem(2) + vmem(9),
        out_specs=tuple(vmem(6)),
        scratch_shapes=[
            pltpu.VMEM((NP, (NR + NP) * BS, BS), BF),
            pltpu.VMEM((NR + NP, BS, NRHS), F32),
            pltpu.VMEM((NRHS, BS), F32),
            pltpu.VMEM((NP, 8, BS), F32),
        ],
        name="panel",
    )(panel_order, meta, mine, *others, small, piece, pivot_inverse, b, y)

    same_core = [[v for v in range(NW) if v % 2 == c] for c in range(2)]
    near = lax.all_to_all(send, "wide", 0, 0, axis_index_groups=same_core)
    far = lax.ppermute(near, "wide", [(v, v ^ 1) for v in range(NW)])

    tspec = pl.BlockSpec((NW // 2, TROWS, BS), lambda g: (0, CPP * BS // TROWS, 0))
    fixed2 = lambda shape: pl.BlockSpec(shape, lambda g: (0,) * len(shape))
    xg = pl.pallas_call(
        solve_kernel,
        out_shape=jax.ShapeDtypeStruct((NW, 8, NP * BS), BF),
        grid=(1,),
        in_specs=smem(2)
        + [tspec, tspec, fixed2((NP, 8, BS)), fixed2((NP, NP * BS, BS)), fixed2((NP, BS, BS))],
        out_specs=fixed2((NW, 8, NP * BS)),
        scratch_shapes=[pltpu.VMEM((NP, 8, BS), F32), pltpu.VMEM((64, BS), F32)],
        name="solve",
    )(panel_order, meta, near, far, zt, lpiv, pivot_inverse)
    xall = lax.all_to_all(xg, "wide", 0, 0).reshape(NRHS, NP * BS)
    window = xall.T.reshape(NP, BS, NRHS)

    h = pl.pallas_call(
        combine_kernel,
        out_shape=jax.ShapeDtypeStruct((8, NR * BS, NP * BS), BF),
        in_specs=smem(1) + vmem(3),
        out_specs=vmem(1)[0],
        name="combine",
    )(panel_order, lown, lpiv, pivot_inverse)

    front_out = pl.pallas_call(
        update_kernel,
        out_shape=jax.ShapeDtypeStruct((NR, BS, NC, BS), BF),
        grid=(NC // GC,),
        in_specs=smem(4)
        + [
            pl.BlockSpec((NR, BS, GC, BS), lambda g: (0, 0, g, 0)),
            pl.BlockSpec((4, CPP * BS, BS), lambda g: (g, 0, 0)),
            pl.BlockSpec((4, CPP * BS, BS), lambda g: (g, 0, 0)),
            fixed2((8, NR * BS, NP * BS)),
            fixed2((NR * BS, BS)),
        ],
        out_specs=pl.BlockSpec((NR, BS, GC, BS), lambda g: (0, 0, g, 0)),
        scratch_shapes=[pltpu.VMEM((NP, GC, BS, BS), BF)],
        name="update",
    )(panel_order, meta, mown, mpiv, blocks, near, far, h, delta)
    return front_out.reshape(front.shape), frhs.reshape(rhs.shape), window


def solution(mesh):
    in_specs = (
        P(None, "wide", None, None, "narrow", None),
        P(),
        P(None, "wide", None, None),
        P(None, "wide", None, None),
        P(None, "wide", None, "narrow"),
        P(),
    )
    out_specs = (P(None, "wide", None, None, "narrow", None), P(None, "wide", None, None), P())
    return jax.shard_map(body, mesh=mesh, in_specs=in_specs, out_specs=out_specs, check_vma=False)
```

```python
import jax
import jax.numpy as jnp
from jax import lax
from jax.experimental import pallas as pl
from jax.experimental.pallas import tpu as pltpu
from jax.sharding import PartitionSpec as P

BF = jnp.bfloat16
F32 = jnp.float32
BS = 128
NP = 4
NR = 4
NC = 32
NRHS = 256
NW = 32
PIECES = 8
CPP = NC // PIECES
SUB = 16
EXTRA = SUB + 8 + 8


def holder(p, i):
    z = i >> 1 if p % 2 == 0 else 3 - (i >> 1)
    return (p >> 1) * 8 + z * 2 + (i & 1)


def dot(a, b, ca=1, cb=0):
    return lax.dot_general(a, b, (((ca,), (cb,)), ((), ())), preferred_element_type=F32)


def ranks_of(order, w):
    rank = [sum(jnp.where(order[s] == i, s, 0) for s in range(NP)) for i in range(NP)]
    own = jnp.int32(NP)
    for i in range(NP):
        own = jnp.where(w == i, rank[i], own)
    return rank, own


def panel_kernel(order, meta, own, d1, d2, d3, got, w_ref, b_ref, y_ref,
                 lown, lpiv, zt, frhs, tpart, delta, pan, bs, ztall, mk):
    w, q = meta[0], meta[1]
    rank, own_rank = ranks_of(order, w)
    for d, ref in enumerate((own, d1, d2, d3)):
        k = lax.rem(q - d + 4, 4)
        pan[k, 0 : NR * BS] = ref[0 : NR * BS]
        mk[k] = ref[NR * BS : NR * BS + 8].astype(F32)
    for k in range(NP):
        for i in range(NP):
            for p in range(PIECES):
                pan[k, NR * BS + i * BS + p * SUB : NR * BS + i * BS + (p + 1) * SUB] = got[holder(p, i), k, 0:SUB]
    for r in range(NR):
        bs[r] = b_ref[r].astype(F32)
    for i in range(NP):
        for p in range(PIECES):
            for n in range(4):
                r0 = p * SUB + 8 * (n >> 1)
                c0 = 128 * (n & 1)
                bs[NR + i, r0 : r0 + 8, c0 : c0 + 128] = got[holder(p, i), n, SUB : SUB + 8].astype(F32)
    row_rank = [own_rank, None, None, None] + rank
    for s in range(NP):
        k = order[s]
        weight = w_ref[k]
        left = dot(pan[k], weight)
        parts = []
        for i in range(NR + NP):
            part = left[i * BS : (i + 1) * BS]
            if row_rank[i] is not None:
                part = jnp.where(row_rank[i] > s, part, 0.0)
            parts.append(part.astype(BF))
        lb = jnp.concatenate(parts, axis=0)
        lown[:, s * BS : (s + 1) * BS] = lb[: NR * BS]
        lpiv[s] = lb[NR * BS :]
        if s + 1 < NP:
            uppers = []
            for j in range(NP):
                akj = pan[j, pl.ds(pl.multiple_of(NR * BS + k * BS, BS), BS), :]
                upper = dot(weight, akj, 0, 0)
                uppers.append(jnp.where(rank[j] > s, upper, 0.0).astype(BF))
            for j in range(NP):
                prod = dot(lb, uppers[j])
                for i in range(NR + NP):
                    sl = slice(i * BS, (i + 1) * BS)
                    if i < NR:
                        m = mk[j, i : i + 1, :]
                    else:
                        m = got[holder(0, i - NR), j, SUB + 8 : SUB + 16].astype(F32)[0:1, 0:1]
                    pan[j, sl] = (pan[j, sl].astype(F32) - m * prod[sl]).astype(BF)
        bk = bs[NR + k].astype(BF)
        z = dot(weight, bk, 0, 0).astype(BF)
        ztall[...] = dot(bk, weight, 0, 0).astype(BF).astype(F32)
        zt[s] = ztall[pl.ds(pl.multiple_of(w * 8, 8), 8), :]
        elim = dot(lb, z)
        for i in range(NR + NP):
            bs[i] = (bs[i] - elim[i * BS : (i + 1) * BS]).astype(BF).astype(F32)
    for r in range(NR):
        frhs[r] = bs[r].astype(BF)
    delta[...] = (own[0 : NR * BS].astype(F32) - pan[q, 0 : NR * BS].astype(F32)).astype(BF)
    y0 = jnp.where(w < NP, jnp.zeros_like(y_ref[0]), y_ref[0])
    y = jnp.concatenate([y0] + [y_ref[r] for r in range(1, NR)], axis=0)
    tpart[...] = dot(y, lown[...], 0, 0)


def solve_kernel(order, parts, zt, lpiv, w_ref, out, xs):
    total = jnp.sum(parts[...], axis=0)
    xs[...] = jnp.zeros_like(xs)
    for s in reversed(range(NP)):
        k = order[s]
        acc = total[:, s * BS : (s + 1) * BS]
        if s + 1 < NP:
            for i in range(NP):
                acc = acc + dot(xs[i].astype(BF), lpiv[s, i * BS : (i + 1) * BS, :])
        c = (zt[s] - acc).astype(BF)
        xs[k] = dot(c, w_ref[k], 1, 1).astype(BF).astype(F32)
    x = jnp.concatenate([xs[i] for i in range(NP)], axis=1).astype(BF)
    for d in range(NW):
        out[d] = x


def combine_kernel(order, lown, lpiv, w_ref, h):
    def low(t, s):
        return lpiv[s, pl.ds(pl.multiple_of(order[t] * BS, BS), BS), :]

    def right(coeff, s):
        return dot(coeff.astype(BF), w_ref[order[s]], 1, 1).astype(BF)

    base = [lown[:, s * BS : (s + 1) * BS].astype(F32) for s in range(NP)]
    r3 = right(base[3], 3)
    r3_low = [dot(r3, low(3, s)) for s in range(3)]
    for m3 in range(2):
        c3 = [base[s] - r3_low[s] if m3 else base[s] for s in range(3)]
        r2 = right(c3[2], 2)
        r2_low = [dot(r2, low(2, s)) for s in range(2)]
        for m2 in range(2):
            c2 = [c3[s] - r2_low[s] if m2 else c3[s] for s in range(2)]
            r1 = right(c2[1], 1)
            r1_low = dot(r1, low(1, 0))
            for m1 in range(2):
                r0 = right(c2[0] - r1_low if m1 else c2[0], 0)
                pat = m1 + 2 * m2 + 4 * m3
                for s, block in enumerate((r0, r1, r2, r3)):
                    h[pat, :, pl.ds(pl.multiple_of(order[s] * BS, BS), BS)] = block


GC = 8


def update_kernel(order, mown, mpiv, a_ref, u_ref, h, delta, out):
    g = pl.program_id(0)
    rows = lax.broadcasted_iota(jnp.int32, (BS, BS), 0)
    cols = lax.broadcasted_iota(jnp.int32, (BS, BS), 1)
    perm = jnp.where((rows % GC) * SUB + rows // GC == cols, 1.0, 0.0).astype(BF)
    cols_out = []
    for col in range(GC):
        c = g * GC + col
        pat = mpiv[order[1] * NC + c] + 2 * mpiv[order[2] * NC + c] + 4 * mpiv[order[3] * NC + c]
        p, cc = divmod(col, CPP)
        raw = [u_ref[holder(p, k), cc * BS : (cc + 1) * BS] for k in range(NP)]
        raw = jnp.concatenate(raw, axis=0)
        lu = dot(h[pat], raw)
        parts = []
        for r in range(NR):
            parts.append(jnp.where(mown[r * NC + c] != 0, lu[r * BS : (r + 1) * BS], 0.0).astype(BF))
        if col == 0:
            parts = [jnp.where(g == 0, delta[r * BS : (r + 1) * BS], parts[r]) for r in range(NR)]
        cols_out.append(parts)
    for r in range(NR):
        for ag in range(0, BS // SUB, 2):
            sls = [slice((ag + e) * SUB, (ag + e + 1) * SUB) for e in range(2)]
            stack = jnp.concatenate(
                [jnp.concatenate([cols_out[col][r][sl] for col in range(GC)], axis=0) for sl in sls], axis=1
            )
            change = dot(perm, stack)
            for e, sl in enumerate(sls):
                part = change[:, e * BS : (e + 1) * BS].reshape(SUB, GC, BS)
                out[r, sl] = (a_ref[r, sl].astype(F32) - part).astype(BF)


def vmem(n):
    return [pl.BlockSpec(memory_space=pltpu.VMEM)] * n


def smem(n):
    return [pl.BlockSpec(memory_space=pltpu.SMEM)] * n


def body(front, pivot_inverse, rhs, trail_sol, block_mask, panel_order):
    w, q = lax.axis_index("wide"), lax.axis_index("narrow")
    meta = jnp.stack([w, q]).astype(jnp.int32)
    blocks = front.reshape(NR, BS, NC, BS)
    mask = block_mask.reshape(NR, NC)
    b = rhs.reshape(NR, BS, NRHS)
    y = trail_sol.reshape(NR, BS, NRHS)

    mine = blocks[:, :, 0, :].reshape(NR * BS, BS)
    mrow = jnp.broadcast_to(jnp.pad(mask[:, :1], ((0, 4), (0, 0))).astype(BF), (8, BS))
    mine = jnp.concatenate([mine, mrow], axis=0)
    others = [lax.ppermute(mine, "narrow", [(i, (i + d) % 4) for i in range(4)]) for d in (1, 2, 3)]

    urows = blocks[0].reshape(BS, PIECES, CPP, BS).transpose(1, 2, 0, 3).reshape(PIECES, CPP * BS, BS)
    prow = blocks[0, :, 0, :].reshape(PIECES, SUB, BS)
    tiles = b[0].reshape(PIECES, 2, 8, 2, BS)
    tile = lax.dynamic_index_in_dim(tiles, q // 2, 1, keepdims=False)
    tile = lax.dynamic_index_in_dim(tile, q % 2, 2, keepdims=False)
    mline = jnp.pad(mask[0].astype(BF), (0, BS - NC))
    mline = jnp.broadcast_to(mline[None, None, :], (PIECES, 8, BS))
    sent = jnp.concatenate([prow, tile, mline], axis=1)

    def scatter(pieces):
        got = jnp.where(w < NP, pieces[0], jnp.zeros_like(pieces[0]))
        for p in range(1, PIECES):
            got = got + lax.ppermute(pieces[p], "wide", [(i, holder(p, i)) for i in range(NP)])
        return got

    got = scatter(jnp.concatenate([urows, sent], axis=1))

    ugath = lax.all_gather(got[: CPP * BS], "wide")

    small = jnp.broadcast_to(got[None, CPP * BS :], (NW * 4, EXTRA, BS))
    small = lax.all_to_all(small, ("wide", "narrow"), 0, 0).reshape(NW, 4, EXTRA, BS)

    mlines = small[:NP, :, SUB + 8, :NC]
    mpiv = lax.dynamic_index_in_dim(mlines, q, 1, keepdims=False).reshape(NP * NC).astype(jnp.int32)
    mown = mask.reshape(-1)

    lown, lpiv, zt, frhs, tpart, delta = pl.pallas_call(
        panel_kernel,
        out_shape=(
            jax.ShapeDtypeStruct((NR * BS, NP * BS), BF),
            jax.ShapeDtypeStruct((NP, NP * BS, BS), BF),
            jax.ShapeDtypeStruct((NP, 8, BS), F32),
            jax.ShapeDtypeStruct((NR, BS, NRHS), BF),
            jax.ShapeDtypeStruct((NRHS, NP * BS), F32),
            jax.ShapeDtypeStruct((NR * BS, BS), BF),
        ),
        in_specs=smem(2) + vmem(8),
        out_specs=tuple(vmem(6)),
        scratch_shapes=[
            pltpu.VMEM((NP, (NR + NP) * BS, BS), BF),
            pltpu.VMEM((NR + NP, BS, NRHS), F32),
            pltpu.VMEM((NRHS, BS), F32),
            pltpu.VMEM((NP, 8, BS), F32),
        ],
        name="panel",
    )(panel_order, meta, mine, *others, small, pivot_inverse, b, y)

    tparts = lax.all_to_all(tpart.reshape(NW, 8, NP * BS), "wide", 0, 0)
    xg = pl.pallas_call(
        solve_kernel,
        out_shape=jax.ShapeDtypeStruct((NW, 8, NP * BS), BF),
        in_specs=smem(1) + vmem(4),
        out_specs=vmem(1)[0],
        scratch_shapes=[pltpu.VMEM((NP, 8, BS), F32)],
        name="solve",
    )(panel_order, tparts, zt, lpiv, pivot_inverse)
    xall = lax.all_to_all(xg, "wide", 0, 0).reshape(NRHS, NP * BS)
    window = xall.T.reshape(NP, BS, NRHS)

    h = pl.pallas_call(
        combine_kernel,
        out_shape=jax.ShapeDtypeStruct((8, NR * BS, NP * BS), BF),
        in_specs=smem(1) + vmem(3),
        out_specs=vmem(1)[0],
        name="combine",
    )(panel_order, lown, lpiv, pivot_inverse)

    fixed2 = lambda shape: pl.BlockSpec(shape, lambda g: (0,) * len(shape))
    front_out = pl.pallas_call(
        update_kernel,
        out_shape=jax.ShapeDtypeStruct((NR, BS, NC, BS), BF),
        grid=(NC // GC,),
        in_specs=smem(3)
        + [
            pl.BlockSpec((NR, BS, GC, BS), lambda g: (0, 0, g, 0)),
            pl.BlockSpec((8, CPP * BS, BS), lambda g: (g, 0, 0)),
            fixed2((8, NR * BS, NP * BS)),
            fixed2((NR * BS, BS)),
        ],
        out_specs=pl.BlockSpec((NR, BS, GC, BS), lambda g: (0, 0, g, 0)),
        name="update",
    )(panel_order, mown, mpiv, blocks, ugath.reshape(NW, CPP * BS, BS), h, delta)
    return front_out.reshape(front.shape), frhs.reshape(rhs.shape), window


def solution(mesh):
    in_specs = (
        P(None, "wide", None, None, "narrow", None),
        P(),
        P(None, "wide", None, None),
        P(None, "wide", None, None),
        P(None, "wide", None, "narrow"),
        P(),
    )
    out_specs = (P(None, "wide", None, None, "narrow", None), P(None, "wide", None, None), P())
    return jax.shard_map(body, mesh=mesh, in_specs=in_specs, out_specs=out_specs, check_vma=False)
```

```python
import jax
import jax.numpy as jnp
from jax import lax
from jax.experimental import pallas as pl
from jax.experimental.pallas import tpu as pltpu
from jax.sharding import PartitionSpec as P

BF = jnp.bfloat16
F32 = jnp.float32
BS = 128
NP = 4
NR = 4
NC = 32
NRHS = 256
NW = 32
PIECES = 8
CPP = NC // PIECES
SUB = 16
EXTRA = SUB + 8 + 8


def holder(p, i):
    z = i >> 1 if p % 2 == 0 else 3 - (i >> 1)
    return (p >> 1) * 8 + z * 2 + (i & 1)


def dot(a, b, ca=1, cb=0):
    return lax.dot_general(a, b, (((ca,), (cb,)), ((), ())), preferred_element_type=F32)


def ranks_of(order, w):
    rank = [sum(jnp.where(order[s] == i, s, 0) for s in range(NP)) for i in range(NP)]
    own = jnp.int32(NP)
    for i in range(NP):
        own = jnp.where(w == i, rank[i], own)
    return rank, own


def one_hot(rows, fn):
    r = lax.broadcasted_iota(jnp.int32, (rows, BS), 0)
    c = lax.broadcasted_iota(jnp.int32, (rows, BS), 1)
    return jnp.where(fn(r) == c, 1.0, 0.0).astype(BF)


def prep_kernel(meta, row_ref, col_ref, b_ref, mask_ref, sent, mine):
    q = meta[1]
    gather = one_hot(BS, lambda r: (r % SUB) * 8 + r // SUB)
    for ct in range(NC // 8):
        for ag in range(BS // SUB):
            native = row_ref[0, ag * SUB : (ag + 1) * SUB, ct * 8 : (ct + 1) * 8, :]
            native = native.astype(F32).reshape(BS, BS).astype(BF)
            blocks = dot(gather, native).astype(BF)
            for e in range(8):
                p, cc = divmod(ct * 8 + e, CPP)
                sent[p, cc * BS + ag * SUB : cc * BS + (ag + 1) * SUB] = blocks[e * SUB : (e + 1) * SUB]
            if ct == 0:
                sent[ag, CPP * BS : CPP * BS + SUB] = blocks[:SUB]
    pick = one_hot(SUB, lambda r: r * 8)
    for r in range(NR):
        for ag in range(BS // SUB):
            native = col_ref[r, ag * SUB : (ag + 1) * SUB].astype(F32).reshape(BS, BS).astype(BF)
            mine[r * BS + ag * SUB : r * BS + (ag + 1) * SUB] = dot(pick, native).astype(BF)
    mask = mask_ref[...].astype(F32)
    widen = one_hot(NC, lambda r: r)
    line = jnp.broadcast_to(dot(mask.astype(BF), widen)[0:1], (8, BS)).astype(BF)
    for p in range(PIECES):
        rows = b_ref[0, p * SUB : (p + 1) * SUB, :].astype(F32)
        rows = jnp.where((q & 2) != 0, rows[8:], rows[:8])
        rows = jnp.where((q & 1) != 0, rows[:, BS:], rows[:, :BS])
        sent[p, CPP * BS + SUB : CPP * BS + SUB + 8] = rows.astype(BF)
        sent[p, CPP * BS + SUB + 8 :] = line
    first = jnp.broadcast_to(mask[:, 0:1], (NR, BS))
    mine[NR * BS :] = jnp.concatenate([first, jnp.zeros((8 - NR, BS), F32)], axis=0).astype(BF)


def panel_kernel(order, meta, own, d1, d2, d3, got, w_ref, b_ref, y_ref,
                 lown, lpiv, zt, frhs, tpart, delta, pan, bs, ztall, tall, mk):
    w, q = meta[0], meta[1]
    rank, own_rank = ranks_of(order, w)
    for d, ref in enumerate((own, d1, d2, d3)):
        k = lax.rem(q - d + 4, 4)
        pan[k, 0 : NR * BS] = ref[0 : NR * BS]
        mk[k] = ref[NR * BS : NR * BS + 8].astype(F32)
    for k in range(NP):
        for i in range(NP):
            for p in range(PIECES):
                pan[k, NR * BS + i * BS + p * SUB : NR * BS + i * BS + (p + 1) * SUB] = got[holder(p, i), k, 0:SUB]
    for r in range(NR):
        bs[r] = b_ref[r].astype(F32)
    for i in range(NP):
        for p in range(PIECES):
            for n in range(4):
                r0 = p * SUB + 8 * (n >> 1)
                c0 = 128 * (n & 1)
                bs[NR + i, r0 : r0 + 8, c0 : c0 + 128] = got[holder(p, i), n, SUB : SUB + 8].astype(F32)
    row_rank = [own_rank, None, None, None] + rank
    for s in range(NP):
        k = order[s]
        weight = w_ref[k]
        left = dot(pan[k], weight)
        parts = []
        for i in range(NR + NP):
            part = left[i * BS : (i + 1) * BS]
            if row_rank[i] is not None:
                part = jnp.where(row_rank[i] > s, part, 0.0)
            parts.append(part.astype(BF))
        lb = jnp.concatenate(parts, axis=0)
        lown[:, s * BS : (s + 1) * BS] = lb[: NR * BS]
        lpiv[s] = lb[NR * BS :]
        if s + 1 < NP:
            uppers = []
            for j in range(NP):
                akj = pan[j, pl.ds(pl.multiple_of(NR * BS + k * BS, BS), BS), :]
                upper = dot(weight, akj, 0, 0)
                uppers.append(jnp.where(rank[j] > s, upper, 0.0).astype(BF))
            for j in range(NP):
                prod = dot(lb, uppers[j])
                for i in range(NR + NP):
                    sl = slice(i * BS, (i + 1) * BS)
                    if i < NR:
                        m = mk[j, i : i + 1, :]
                    else:
                        m = got[holder(0, i - NR), j, SUB + 8 : SUB + 16].astype(F32)[0:1, 0:1]
                    pan[j, sl] = (pan[j, sl].astype(F32) - m * prod[sl]).astype(BF)
        bk = bs[NR + k].astype(BF)
        z = dot(weight, bk, 0, 0).astype(BF)
        ztall[...] = dot(bk, weight, 0, 0).astype(BF).astype(F32)
        for j in range(2):
            zt[s * 2 + j : s * 2 + j + 1] = ztall[pl.ds(j * BS + q * NW + w, 1), :]
        elim = dot(lb, z)
        for i in range(NR + NP):
            bs[i] = (bs[i] - elim[i * BS : (i + 1) * BS]).astype(BF).astype(F32)
    for r in range(NR):
        frhs[r] = bs[r].astype(BF)
    delta[...] = (own[0 : NR * BS].astype(F32) - pan[q, 0 : NR * BS].astype(F32)).astype(BF)
    y0 = jnp.where(w < NP, jnp.zeros_like(y_ref[0]), y_ref[0])
    y = jnp.concatenate([y0] + [y_ref[r] for r in range(1, NR)], axis=0)
    tall[...] = dot(y, lown[...], 0, 0)
    for j in range(2):
        mine_cols = tall[pl.ds(pl.multiple_of(j * BS + q * NW, NW), NW), :]
        for s in range(NP):
            tpart[:, s * 2 + j, :] = mine_cols[:, s * BS : (s + 1) * BS]


def solve_kernel(order, mown, mpiv, parts, zt, lpiv, w_ref, h, out, xs):
    total = jnp.sum(parts[...], axis=0)
    xs[...] = jnp.zeros_like(xs)
    for s in reversed(range(NP)):
        k = order[s]
        acc = total[s * 2 : s * 2 + 2]
        if s + 1 < NP:
            for i in range(NP):
                acc = acc + dot(xs[i].astype(BF), lpiv[s, i * BS : (i + 1) * BS, :])
        c = (zt[s * 2 : s * 2 + 2] - acc).astype(BF)
        xs[k] = dot(c, w_ref[k], 1, 1).astype(BF).astype(F32)
    x = jnp.concatenate([xs[i] for i in range(NP)], axis=0).astype(BF)
    for d in range(NW * 4):
        out[d] = x


def combine_kernel(order, lown, lpiv, w_ref, h):
    def low(t, s):
        return lpiv[s, pl.ds(pl.multiple_of(order[t] * BS, BS), BS), :]

    def right(coeff, s):
        return dot(coeff.astype(BF), w_ref[order[s]], 1, 1).astype(BF)

    base = [lown[:, s * BS : (s + 1) * BS].astype(F32) for s in range(NP)]
    r3 = right(base[3], 3)
    r3_low = [dot(r3, low(3, s)) for s in range(3)]
    for m3 in range(2):
        c3 = [base[s] - r3_low[s] if m3 else base[s] for s in range(3)]
        r2 = right(c3[2], 2)
        r2_low = [dot(r2, low(2, s)) for s in range(2)]
        for m2 in range(2):
            c2 = [c3[s] - r2_low[s] if m2 else c3[s] for s in range(2)]
            r1 = right(c2[1], 1)
            r1_low = dot(r1, low(1, 0))
            for m1 in range(2):
                r0 = right(c2[0] - r1_low if m1 else c2[0], 0)
                pat = m1 + 2 * m2 + 4 * m3
                for s, block in enumerate((r0, r1, r2, r3)):
                    h[pat, :, pl.ds(pl.multiple_of(order[s] * BS, BS), BS)] = block


GC = 8


def update_kernel(order, mown, mpiv, a_ref, u_ref, h, delta, out):
    g = pl.program_id(0)
    rows = lax.broadcasted_iota(jnp.int32, (BS, BS), 0)
    cols = lax.broadcasted_iota(jnp.int32, (BS, BS), 1)
    perm = jnp.where((rows % GC) * SUB + rows // GC == cols, 1.0, 0.0).astype(BF)
    cols_out = []
    for col in range(GC):
        c = g * GC + col
        pat = mpiv[order[1] * NC + c] + 2 * mpiv[order[2] * NC + c] + 4 * mpiv[order[3] * NC + c]
        p, cc = divmod(col, CPP)
        raw = [u_ref[holder(p, k), cc * BS : (cc + 1) * BS] for k in range(NP)]
        raw = jnp.concatenate(raw, axis=0)
        lu = dot(h[pat], raw)
        parts = []
        for r in range(NR):
            parts.append(jnp.where(mown[r * NC + c] != 0, lu[r * BS : (r + 1) * BS], 0.0).astype(BF))
        if col == 0:
            parts = [jnp.where(g == 0, delta[r * BS : (r + 1) * BS], parts[r]) for r in range(NR)]
        cols_out.append(parts)
    for r in range(NR):
        for ag in range(0, BS // SUB, 2):
            sls = [slice((ag + e) * SUB, (ag + e + 1) * SUB) for e in range(2)]
            stack = jnp.concatenate(
                [jnp.concatenate([cols_out[col][r][sl] for col in range(GC)], axis=0) for sl in sls], axis=1
            )
            change = dot(perm, stack)
            for e, sl in enumerate(sls):
                part = change[:, e * BS : (e + 1) * BS].reshape(SUB, GC, BS)
                out[r, sl] = (a_ref[r, sl].astype(F32) - part).astype(BF)


def vmem(n):
    return [pl.BlockSpec(memory_space=pltpu.VMEM)] * n


def smem(n):
    return [pl.BlockSpec(memory_space=pltpu.SMEM)] * n


def body(front, pivot_inverse, rhs, trail_sol, block_mask, panel_order):
    w, q = lax.axis_index("wide"), lax.axis_index("narrow")
    meta = jnp.stack([w, q]).astype(jnp.int32)
    blocks = front.reshape(NR, BS, NC, BS)
    mask = block_mask.reshape(NR, NC)
    b = rhs.reshape(NR, BS, NRHS)
    y = trail_sol.reshape(NR, BS, NRHS)

    fixed = lambda shape: pl.BlockSpec(shape, lambda g: (0,) * len(shape))
    sent, mine = pl.pallas_call(
        prep_kernel,
        out_shape=(
            jax.ShapeDtypeStruct((PIECES, CPP * BS + EXTRA, BS), BF),
            jax.ShapeDtypeStruct((NR * BS + 8, BS), BF),
        ),
        grid=(1,),
        in_specs=smem(1)
        + [fixed((1, BS, NC, BS)), fixed((NR, BS, 8, BS)), fixed((1, BS, NRHS)), fixed((NR, NC))],
        out_specs=(fixed((PIECES, CPP * BS + EXTRA, BS)), fixed((NR * BS + 8, BS))),
        name="prep",
    )(meta, blocks, blocks, b, mask)

    others = [lax.ppermute(mine, "narrow", [(i, (i + d) % 4) for i in range(4)]) for d in (1, 2, 3)]

    pieces = [
        lax.ppermute(sent[p], "wide", [(i, holder(p, i)) for i in range(NP)]) for p in range(1, PIECES)
    ]
    pieces, others = lax.optimization_barrier((pieces, others))
    got = sum(pieces, jnp.where(w < NP, sent[0], jnp.zeros_like(sent[0])))

    ugath = lax.all_gather(got[: CPP * BS], "wide")

    small = jnp.broadcast_to(got[None, CPP * BS :], (NW * 4, EXTRA, BS))
    small = lax.all_to_all(small, ("wide", "narrow"), 0, 0).reshape(NW, 4, EXTRA, BS)

    mlines = small[:NP, :, SUB + 8, :NC]
    mpiv = lax.dynamic_index_in_dim(mlines, q, 1, keepdims=False).reshape(NP * NC).astype(jnp.int32)
    mown = mask.reshape(-1)

    lown, lpiv, zt, frhs, tpart, delta = pl.pallas_call(
        panel_kernel,
        out_shape=(
            jax.ShapeDtypeStruct((NR * BS, NP * BS), BF),
            jax.ShapeDtypeStruct((NP, NP * BS, BS), BF),
            jax.ShapeDtypeStruct((8, BS), F32),
            jax.ShapeDtypeStruct((NR, BS, NRHS), BF),
            jax.ShapeDtypeStruct((NW, 8, BS), F32),
            jax.ShapeDtypeStruct((NR * BS, BS), BF),
        ),
        in_specs=smem(2) + vmem(8),
        out_specs=tuple(vmem(6)),
        scratch_shapes=[
            pltpu.VMEM((NP, (NR + NP) * BS, BS), BF),
            pltpu.VMEM((NR + NP, BS, NRHS), F32),
            pltpu.VMEM((NRHS, BS), F32),
            pltpu.VMEM((NRHS, NP * BS), F32),
            pltpu.VMEM((NP, 8, BS), F32),
        ],
        name="panel",
    )(panel_order, meta, mine, *others, small, pivot_inverse, b, y)

    h = pl.pallas_call(
        combine_kernel,
        out_shape=jax.ShapeDtypeStruct((8, NR * BS, NP * BS), BF),
        in_specs=smem(1) + vmem(3),
        out_specs=vmem(1)[0],
        name="combine",
    )(panel_order, lown, lpiv, pivot_inverse)

    tparts = lax.all_to_all(tpart, "wide", 0, 0)
    xg = pl.pallas_call(
        solve_kernel,
        out_shape=jax.ShapeDtypeStruct((NW * 4, 8, BS), BF),
        in_specs=smem(3) + vmem(4) + [pl.BlockSpec(memory_space=pl.ANY)],
        out_specs=vmem(1)[0],
        scratch_shapes=[pltpu.VMEM((NP, 2, BS), F32)],
        name="solve",
    )(panel_order, mown, mpiv, tparts, zt, lpiv, pivot_inverse, h)
    xall = lax.all_to_all(xg, ("narrow", "wide"), 0, 0)

    front_out = pl.pallas_call(
        update_kernel,
        out_shape=jax.ShapeDtypeStruct((NR, BS, NC, BS), BF),
        grid=(NC // GC,),
        in_specs=smem(3)
        + [
            pl.BlockSpec((NR, BS, GC, BS), lambda g: (0, 0, g, 0)),
            pl.BlockSpec((8, CPP * BS, BS), lambda g: (g, 0, 0)),
            fixed((8, NR * BS, NP * BS)),
            fixed((NR * BS, BS)),
        ],
        out_specs=pl.BlockSpec((NR, BS, GC, BS), lambda g: (0, 0, g, 0)),
        name="update",
    )(panel_order, mown, mpiv, blocks, ugath.reshape(NW, CPP * BS, BS), h, delta)
    front_out, xall = lax.optimization_barrier((front_out, xall))
    window = xall.reshape(NW * 4, NP, 2, BS).transpose(1, 3, 2, 0).reshape(NP, BS, NRHS)
    return front_out.reshape(front.shape), frhs.reshape(rhs.shape), window


def solution(mesh):
    in_specs = (
        P(None, "wide", None, None, "narrow", None),
        P(),
        P(None, "wide", None, None),
        P(None, "wide", None, None),
        P(None, "wide", None, "narrow"),
        P(),
    )
    out_specs = (P(None, "wide", None, None, "narrow", None), P(None, "wide", None, None), P())
    return jax.shard_map(body, mesh=mesh, in_specs=in_specs, out_specs=out_specs, check_vma=False)
```

```python
import jax
import jax.numpy as jnp
from jax import lax
from jax.experimental import pallas as pl
from jax.experimental.pallas import tpu as pltpu
from jax.sharding import PartitionSpec as P


BF = jnp.bfloat16
F32 = jnp.float32
BS = 128
NP = 4
NR = 4
NC = 32
NRHS = 256
NW = 32
PIECES = 8
CPP = NC // PIECES
SUB = 16
EXTRA = SUB + 8 + 8


def holder(p, i):
    z = i >> 1 if p % 2 == 0 else 3 - (i >> 1)
    return (p >> 1) * 8 + z * 2 + (i & 1)


def dot(a, b, ca=1, cb=0):
    return lax.dot_general(a, b, (((ca,), (cb,)), ((), ())), preferred_element_type=F32)


def ranks_of(order, w):
    rank = [sum(jnp.where(order[s] == i, s, 0) for s in range(NP)) for i in range(NP)]
    own = jnp.int32(NP)
    for i in range(NP):
        own = jnp.where(w == i, rank[i], own)
    return rank, own


def one_hot(rows, fn):
    r = lax.broadcasted_iota(jnp.int32, (rows, BS), 0)
    c = lax.broadcasted_iota(jnp.int32, (rows, BS), 1)
    return jnp.where(fn(r) == c, 1.0, 0.0).astype(BF)


def prep_kernel(row_ref, col_ref, b_ref, mask_ref, *outs):
    q = lax.axis_index("narrow")
    sent, mine = outs[:PIECES], outs[PIECES]
    gather = one_hot(BS, lambda r: (r % SUB) * 8 + r // SUB)
    for ct in range(NC // 8):
        for ag in range(BS // SUB):
            native = row_ref[0, ag * SUB : (ag + 1) * SUB, ct * 8 : (ct + 1) * 8, :]
            native = native.astype(F32).reshape(BS, BS).astype(BF)
            blocks = dot(gather, native).astype(BF)
            for e in range(8):
                p, cc = divmod(ct * 8 + e, CPP)
                sent[p][cc * BS + ag * SUB : cc * BS + (ag + 1) * SUB] = blocks[e * SUB : (e + 1) * SUB]
            if ct == 0:
                sent[ag][CPP * BS : CPP * BS + SUB] = blocks[:SUB]
    pick = one_hot(SUB, lambda r: r * 8)
    for r in range(NR):
        for ag in range(BS // SUB):
            native = col_ref[r, ag * SUB : (ag + 1) * SUB].astype(F32).reshape(BS, BS).astype(BF)
            mine[r * BS + ag * SUB : r * BS + (ag + 1) * SUB] = dot(pick, native).astype(BF)
    mask = mask_ref[...].astype(F32)
    widen = one_hot(NC, lambda r: r)
    line = jnp.broadcast_to(dot(mask.astype(BF), widen)[0:1], (8, BS)).astype(BF)
    for p in range(PIECES):
        rows = b_ref[0, p * SUB : (p + 1) * SUB, :].astype(F32)
        rows = jnp.where((q & 2) != 0, rows[8:], rows[:8])
        rows = jnp.where((q & 1) != 0, rows[:, BS:], rows[:, :BS])
        sent[p][CPP * BS + SUB : CPP * BS + SUB + 8] = rows.astype(BF)
        sent[p][CPP * BS + SUB + 8 :] = line
    first = jnp.broadcast_to(mask[:, 0:1], (NR, BS))
    mine[NR * BS :] = jnp.concatenate([first, jnp.zeros((8 - NR, BS), F32)], axis=0).astype(BF)


def panel_kernel(order, own, d1, d2, d3, got, w_ref, b_ref, y_ref,
                 lown, lpiv, zt, frhs, tpart, delta, mpiv, pan, bs, ztall, tall, mk):
    w, q = lax.axis_index("wide"), lax.axis_index("narrow")
    rank, own_rank = ranks_of(order, w)
    for i in range(NP):
        mpiv[i : i + 1] = got[holder(0, i), q, SUB + 8 : SUB + 16].astype(F32)[0:1].astype(jnp.int32)
    for d, ref in enumerate((own, d1, d2, d3)):
        k = lax.rem(q - d + 4, 4)
        pan[k, 0 : NR * BS] = ref[0 : NR * BS]
        mk[k] = ref[NR * BS : NR * BS + 8].astype(F32)
    for k in range(NP):
        for i in range(NP):
            for p in range(PIECES):
                pan[k, NR * BS + i * BS + p * SUB : NR * BS + i * BS + (p + 1) * SUB] = got[holder(p, i), k, 0:SUB]
    for r in range(NR):
        bs[r] = b_ref[r].astype(F32)
    for i in range(NP):
        for p in range(PIECES):
            for n in range(4):
                r0 = p * SUB + 8 * (n >> 1)
                c0 = 128 * (n & 1)
                bs[NR + i, r0 : r0 + 8, c0 : c0 + 128] = got[holder(p, i), n, SUB : SUB + 8].astype(F32)
    row_rank = [own_rank, None, None, None] + rank
    for s in range(NP):
        k = order[s]
        weight = w_ref[k]
        left = dot(pan[k], weight)
        parts = []
        for i in range(NR + NP):
            part = left[i * BS : (i + 1) * BS]
            if row_rank[i] is not None:
                part = jnp.where(row_rank[i] > s, part, 0.0)
            parts.append(part.astype(BF))
        lb = jnp.concatenate(parts, axis=0)
        lown[:, s * BS : (s + 1) * BS] = lb[: NR * BS]
        lpiv[s] = lb[NR * BS :]
        for t in range(s + 1, NP):
            j = order[t]
            akj = pan[j, pl.ds(pl.multiple_of(NR * BS + k * BS, BS), BS), :]
            prod = dot(lb, dot(weight, akj, 0, 0).astype(BF))
            for i in range(NR + NP):
                sl = slice(i * BS, (i + 1) * BS)
                if i < NR:
                    m = mk[j, i : i + 1, :]
                else:
                    m = got[holder(0, i - NR), j, SUB + 8 : SUB + 16].astype(F32)[0:1, 0:1]
                pan[j, sl] = (pan[j, sl].astype(F32) - m * prod[sl]).astype(BF)
        bk = bs[NR + k].astype(BF)
        z = dot(weight, bk, 0, 0).astype(BF)
        ztall[...] = dot(bk, weight, 0, 0).astype(BF).astype(F32)
        for j in range(2):
            zt[s * 2 + j : s * 2 + j + 1] = ztall[pl.ds(j * BS + q * NW + w, 1), :]
        elim = dot(lb, z)
        for i in range(NR + NP):
            bs[i] = (bs[i] - elim[i * BS : (i + 1) * BS]).astype(BF).astype(F32)
    for r in range(NR):
        frhs[r] = bs[r].astype(BF)
    delta[...] = (own[0 : NR * BS].astype(F32) - pan[q, 0 : NR * BS].astype(F32)).astype(BF)
    y0 = jnp.where(w < NP, jnp.zeros_like(y_ref[0]), y_ref[0])
    y = jnp.concatenate([y0] + [y_ref[r] for r in range(1, NR)], axis=0)
    tall[...] = dot(y, lown[...], 0, 0)
    for j in range(2):
        mine_cols = tall[pl.ds(pl.multiple_of(j * BS + q * NW, NW), NW), :]
        for s in range(NP):
            tpart[:, s * 2 + j, :] = mine_cols[:, s * BS : (s + 1) * BS]


def solve_kernel(order, parts, zt, lpiv, w_ref, h, out, xs):
    total = jnp.sum(parts[...], axis=0)
    for s in reversed(range(NP)):
        k = order[s]
        acc = total[s * 2 : s * 2 + 2]
        for t in range(s + 1, NP):
            i = order[t]
            acc = acc + dot(xs[i].astype(BF), lpiv[s, pl.ds(pl.multiple_of(i * BS, BS), BS), :])
        c = (zt[s * 2 : s * 2 + 2] - acc).astype(BF)
        xs[k] = dot(c, w_ref[k], 1, 1).astype(BF).astype(F32)
    x = jnp.concatenate([xs[i] for i in range(NP)], axis=0).astype(BF)
    for d in range(NW * 4):
        out[d] = x


def combine_kernel(order, lown, lpiv, w_ref, h):
    def low(t, s):
        return lpiv[s, pl.ds(pl.multiple_of(order[t] * BS, BS), BS), :]

    def right(coeff, s):
        return dot(coeff.astype(BF), w_ref[order[s]], 1, 1).astype(BF)

    base = [lown[:, s * BS : (s + 1) * BS].astype(F32) for s in range(NP)]
    r3 = right(base[3], 3)
    r3_low = [dot(r3, low(3, s)) for s in range(3)]
    for m3 in range(2):
        c3 = [base[s] - r3_low[s] if m3 else base[s] for s in range(3)]
        r2 = right(c3[2], 2)
        r2_low = [dot(r2, low(2, s)) for s in range(2)]
        for m2 in range(2):
            c2 = [c3[s] - r2_low[s] if m2 else c3[s] for s in range(2)]
            r1 = right(c2[1], 1)
            r1_low = dot(r1, low(1, 0))
            for m1 in range(2):
                r0 = right(c2[0] - r1_low if m1 else c2[0], 0)
                pat = m1 + 2 * m2 + 4 * m3
                for s, block in enumerate((r0, r1, r2, r3)):
                    h[pat, :, pl.ds(pl.multiple_of(order[s] * BS, BS), BS)] = block


GC = 8


def update_kernel(order, mown, mpiv, a_ref, u_ref, h, delta, out):
    g = pl.program_id(0)
    rows = lax.broadcasted_iota(jnp.int32, (BS, BS), 0)
    cols = lax.broadcasted_iota(jnp.int32, (BS, BS), 1)
    perm = jnp.where((rows % GC) * SUB + rows // GC == cols, 1.0, 0.0).astype(BF)
    cols_out = []
    for col in range(GC):
        c = g * GC + col
        pat = mpiv[order[1], c] + 2 * mpiv[order[2], c] + 4 * mpiv[order[3], c]
        p, cc = divmod(col, CPP)
        raw = [u_ref[holder(p, k), cc * BS : (cc + 1) * BS] for k in range(NP)]
        raw = jnp.concatenate(raw, axis=0)
        lu = dot(h[pat], raw)
        parts = []
        for r in range(NR):
            parts.append(jnp.where(mown[r, c] != 0, lu[r * BS : (r + 1) * BS], 0.0).astype(BF))
        if col == 0:
            parts = [jnp.where(g == 0, delta[r * BS : (r + 1) * BS], parts[r]) for r in range(NR)]
        cols_out.append(parts)
    for r in range(NR):
        for ag in range(0, BS // SUB, 2):
            sls = [slice((ag + e) * SUB, (ag + e + 1) * SUB) for e in range(2)]
            stack = jnp.concatenate(
                [jnp.concatenate([cols_out[col][r][sl] for col in range(GC)], axis=0) for sl in sls], axis=1
            )
            change = dot(perm, stack)
            for e, sl in enumerate(sls):
                part = change[:, e * BS : (e + 1) * BS].reshape(SUB, GC, BS)
                out[r, sl] = (a_ref[r, sl].astype(F32) - part).astype(BF)


def vmem(n):
    return [pl.BlockSpec(memory_space=pltpu.VMEM)] * n


def smem(n):
    return [pl.BlockSpec(memory_space=pltpu.SMEM)] * n


def body(front, pivot_inverse, rhs, trail_sol, block_mask, panel_order):
    w = lax.axis_index("wide")
    blocks = front.reshape(NR, BS, NC, BS)
    mask = block_mask.reshape(NR, NC)
    b = rhs.reshape(NR, BS, NRHS)
    y = trail_sol.reshape(NR, BS, NRHS)

    fixed = lambda shape: pl.BlockSpec(shape, lambda g: (0,) * len(shape))
    shapes = [(CPP * BS + EXTRA, BS)] * PIECES + [(NR * BS + 8, BS)]
    *sent, mine = pl.pallas_call(
        prep_kernel,
        out_shape=tuple(jax.ShapeDtypeStruct(shape, BF) for shape in shapes),
        grid=(1,),
        in_specs=[fixed((1, BS, NC, BS)), fixed((NR, BS, 8, BS)), fixed((1, BS, NRHS)), fixed((NR, NC))],
        out_specs=tuple(fixed(shape) for shape in shapes),
        name="prep",
    )(blocks, blocks, b, mask)

    others = [lax.ppermute(mine, "narrow", [(i, (i + d) % 4) for i in range(4)]) for d in (1, 2, 3)]

    pieces = [
        lax.ppermute(sent[p], "wide", [(i, holder(p, i)) for i in range(NP)]) for p in range(1, PIECES)
    ]
    got = sum(pieces, jnp.where(w < NP, sent[0], jnp.zeros_like(sent[0])))

    ugath = lax.all_gather(got[: CPP * BS], "wide")

    small = jnp.broadcast_to(got[None, CPP * BS :], (NW * 4, EXTRA, BS))
    small = lax.all_to_all(small, ("wide", "narrow"), 0, 0).reshape(NW, 4, EXTRA, BS)

    lown, lpiv, zt, frhs, tpart, delta, mpiv = pl.pallas_call(
        panel_kernel,
        out_shape=(
            jax.ShapeDtypeStruct((NR * BS, NP * BS), BF),
            jax.ShapeDtypeStruct((NP, NP * BS, BS), BF),
            jax.ShapeDtypeStruct((8, BS), F32),
            jax.ShapeDtypeStruct((NR, BS, NRHS), BF),
            jax.ShapeDtypeStruct((NW, 8, BS), F32),
            jax.ShapeDtypeStruct((NR * BS, BS), BF),
            jax.ShapeDtypeStruct((NP, BS), jnp.int32),
        ),
        in_specs=smem(1) + vmem(8),
        out_specs=tuple(vmem(7)),
        scratch_shapes=[
            pltpu.VMEM((NP, (NR + NP) * BS, BS), BF),
            pltpu.VMEM((NR + NP, BS, NRHS), F32),
            pltpu.VMEM((NRHS, BS), F32),
            pltpu.VMEM((NRHS, NP * BS), F32),
            pltpu.VMEM((NP, 8, BS), F32),
        ],
        name="panel",
    )(panel_order, mine, *others, small, pivot_inverse, b, y)

    h = pl.pallas_call(
        combine_kernel,
        out_shape=jax.ShapeDtypeStruct((8, NR * BS, NP * BS), BF),
        in_specs=smem(1) + vmem(3),
        out_specs=vmem(1)[0],
        name="combine",
    )(panel_order, lown, lpiv, pivot_inverse)

    tparts = lax.all_to_all(tpart, "wide", 0, 0)
    xg = pl.pallas_call(
        solve_kernel,
        out_shape=jax.ShapeDtypeStruct((NW * 4, 8, BS), BF),
        in_specs=smem(1) + vmem(4) + [pl.BlockSpec(memory_space=pl.ANY)],
        out_specs=vmem(1)[0],
        scratch_shapes=[pltpu.VMEM((NP, 2, BS), F32)],
        name="solve",
    )(panel_order, tparts, zt, lpiv, pivot_inverse, h)
    xall = lax.all_to_all(xg, ("narrow", "wide"), 0, 0)

    front_out = pl.pallas_call(
        update_kernel,
        out_shape=jax.ShapeDtypeStruct((NR, BS, NC, BS), BF),
        grid=(NC // GC,),
        in_specs=smem(3)
        + [
            pl.BlockSpec((NR, BS, GC, BS), lambda g: (0, 0, g, 0)),
            pl.BlockSpec((8, CPP * BS, BS), lambda g: (g, 0, 0)),
            fixed((8, NR * BS, NP * BS)),
            fixed((NR * BS, BS)),
        ],
        out_specs=pl.BlockSpec((NR, BS, GC, BS), lambda g: (0, 0, g, 0)),
        name="update",
    )(panel_order, mask, mpiv, blocks, ugath.reshape(NW, CPP * BS, BS), h, delta)
    front_out, xall = lax.optimization_barrier((front_out, xall))
    window = xall.reshape(NW * 4, NP, 2, BS).transpose(1, 3, 2, 0).reshape(NP, BS, NRHS)
    return front_out.reshape(front.shape), frhs.reshape(rhs.shape), window


def solution(mesh):
    in_specs = (
        P(None, "wide", None, None, "narrow", None),
        P(),
        P(None, "wide", None, None),
        P(None, "wide", None, None),
        P(None, "wide", None, "narrow"),
        P(),
    )
    out_specs = (P(None, "wide", None, None, "narrow", None), P(None, "wide", None, None), P())

    def step(*args):
        return body(*args)

    step = jax.shard_map(step, mesh=mesh, in_specs=in_specs, out_specs=out_specs, check_vma=False)
    return step
```

```python
import jax
import jax.numpy as jnp
from jax import lax
from jax.experimental import pallas as pl
from jax.experimental.pallas import tpu as pltpu
from jax.sharding import Mesh
from jax.sharding import PartitionSpec as P


BF = jnp.bfloat16
F32 = jnp.float32
BS = 128
NP = 4
NR = 4
NC = 32
NRHS = 256
NW = 32
WIDE = ("chip", "core")
PIECES = 8
CPP = NC // PIECES
SUB = 16
EXTRA = SUB + 8 + 8


def holder(p, i):
    z = i >> 1 if p % 2 == 0 else 3 - (i >> 1)
    return (p >> 1) * 8 + z * 2 + (i & 1)


def dot(a, b, ca=1, cb=0):
    return lax.dot_general(a, b, (((ca,), (cb,)), ((), ())), preferred_element_type=F32)


def ranks_of(order, w):
    rank = [sum(jnp.where(order[s] == i, s, 0) for s in range(NP)) for i in range(NP)]
    own = jnp.int32(NP)
    for i in range(NP):
        own = jnp.where(w == i, rank[i], own)
    return rank, own


def one_hot(rows, fn):
    r = lax.broadcasted_iota(jnp.int32, (rows, BS), 0)
    c = lax.broadcasted_iota(jnp.int32, (rows, BS), 1)
    return jnp.where(fn(r) == c, 1.0, 0.0).astype(BF)


def prep_kernel(row_ref, col_ref, b_ref, mask_ref, *outs):
    q = lax.axis_index("narrow")
    sent, mine = outs[:PIECES], outs[PIECES]
    gather = one_hot(BS, lambda r: (r % SUB) * 8 + r // SUB)
    for ct in range(NC // 8):
        for ag in range(BS // SUB):
            native = row_ref[0, ag * SUB : (ag + 1) * SUB, ct * 8 : (ct + 1) * 8, :]
            native = native.astype(F32).reshape(BS, BS).astype(BF)
            blocks = dot(gather, native).astype(BF)
            for e in range(8):
                p, cc = divmod(ct * 8 + e, CPP)
                sent[p][cc * BS + ag * SUB : cc * BS + (ag + 1) * SUB] = blocks[e * SUB : (e + 1) * SUB]
            if ct == 0:
                sent[ag][CPP * BS : CPP * BS + SUB] = blocks[:SUB]
    pick = one_hot(SUB, lambda r: r * 8)
    for r in range(NR):
        for ag in range(BS // SUB):
            native = col_ref[r, ag * SUB : (ag + 1) * SUB].astype(F32).reshape(BS, BS).astype(BF)
            mine[r * BS + ag * SUB : r * BS + (ag + 1) * SUB] = dot(pick, native).astype(BF)
    mask = mask_ref[...].astype(F32)
    widen = one_hot(NC, lambda r: r)
    line = jnp.broadcast_to(dot(mask.astype(BF), widen)[0:1], (8, BS)).astype(BF)
    for p in range(PIECES):
        rows = b_ref[0, p * SUB : (p + 1) * SUB, :].astype(F32)
        rows = jnp.where((q & 2) != 0, rows[8:], rows[:8])
        rows = jnp.where((q & 1) != 0, rows[:, BS:], rows[:, :BS])
        sent[p][CPP * BS + SUB : CPP * BS + SUB + 8] = rows.astype(BF)
        sent[p][CPP * BS + SUB + 8 :] = line
    first = jnp.broadcast_to(mask[:, 0:1], (NR, BS))
    mine[NR * BS :] = jnp.concatenate([first, jnp.zeros((8 - NR, BS), F32)], axis=0).astype(BF)


def merge_kernel(*refs):
    parts, (piece, copies) = refs[:PIECES], refs[PIECES:]
    first = parts[0][...]
    is_source = lax.axis_index("chip") < 2
    total = jnp.where(is_source, first, jnp.zeros_like(first))
    for part in parts[1:]:
        total = total + part[...]
    piece[...] = total[: CPP * BS]
    for d in range(NW * 2):
        copies[d] = total[CPP * BS :]


def wide_index():
    return lax.axis_index("chip") * 2 + lax.axis_index("core")


def arrivals(near, far):
    core = lax.axis_index("core")
    for ref, c in ((near, core), (far, 1 - core)):
        for zg in range(2):
            for p in range(PIECES):
                z = zg if p % 2 == 0 else 3 - zg
                yield 2 * zg + c, p, ref.at[(p >> 1) * 4 + z]


def panel_kernel(order, own, d1, d2, d3, near, far, w_ref, y_ref,
                 lown, lpiv, tpart, delta, mpiv, pan, tall, mk, mkp):
    w, q = wide_index(), lax.axis_index("narrow")
    rank, own_rank = ranks_of(order, w)
    for d, ref in enumerate((own, d1, d2, d3)):
        k = lax.rem(q - d + 4, 4)
        pan[k, 0 : NR * BS] = ref[0 : NR * BS]
        mk[k] = ref[NR * BS : NR * BS + 8].astype(F32)
    for i, p, tile in arrivals(near, far):
        row = pl.multiple_of(NR * BS + i * BS + p * SUB, SUB)
        for k in range(NP):
            pan[k, pl.ds(row, SUB), :] = tile[k, 0:SUB]
            if p == 0:
                mkp[i, k] = tile[k, SUB + 8 : SUB + 16].astype(F32)
    for i in range(NP):
        mpiv[i : i + 1] = mkp[i, q, 0:1].astype(jnp.int32)
    row_rank = [own_rank, None, None, None] + rank
    for s in range(NP):
        k = order[s]
        weight = w_ref[k]
        left = dot(pan[k], weight)
        parts = []
        for i in range(NR + NP):
            part = left[i * BS : (i + 1) * BS]
            if row_rank[i] is not None:
                part = jnp.where(row_rank[i] > s, part, 0.0)
            parts.append(part.astype(BF))
        lb = jnp.concatenate(parts, axis=0)
        lown[:, s * BS : (s + 1) * BS] = lb[: NR * BS]
        lpiv[s] = lb[NR * BS :]
        for t in range(s + 1, NP):
            j = order[t]
            akj = pan[j, pl.ds(pl.multiple_of(NR * BS + k * BS, BS), BS), :]
            prod = dot(lb, dot(weight, akj, 0, 0).astype(BF))
            for i in range(NR + NP):
                sl = slice(i * BS, (i + 1) * BS)
                m = mk[j, i : i + 1, :] if i < NR else mkp[i - NR, j, 0:1, 0:1]
                pan[j, sl] = (pan[j, sl].astype(F32) - m * prod[sl]).astype(BF)
    delta[...] = (own[0 : NR * BS].astype(F32) - pan[q, 0 : NR * BS].astype(F32)).astype(BF)
    y0 = jnp.where(w < NP, jnp.zeros_like(y_ref[0]), y_ref[0])
    y = jnp.concatenate([y0] + [y_ref[r] for r in range(1, NR)], axis=0)
    tall[...] = dot(y, lown[...], 0, 0)
    for j in range(2):
        mine_cols = tall[pl.ds(pl.multiple_of(j * BS + q * NW, NW), NW), :]
        for s in range(NP):
            tpart[:, s * 2 + j, :] = mine_cols[:, s * BS : (s + 1) * BS]


def forward_kernel(order, near, far, w_ref, b_ref, lown, lpiv, zt, frhs, bs, ztall):
    w, q = wide_index(), lax.axis_index("narrow")
    for r in range(NR):
        bs[r] = b_ref[r].astype(F32)
    for i, p, tile in arrivals(near, far):
        for n in range(4):
            r0 = p * SUB + 8 * (n >> 1)
            c0 = 128 * (n & 1)
            bs[NR + i, r0 : r0 + 8, c0 : c0 + 128] = tile[n, SUB : SUB + 8].astype(F32)
    for s in range(NP):
        k = order[s]
        weight = w_ref[k]
        bk = bs[NR + k].astype(BF)
        z = dot(weight, bk, 0, 0).astype(BF)
        ztall[...] = dot(bk, weight, 0, 0).astype(BF).astype(F32)
        for j in range(2):
            zt[s * 2 + j : s * 2 + j + 1] = ztall[pl.ds(j * BS + q * NW + w, 1), :]
        for ref, base, part in ((lown[:, s * BS : (s + 1) * BS], 0, NR), (lpiv[s], NR, NP)):
            elim = dot(ref, z)
            for i in range(part):
                bs[base + i] = (bs[base + i] - elim[i * BS : (i + 1) * BS]).astype(BF).astype(F32)
    for r in range(NR):
        frhs[r] = bs[r].astype(BF)


def solve_kernel(order, parts, zt, lpiv, w_ref, h, out, xs):
    total = jnp.sum(parts[...], axis=0)
    for s in reversed(range(NP)):
        k = order[s]
        acc = total[s * 2 : s * 2 + 2]
        for t in range(s + 1, NP):
            i = order[t]
            acc = acc + dot(xs[i].astype(BF), lpiv[s, pl.ds(pl.multiple_of(i * BS, BS), BS), :])
        c = (zt[s * 2 : s * 2 + 2] - acc).astype(BF)
        xs[k] = dot(c, w_ref[k], 1, 1).astype(BF).astype(F32)
    x = jnp.concatenate([xs[i] for i in range(NP)], axis=0).astype(BF)
    for d in range(NW * 4):
        out[d] = x


def combine_kernel(order, lown, lpiv, w_ref, h):
    def low(t, s):
        return lpiv[s, pl.ds(pl.multiple_of(order[t] * BS, BS), BS), :]

    def right(coeff, s):
        return dot(coeff.astype(BF), w_ref[order[s]], 1, 1).astype(BF)

    base = [lown[:, s * BS : (s + 1) * BS].astype(F32) for s in range(NP)]
    r3 = right(base[3], 3)
    r3_low = [dot(r3, low(3, s)) for s in range(3)]
    for m3 in range(2):
        c3 = [base[s] - r3_low[s] if m3 else base[s] for s in range(3)]
        r2 = right(c3[2], 2)
        r2_low = [dot(r2, low(2, s)) for s in range(2)]
        for m2 in range(2):
            c2 = [c3[s] - r2_low[s] if m2 else c3[s] for s in range(2)]
            r1 = right(c2[1], 1)
            r1_low = dot(r1, low(1, 0))
            for m1 in range(2):
                r0 = right(c2[0] - r1_low if m1 else c2[0], 0)
                pat = m1 + 2 * m2 + 4 * m3
                for s, block in enumerate((r0, r1, r2, r3)):
                    h[pat, :, pl.ds(pl.multiple_of(order[s] * BS, BS), BS)] = block


GC = 8


def update_kernel(order, mown, mpiv, a_ref, u_ref, h, delta, out):
    g = pl.program_id(0)
    rows = lax.broadcasted_iota(jnp.int32, (BS, BS), 0)
    cols = lax.broadcasted_iota(jnp.int32, (BS, BS), 1)
    perm = jnp.where((rows % GC) * SUB + rows // GC == cols, 1.0, 0.0).astype(BF)
    cols_out = []
    for col in range(GC):
        c = g * GC + col
        pat = mpiv[order[1], c] + 2 * mpiv[order[2], c] + 4 * mpiv[order[3], c]
        p, cc = divmod(col, CPP)
        raw = [u_ref[holder(p, k), cc * BS : (cc + 1) * BS] for k in range(NP)]
        raw = jnp.concatenate(raw, axis=0)
        lu = dot(h[pat], raw)
        parts = []
        for r in range(NR):
            parts.append(jnp.where(mown[r, c] != 0, lu[r * BS : (r + 1) * BS], 0.0).astype(BF))
        if col == 0:
            parts = [jnp.where(g == 0, delta[r * BS : (r + 1) * BS], parts[r]) for r in range(NR)]
        cols_out.append(parts)
    for r in range(NR):
        for ag in range(0, BS // SUB, 2):
            sls = [slice((ag + e) * SUB, (ag + e + 1) * SUB) for e in range(2)]
            stack = jnp.concatenate(
                [jnp.concatenate([cols_out[col][r][sl] for col in range(GC)], axis=0) for sl in sls], axis=1
            )
            change = dot(perm, stack)
            for e, sl in enumerate(sls):
                part = change[:, e * BS : (e + 1) * BS].reshape(SUB, GC, BS)
                out[r, sl] = (a_ref[r, sl].astype(F32) - part).astype(BF)


def vmem(n):
    return [pl.BlockSpec(memory_space=pltpu.VMEM)] * n


def smem(n):
    return [pl.BlockSpec(memory_space=pltpu.SMEM)] * n


def body(front, pivot_inverse, rhs, trail_sol, block_mask, panel_order):
    blocks = front.reshape(NR, BS, NC, BS)
    mask = block_mask.reshape(NR, NC)
    b = rhs.reshape(NR, BS, NRHS)
    y = trail_sol.reshape(NR, BS, NRHS)

    fixed = lambda shape: pl.BlockSpec(shape, lambda g: (0,) * len(shape))
    shapes = [(CPP * BS + EXTRA, BS)] * PIECES + [(NR * BS + 8, BS)]
    *sent, mine = pl.pallas_call(
        prep_kernel,
        out_shape=tuple(jax.ShapeDtypeStruct(shape, BF) for shape in shapes),
        grid=(1,),
        in_specs=[fixed((1, BS, NC, BS)), fixed((NR, BS, 8, BS)), fixed((1, BS, NRHS)), fixed((NR, NC))],
        out_specs=tuple(fixed(shape) for shape in shapes),
        name="prep",
    )(blocks, blocks, b, mask)

    others = [lax.ppermute(mine, "narrow", [(i, (i + d) % 4) for i in range(4)]) for d in (1, 2, 3)]

    pieces = [
        lax.ppermute(sent[p], WIDE, [(i, holder(p, i)) for i in range(NP)]) for p in range(1, PIECES)
    ]
    piece, copies = pl.pallas_call(
        merge_kernel,
        out_shape=(
            jax.ShapeDtypeStruct((CPP * BS, BS), BF),
            jax.ShapeDtypeStruct((NW * 2, EXTRA, BS), BF),
        ),
        in_specs=vmem(PIECES),
        out_specs=tuple(vmem(2)),
        name="merge",
    )(sent[0], *pieces)

    ugath = lax.all_gather(piece, WIDE)

    near = lax.all_to_all(copies, ("chip", "narrow"), 0, 0).reshape(NW // 2, 4, EXTRA, BS)
    far = lax.ppermute(near, "core", [(0, 1), (1, 0)])

    lown, lpiv, tpart, delta, mpiv = pl.pallas_call(
        panel_kernel,
        out_shape=(
            jax.ShapeDtypeStruct((NR * BS, NP * BS), BF),
            jax.ShapeDtypeStruct((NP, NP * BS, BS), BF),
            jax.ShapeDtypeStruct((NW, 8, BS), F32),
            jax.ShapeDtypeStruct((NR * BS, BS), BF),
            jax.ShapeDtypeStruct((NP, BS), jnp.int32),
        ),
        in_specs=smem(1) + vmem(8),
        out_specs=tuple(vmem(5)),
        scratch_shapes=[
            pltpu.VMEM((NP, (NR + NP) * BS, BS), BF),
            pltpu.VMEM((NRHS, NP * BS), F32),
            pltpu.VMEM((NP, 8, BS), F32),
            pltpu.VMEM((NP, NP, 8, BS), F32),
        ],
        name="panel",
    )(panel_order, mine, *others, near, far, pivot_inverse, y)

    zt, frhs = pl.pallas_call(
        forward_kernel,
        out_shape=(
            jax.ShapeDtypeStruct((8, BS), F32),
            jax.ShapeDtypeStruct((NR, BS, NRHS), BF),
        ),
        in_specs=smem(1) + vmem(6),
        out_specs=tuple(vmem(2)),
        scratch_shapes=[
            pltpu.VMEM((NR + NP, BS, NRHS), F32),
            pltpu.VMEM((NRHS, BS), F32),
        ],
        name="forward",
    )(panel_order, near, far, pivot_inverse, b, lown, lpiv)

    h = pl.pallas_call(
        combine_kernel,
        out_shape=jax.ShapeDtypeStruct((8, NR * BS, NP * BS), BF),
        in_specs=smem(1) + vmem(3),
        out_specs=vmem(1)[0],
        name="combine",
    )(panel_order, lown, lpiv, pivot_inverse)

    tparts = lax.all_to_all(tpart, WIDE, 0, 0)
    xg = pl.pallas_call(
        solve_kernel,
        out_shape=jax.ShapeDtypeStruct((NW * 4, 8, BS), BF),
        in_specs=smem(1) + vmem(4) + [pl.BlockSpec(memory_space=pl.ANY)],
        out_specs=vmem(1)[0],
        scratch_shapes=[pltpu.VMEM((NP, 2, BS), F32)],
        name="solve",
    )(panel_order, tparts, zt, lpiv, pivot_inverse, h)
    xall = lax.all_to_all(xg, ("narrow", *WIDE), 0, 0)

    front_out = pl.pallas_call(
        update_kernel,
        out_shape=jax.ShapeDtypeStruct((NR, BS, NC, BS), BF),
        grid=(NC // GC,),
        in_specs=smem(3)
        + [
            pl.BlockSpec((NR, BS, GC, BS), lambda g: (0, 0, g, 0)),
            pl.BlockSpec((8, CPP * BS, BS), lambda g: (g, 0, 0)),
            fixed((8, NR * BS, NP * BS)),
            fixed((NR * BS, BS)),
        ],
        out_specs=pl.BlockSpec((NR, BS, GC, BS), lambda g: (0, 0, g, 0)),
        name="update",
    )(panel_order, mask, mpiv, blocks, ugath.reshape(NW, CPP * BS, BS), h, delta)
    front_out, xall = lax.optimization_barrier((front_out, xall))
    window = xall.reshape(NW * 4, NP, 2, BS).transpose(1, 3, 2, 0).reshape(NP, BS, NRHS)
    return front_out.reshape(front.shape), frhs.reshape(rhs.shape), window


def solution(mesh):
    in_specs = (
        P(None, WIDE, None, None, "narrow", None),
        P(),
        P(None, WIDE, None, None),
        P(None, WIDE, None, None),
        P(None, WIDE, None, "narrow"),
        P(),
    )
    out_specs = (P(None, WIDE, None, None, "narrow", None), P(None, WIDE, None, None), P())
    axes = {"chip": NW // 2, "core": 2, "narrow": 4}
    mesh = Mesh(mesh.devices.reshape(tuple(axes.values())), tuple(axes))

    def step(*args):
        return body(*args)

    step = jax.shard_map(step, mesh=mesh, in_specs=in_specs, out_specs=out_specs, check_vma=False)
    return step
```

```python
import jax
import jax.numpy as jnp
from jax import lax
from jax.experimental import pallas as pl
from jax.experimental.pallas import tpu as pltpu
from jax.sharding import Mesh
from jax.sharding import PartitionSpec as P


BF = jnp.bfloat16
F32 = jnp.float32
BS = 128
NP = 4
NR = 4
NC = 32
NRHS = 256
NW = 32
WIDE = ("chip", "core")
PIECES = 8
CPP = NC // PIECES
SCATTER_ORDER = (4, 5, 2, 3, 6, 7, 1)
SUB = 16
EXTRA = SUB + 8 + 8


def holder(p, i):
    z = i >> 1 if p % 2 == 0 else 3 - (i >> 1)
    return (p >> 1) * 8 + z * 2 + (i & 1)


def dot(a, b, ca=1, cb=0):
    return lax.dot_general(a, b, (((ca,), (cb,)), ((), ())), preferred_element_type=F32)


def ranks_of(order, w):
    rank = [sum(jnp.where(order[s] == i, s, 0) for s in range(NP)) for i in range(NP)]
    own = jnp.int32(NP)
    for i in range(NP):
        own = jnp.where(w == i, rank[i], own)
    return rank, own


def one_hot(rows, fn):
    r = lax.broadcasted_iota(jnp.int32, (rows, BS), 0)
    c = lax.broadcasted_iota(jnp.int32, (rows, BS), 1)
    return jnp.where(fn(r) == c, 1.0, 0.0).astype(BF)


def row_kernel(row_ref, b_ref, mask_ref, *sent):
    q = lax.axis_index("narrow")
    gather = one_hot(BS, lambda r: (r % SUB) * 8 + r // SUB)
    for ct in range(NC // 8):
        for ag in range(BS // SUB):
            native = row_ref[0, ag * SUB : (ag + 1) * SUB, ct * 8 : (ct + 1) * 8, :]
            native = native.astype(F32).reshape(BS, BS).astype(BF)
            blocks = dot(gather, native).astype(BF)
            for e in range(8):
                p, cc = divmod(ct * 8 + e, CPP)
                sent[p][cc * BS + ag * SUB : cc * BS + (ag + 1) * SUB] = blocks[e * SUB : (e + 1) * SUB]
            if ct == 0:
                sent[ag][CPP * BS : CPP * BS + SUB] = blocks[:SUB]
    mask = mask_ref[...].astype(F32)
    widen = one_hot(NC, lambda r: r)
    line = jnp.broadcast_to(dot(mask.astype(BF), widen)[0:1], (8, BS)).astype(BF)
    for p in range(PIECES):
        rows = b_ref[0, p * SUB : (p + 1) * SUB, :].astype(F32)
        rows = jnp.where((q & 2) != 0, rows[8:], rows[:8])
        rows = jnp.where((q & 1) != 0, rows[:, BS:], rows[:, :BS])
        sent[p][CPP * BS + SUB : CPP * BS + SUB + 8] = rows.astype(BF)
        sent[p][CPP * BS + SUB + 8 :] = line


def column_kernel(col_ref, mask_ref, mine):
    pick = one_hot(SUB, lambda r: r * 8)
    for r in range(NR):
        for ag in range(BS // SUB):
            native = col_ref[r, ag * SUB : (ag + 1) * SUB].astype(F32).reshape(BS, BS).astype(BF)
            mine[r * BS + ag * SUB : r * BS + (ag + 1) * SUB] = dot(pick, native).astype(BF)
    first = jnp.broadcast_to(mask_ref[...].astype(F32)[:, 0:1], (NR, BS))
    mine[NR * BS :] = jnp.concatenate([first, jnp.zeros((8 - NR, BS), F32)], axis=0).astype(BF)


def merge_kernel(*refs):
    parts, (piece, copies) = refs[:PIECES], refs[PIECES:]
    first = parts[0][...]
    is_source = lax.axis_index("chip") < 2
    total = jnp.where(is_source, first, jnp.zeros_like(first))
    for part in parts[1:]:
        total = total + part[...]
    piece[...] = total[: CPP * BS]
    for d in range(NW * 2):
        copies[d] = total[CPP * BS :]


def wide_index():
    return lax.axis_index("chip") * 2 + lax.axis_index("core")


def arrivals(near, far):
    core = lax.axis_index("core")
    for ref, c in ((near, core), (far, 1 - core)):
        for zg in range(2):
            for p in range(PIECES):
                z = zg if p % 2 == 0 else 3 - zg
                yield 2 * zg + c, p, ref.at[(p >> 1) * 4 + z]


def panel_kernel(order, own, d1, d2, d3, near, far, w_ref, y_ref,
                 lown, lpiv, tpart, delta, mpiv, pan, tall, mk, mkp):
    w, q = wide_index(), lax.axis_index("narrow")
    rank, own_rank = ranks_of(order, w)
    for d, ref in enumerate((own, d1, d2, d3)):
        k = lax.rem(q - d + 4, 4)
        pan[k, 0 : NR * BS] = ref[0 : NR * BS]
        mk[k] = ref[NR * BS : NR * BS + 8].astype(F32)
    for i, p, tile in arrivals(near, far):
        row = pl.multiple_of(NR * BS + i * BS + p * SUB, SUB)
        for k in range(NP):
            pan[k, pl.ds(row, SUB), :] = tile[k, 0:SUB]
            if p == 0:
                mkp[i, k] = tile[k, SUB + 8 : SUB + 16].astype(F32)
    for i in range(NP):
        mpiv[i : i + 1] = mkp[i, q, 0:1].astype(jnp.int32)
    row_rank = [own_rank, None, None, None] + rank
    for s in range(NP):
        k = order[s]
        weight = w_ref[k]
        left = dot(pan[k], weight)
        parts = []
        for i in range(NR + NP):
            part = left[i * BS : (i + 1) * BS]
            if row_rank[i] is not None:
                part = jnp.where(row_rank[i] > s, part, 0.0)
            parts.append(part.astype(BF))
        lb = jnp.concatenate(parts, axis=0)
        lown[:, s * BS : (s + 1) * BS] = lb[: NR * BS]
        lpiv[s] = lb[NR * BS :]
        for t in range(s + 1, NP):
            j = order[t]
            akj = pan[j, pl.ds(pl.multiple_of(NR * BS + k * BS, BS), BS), :]
            prod = dot(lb, dot(weight, akj, 0, 0).astype(BF))
            for i in range(NR + NP):
                sl = slice(i * BS, (i + 1) * BS)
                m = mk[j, i : i + 1, :] if i < NR else mkp[i - NR, j, 0:1, 0:1]
                pan[j, sl] = (pan[j, sl].astype(F32) - m * prod[sl]).astype(BF)
    delta[...] = (own[0 : NR * BS].astype(F32) - pan[q, 0 : NR * BS].astype(F32)).astype(BF)
    y0 = jnp.where(w < NP, jnp.zeros_like(y_ref[0]), y_ref[0])
    y = jnp.concatenate([y0] + [y_ref[r] for r in range(1, NR)], axis=0)
    tall[...] = dot(y, lown[...], 0, 0)
    for j in range(2):
        mine_cols = tall[pl.ds(pl.multiple_of(j * BS + q * NW, NW), NW), :]
        for s in range(NP):
            tpart[:, s * 2 + j, :] = mine_cols[:, s * BS : (s + 1) * BS]


def forward_kernel(order, near, far, w_ref, b_ref, lown, lpiv, zt, frhs, bs, ztall):
    w, q = wide_index(), lax.axis_index("narrow")
    for r in range(NR):
        bs[r] = b_ref[r].astype(F32)
    for i, p, tile in arrivals(near, far):
        for n in range(4):
            r0 = p * SUB + 8 * (n >> 1)
            c0 = 128 * (n & 1)
            bs[NR + i, r0 : r0 + 8, c0 : c0 + 128] = tile[n, SUB : SUB + 8].astype(F32)
    for s in range(NP):
        k = order[s]
        weight = w_ref[k]
        bk = bs[NR + k].astype(BF)
        z = dot(weight, bk, 0, 0).astype(BF)
        ztall[...] = dot(bk, weight, 0, 0).astype(BF).astype(F32)
        for j in range(2):
            zt[s * 2 + j : s * 2 + j + 1] = ztall[pl.ds(j * BS + q * NW + w, 1), :]
        elim = dot(lown[:, s * BS : (s + 1) * BS], z)
        for i in range(NR):
            bs[i] = (bs[i] - elim[i * BS : (i + 1) * BS]).astype(BF).astype(F32)
        for t in range(s + 1, NP):
            i = order[t]
            elim = dot(lpiv[s, pl.ds(pl.multiple_of(i * BS, BS), BS), :], z)
            bs[NR + i] = (bs[NR + i] - elim).astype(BF).astype(F32)
    for r in range(NR):
        frhs[r] = bs[r].astype(BF)


def solve_kernel(order, parts, zt, lpiv, w_ref, h, out, xs):
    total = jnp.sum(parts[...], axis=0)
    for s in reversed(range(NP)):
        k = order[s]
        acc = total[s * 2 : s * 2 + 2]
        for t in range(s + 1, NP):
            i = order[t]
            acc = acc + dot(xs[i].astype(BF), lpiv[s, pl.ds(pl.multiple_of(i * BS, BS), BS), :])
        c = (zt[s * 2 : s * 2 + 2] - acc).astype(BF)
        xs[k] = dot(c, w_ref[k], 1, 1).astype(BF).astype(F32)
    x = jnp.concatenate([xs[i] for i in range(NP)], axis=0).astype(BF)
    for d in range(NW * 4):
        out[d] = x


def combine_kernel(order, lown, lpiv, w_ref, h):
    def low(t, s):
        return lpiv[s, pl.ds(pl.multiple_of(order[t] * BS, BS), BS), :]

    def right(coeff, s):
        return dot(coeff.astype(BF), w_ref[order[s]], 1, 1).astype(BF)

    base = [lown[:, s * BS : (s + 1) * BS].astype(F32) for s in range(NP)]
    r3 = right(base[3], 3)
    h[14] = r3
    r3_low = [dot(r3, low(3, s)) for s in range(3)]
    for m3 in range(2):
        c3 = [base[s] - r3_low[s] if m3 else base[s] for s in range(3)]
        r2 = right(c3[2], 2)
        h[12 + m3] = r2
        r2_low = [dot(r2, low(2, s)) for s in range(2)]
        for m2 in range(2):
            c2 = [c3[s] - r2_low[s] if m2 else c3[s] for s in range(2)]
            r1 = right(c2[1], 1)
            h[8 + m2 + 2 * m3] = r1
            r1_low = dot(r1, low(1, 0))
            for m1 in range(2):
                r0 = right(c2[0] - r1_low if m1 else c2[0], 0)
                h[m1 + 2 * m2 + 4 * m3] = r0


GC = 8


def update_kernel(order, mown, mpiv, a_ref, u_ref, h, delta, out):
    g = pl.program_id(0)
    rows = lax.broadcasted_iota(jnp.int32, (BS, BS), 0)
    cols = lax.broadcasted_iota(jnp.int32, (BS, BS), 1)
    perm = jnp.where((rows % GC) * SUB + rows // GC == cols, 1.0, 0.0).astype(BF)
    cols_out = []
    for col in range(GC):
        c = g * GC + col
        m1, m2, m3 = (mpiv[order[s], c] for s in range(1, NP))
        left = [h[m1 + 2 * m2 + 4 * m3], h[8 + m2 + 2 * m3], h[12 + m3], h[14]]
        p, cc = divmod(col, CPP)
        raw = []
        for s in range(NP):
            zg, core = order[s] >> 1, order[s] & 1
            z = zg if p == 0 else 3 - zg
            raw.append(u_ref[2 * z + core, cc * BS : (cc + 1) * BS])
        lu = dot(jnp.concatenate(left, axis=1), jnp.concatenate(raw, axis=0))
        parts = []
        for r in range(NR):
            parts.append(jnp.where(mown[r, c] != 0, lu[r * BS : (r + 1) * BS], 0.0).astype(BF))
        if col == 0:
            parts = [jnp.where(g == 0, delta[r * BS : (r + 1) * BS], parts[r]) for r in range(NR)]
        cols_out.append(parts)
    for r in range(NR):
        for ag in range(0, BS // SUB, 2):
            sls = [slice((ag + e) * SUB, (ag + e + 1) * SUB) for e in range(2)]
            stack = jnp.concatenate(
                [jnp.concatenate([cols_out[col][r][sl] for col in range(GC)], axis=0) for sl in sls], axis=1
            )
            change = dot(perm, stack)
            for e, sl in enumerate(sls):
                part = change[:, e * BS : (e + 1) * BS].reshape(SUB, GC, BS)
                out[r, sl] = (a_ref[r, sl].astype(F32) - part).astype(BF)


def vmem(n):
    return [pl.BlockSpec(memory_space=pltpu.VMEM)] * n


def smem(n):
    return [pl.BlockSpec(memory_space=pltpu.SMEM)] * n


def body(front, pivot_inverse, rhs, trail_sol, block_mask, panel_order):
    blocks = front.reshape(NR, BS, NC, BS)
    mask = block_mask.reshape(NR, NC)
    b = rhs.reshape(NR, BS, NRHS)
    y = trail_sol.reshape(NR, BS, NRHS)

    fixed = lambda shape: pl.BlockSpec(shape, lambda g: (0,) * len(shape))
    sent = pl.pallas_call(
        row_kernel,
        out_shape=(jax.ShapeDtypeStruct((CPP * BS + EXTRA, BS), BF),) * PIECES,
        grid=(1,),
        in_specs=[fixed((1, BS, NC, BS)), fixed((1, BS, NRHS)), fixed((NR, NC))],
        out_specs=(fixed((CPP * BS + EXTRA, BS)),) * PIECES,
        name="row",
    )(blocks, b, mask)

    pieces = []
    for p in SCATTER_ORDER:
        pieces.append(lax.ppermute(sent[p], WIDE, [(i, holder(p, i)) for i in range(NP)]))

    mine = pl.pallas_call(
        column_kernel,
        out_shape=jax.ShapeDtypeStruct((NR * BS + 8, BS), BF),
        grid=(1,),
        in_specs=[fixed((NR, BS, 8, BS)), fixed((NR, NC))],
        out_specs=fixed((NR * BS + 8, BS)),
        name="own",
    )(blocks, mask)
    others = [lax.ppermute(mine, "narrow", [(i, (i + d) % 4) for i in range(4)]) for d in (1, 2, 3)]

    piece, copies = pl.pallas_call(
        merge_kernel,
        out_shape=(
            jax.ShapeDtypeStruct((CPP * BS, BS), BF),
            jax.ShapeDtypeStruct((NW * 2, EXTRA, BS), BF),
        ),
        in_specs=vmem(PIECES),
        out_specs=tuple(vmem(2)),
        name="merge",
    )(sent[0], *pieces)

    ugath = lax.all_gather(piece, WIDE)

    near = lax.all_to_all(copies, ("chip", "narrow"), 0, 0).reshape(NW // 2, 4, EXTRA, BS)
    far = lax.ppermute(near, "core", [(0, 1), (1, 0)])

    lown, lpiv, tpart, delta, mpiv = pl.pallas_call(
        panel_kernel,
        out_shape=(
            jax.ShapeDtypeStruct((NR * BS, NP * BS), BF),
            jax.ShapeDtypeStruct((NP, NP * BS, BS), BF),
            jax.ShapeDtypeStruct((NW, 8, BS), F32),
            jax.ShapeDtypeStruct((NR * BS, BS), BF),
            jax.ShapeDtypeStruct((NP, BS), jnp.int32),
        ),
        in_specs=smem(1) + vmem(8),
        out_specs=tuple(vmem(5)),
        scratch_shapes=[
            pltpu.VMEM((NP, (NR + NP) * BS, BS), BF),
            pltpu.VMEM((NRHS, NP * BS), F32),
            pltpu.VMEM((NP, 8, BS), F32),
            pltpu.VMEM((NP, NP, 8, BS), F32),
        ],
        name="panel",
    )(panel_order, mine, *others, near, far, pivot_inverse, y)

    zt, frhs = pl.pallas_call(
        forward_kernel,
        out_shape=(
            jax.ShapeDtypeStruct((8, BS), F32),
            jax.ShapeDtypeStruct((NR, BS, NRHS), BF),
        ),
        in_specs=smem(1) + vmem(6),
        out_specs=tuple(vmem(2)),
        scratch_shapes=[
            pltpu.VMEM((NR + NP, BS, NRHS), F32),
            pltpu.VMEM((NRHS, BS), F32),
        ],
        name="forward",
    )(panel_order, near, far, pivot_inverse, b, lown, lpiv)

    h = pl.pallas_call(
        combine_kernel,
        out_shape=jax.ShapeDtypeStruct((15, NR * BS, BS), BF),
        in_specs=smem(1) + vmem(3),
        out_specs=vmem(1)[0],
        name="combine",
    )(panel_order, lown, lpiv, pivot_inverse)

    tparts = lax.all_to_all(tpart, WIDE, 0, 0)
    xg = pl.pallas_call(
        solve_kernel,
        out_shape=jax.ShapeDtypeStruct((NW * 4, 8, BS), BF),
        in_specs=smem(1) + vmem(4) + [pl.BlockSpec(memory_space=pl.ANY)],
        out_specs=vmem(1)[0],
        scratch_shapes=[pltpu.VMEM((NP, 2, BS), F32)],
        name="solve",
    )(panel_order, tparts, zt, lpiv, pivot_inverse, h)
    xall = lax.all_to_all(xg, ("narrow", *WIDE), 0, 0)

    front_out = pl.pallas_call(
        update_kernel,
        out_shape=jax.ShapeDtypeStruct((NR, BS, NC, BS), BF),
        grid=(NC // GC,),
        in_specs=smem(3)
        + [
            pl.BlockSpec((NR, BS, GC, BS), lambda g: (0, 0, g, 0)),
            pl.BlockSpec((8, CPP * BS, BS), lambda g: (g, 0, 0)),
            fixed((15, NR * BS, BS)),
            fixed((NR * BS, BS)),
        ],
        out_specs=pl.BlockSpec((NR, BS, GC, BS), lambda g: (0, 0, g, 0)),
        name="update",
    )(panel_order, mask, mpiv, blocks, ugath.reshape(NW, CPP * BS, BS), h, delta)
    front_out, xall = lax.optimization_barrier((front_out, xall))
    window = xall.reshape(NW * 4, NP, 2, BS).transpose(1, 3, 2, 0).reshape(NP, BS, NRHS)
    return front_out.reshape(front.shape), frhs.reshape(rhs.shape), window


def solution(mesh):
    in_specs = (
        P(None, WIDE, None, None, "narrow", None),
        P(),
        P(None, WIDE, None, None),
        P(None, WIDE, None, None),
        P(None, WIDE, None, "narrow"),
        P(),
    )
    out_specs = (P(None, WIDE, None, None, "narrow", None), P(None, WIDE, None, None), P())
    axes = {"chip": NW // 2, "core": 2, "narrow": 4}
    mesh = Mesh(mesh.devices.reshape(tuple(axes.values())), tuple(axes))

    def step(*args):
        return body(*args)

    step = jax.shard_map(step, mesh=mesh, in_specs=in_specs, out_specs=out_specs, check_vma=False)
    return step
```

```python
import jax
import jax.numpy as jnp
from jax import lax
from jax.experimental import pallas as pl
from jax.experimental.pallas import tpu as pltpu
from jax.sharding import Mesh
from jax.sharding import PartitionSpec as P


BF = jnp.bfloat16
F32 = jnp.float32
BS = 128
NP = 4
NR = 4
NC = 32
NRHS = 256
NW = 32
WIDE = ("chip", "core")
PIECES = 8
CPP = NC // PIECES
SCATTER_ORDER = (2, 4, 3, 5, 6, 7, 1)
SUB = 16
EXTRA = SUB + 8 + 8


def holder(p, i):
    z = i >> 1 if p % 2 == 0 else 3 - (i >> 1)
    return (p >> 1) * 8 + z * 2 + (i & 1)


def dot(a, b, ca=1, cb=0):
    return lax.dot_general(a, b, (((ca,), (cb,)), ((), ())), preferred_element_type=F32)


def ranks_of(order, w):
    rank = [sum(jnp.where(order[s] == i, s, 0) for s in range(NP)) for i in range(NP)]
    own = jnp.int32(NP)
    for i in range(NP):
        own = jnp.where(w == i, rank[i], own)
    return rank, own


def one_hot(rows, fn):
    r = lax.broadcasted_iota(jnp.int32, (rows, BS), 0)
    c = lax.broadcasted_iota(jnp.int32, (rows, BS), 1)
    return jnp.where(fn(r) == c, 1.0, 0.0).astype(BF)


def row_kernel(row_ref, b_ref, mask_ref, *sent):
    q = lax.axis_index("narrow")
    gather = one_hot(BS, lambda r: (r % SUB) * 8 + r // SUB)
    for ct in range(NC // 8):
        for ag in range(BS // SUB):
            native = row_ref[0, ag * SUB : (ag + 1) * SUB, ct * 8 : (ct + 1) * 8, :]
            native = native.astype(F32).reshape(BS, BS).astype(BF)
            blocks = dot(gather, native).astype(BF)
            for e in range(8):
                p, cc = divmod(ct * 8 + e, CPP)
                sent[p][cc * BS + ag * SUB : cc * BS + (ag + 1) * SUB] = blocks[e * SUB : (e + 1) * SUB]
            if ct == 0:
                sent[ag][CPP * BS : CPP * BS + SUB] = blocks[:SUB]
    mask = mask_ref[...].astype(F32)
    widen = one_hot(NC, lambda r: r)
    line = jnp.broadcast_to(dot(mask.astype(BF), widen)[0:1], (8, BS)).astype(BF)
    for p in range(PIECES):
        rows = b_ref[0, p * SUB : (p + 1) * SUB, :].astype(F32)
        rows = jnp.where((q & 2) != 0, rows[8:], rows[:8])
        rows = jnp.where((q & 1) != 0, rows[:, BS:], rows[:, :BS])
        sent[p][CPP * BS + SUB : CPP * BS + SUB + 8] = rows.astype(BF)
        sent[p][CPP * BS + SUB + 8 :] = line


def column_kernel(col_ref, mask_ref, mine):
    pick = one_hot(SUB, lambda r: r * 8)
    for r in range(NR):
        for ag in range(BS // SUB):
            native = col_ref[r, ag * SUB : (ag + 1) * SUB].astype(F32).reshape(BS, BS).astype(BF)
            mine[r * BS + ag * SUB : r * BS + (ag + 1) * SUB] = dot(pick, native).astype(BF)
    first = jnp.broadcast_to(mask_ref[...].astype(F32)[:, 0:1], (NR, BS))
    mine[NR * BS :] = jnp.concatenate([first, jnp.zeros((8 - NR, BS), F32)], axis=0).astype(BF)


def merge_kernel(*refs):
    parts, (piece, copies) = refs[:PIECES], refs[PIECES:]
    first = parts[0][...]
    is_source = lax.axis_index("chip") < 2
    total = jnp.where(is_source, first, jnp.zeros_like(first))
    for part in parts[1:]:
        total = total + part[...]
    piece[...] = total[: CPP * BS]
    for d in range(NW * 2):
        copies[d] = total[CPP * BS :]


def wide_index():
    return lax.axis_index("chip") * 2 + lax.axis_index("core")


def arrivals(near, far):
    core = lax.axis_index("core")
    for ref, c in ((near, core), (far, 1 - core)):
        for zg in range(2):
            for p in range(PIECES):
                z = zg if p % 2 == 0 else 3 - zg
                yield 2 * zg + c, p, ref.at[(p >> 1) * 4 + z]


def panel_kernel(order, own, d1, d2, d3, near, far, w_ref, y_ref,
                 lown, lpiv, tpart, delta, mpiv, pan, tall, mk, mkp):
    w, q = wide_index(), lax.axis_index("narrow")
    rank, own_rank = ranks_of(order, w)
    for d, ref in enumerate((own, d1, d2, d3)):
        k = lax.rem(q - d + 4, 4)
        pan[k, 0 : NR * BS] = ref[0 : NR * BS]
        mk[k] = ref[NR * BS : NR * BS + 8].astype(F32)
    for i, p, tile in arrivals(near, far):
        row = pl.multiple_of(NR * BS + i * BS + p * SUB, SUB)
        for k in range(NP):
            pan[k, pl.ds(row, SUB), :] = tile[k, 0:SUB]
            if p == 0:
                mkp[i, k] = tile[k, SUB + 8 : SUB + 16].astype(F32)
    for i in range(NP):
        mpiv[i : i + 1] = mkp[i, q, 0:1].astype(jnp.int32)
    row_rank = [own_rank, None, None, None] + rank
    for s in range(NP):
        k = order[s]
        weight = w_ref[k]
        left = dot(pan[k], weight)
        parts = []
        for i in range(NR + NP):
            part = left[i * BS : (i + 1) * BS]
            if row_rank[i] is not None:
                part = jnp.where(row_rank[i] > s, part, 0.0)
            parts.append(part.astype(BF))
        lb = jnp.concatenate(parts, axis=0)
        lown[:, s * BS : (s + 1) * BS] = lb[: NR * BS]
        lpiv[s] = lb[NR * BS :]
        for t in range(s + 1, NP):
            j = order[t]
            akj = pan[j, pl.ds(pl.multiple_of(NR * BS + k * BS, BS), BS), :]
            prod = dot(lb, dot(weight, akj, 0, 0).astype(BF))
            for i in range(NR + NP):
                sl = slice(i * BS, (i + 1) * BS)
                m = mk[j, i : i + 1, :] if i < NR else mkp[i - NR, j, 0:1, 0:1]
                pan[j, sl] = (pan[j, sl].astype(F32) - m * prod[sl]).astype(BF)
    delta[...] = (own[0 : NR * BS].astype(F32) - pan[q, 0 : NR * BS].astype(F32)).astype(BF)
    y0 = jnp.where(w < NP, jnp.zeros_like(y_ref[0]), y_ref[0])
    y = jnp.concatenate([y0] + [y_ref[r] for r in range(1, NR)], axis=0)
    tall[...] = dot(y, lown[...], 0, 0)
    for j in range(2):
        mine_cols = tall[pl.ds(pl.multiple_of(j * BS + q * NW, NW), NW), :]
        for s in range(NP):
            tpart[:, s * 2 + j, :] = mine_cols[:, s * BS : (s + 1) * BS]


def forward_kernel(order, near, far, w_ref, b_ref, lown, lpiv, zt, frhs, bs, ztall):
    w, q = wide_index(), lax.axis_index("narrow")
    for r in range(NR):
        bs[r] = b_ref[r].astype(F32)
    for i, p, tile in arrivals(near, far):
        for n in range(4):
            r0 = p * SUB + 8 * (n >> 1)
            c0 = 128 * (n & 1)
            bs[NR + i, r0 : r0 + 8, c0 : c0 + 128] = tile[n, SUB : SUB + 8].astype(F32)
    for s in range(NP):
        k = order[s]
        weight = w_ref[k]
        bk = bs[NR + k].astype(BF)
        z = dot(weight, bk, 0, 0).astype(BF)
        ztall[...] = dot(bk, weight, 0, 0).astype(BF).astype(F32)
        for j in range(2):
            zt[s * 2 + j : s * 2 + j + 1] = ztall[pl.ds(j * BS + q * NW + w, 1), :]
        elim = dot(lown[:, s * BS : (s + 1) * BS], z)
        for i in range(NR):
            bs[i] = (bs[i] - elim[i * BS : (i + 1) * BS]).astype(BF).astype(F32)
        for t in range(s + 1, NP):
            i = order[t]
            elim = dot(lpiv[s, pl.ds(pl.multiple_of(i * BS, BS), BS), :], z)
            bs[NR + i] = (bs[NR + i] - elim).astype(BF).astype(F32)
    for r in range(NR):
        frhs[r] = bs[r].astype(BF)


def solve_kernel(order, parts, zt, lpiv, w_ref, h, out, xs):
    total = jnp.sum(parts[...], axis=0)
    for s in reversed(range(NP)):
        k = order[s]
        acc = total[s * 2 : s * 2 + 2]
        for t in range(s + 1, NP):
            i = order[t]
            acc = acc + dot(xs[i].astype(BF), lpiv[s, pl.ds(pl.multiple_of(i * BS, BS), BS), :])
        c = (zt[s * 2 : s * 2 + 2] - acc).astype(BF)
        xs[k] = dot(c, w_ref[k], 1, 1).astype(BF).astype(F32)
    x = jnp.concatenate([xs[i] for i in range(NP)], axis=0).astype(BF)
    for d in range(NW * 4):
        out[d] = x


def combine_kernel(order, lown, lpiv, w_ref, h):
    def low(t, s):
        return lpiv[s, pl.ds(pl.multiple_of(order[t] * BS, BS), BS), :]

    def right(coeff, s):
        return dot(coeff.astype(BF), w_ref[order[s]], 1, 1).astype(BF)

    base = [lown[:, s * BS : (s + 1) * BS].astype(F32) for s in range(NP)]
    r3 = right(base[3], 3)
    h[14] = r3
    r3_low = [dot(r3, low(3, s)) for s in range(3)]
    for m3 in range(2):
        c3 = [base[s] - r3_low[s] if m3 else base[s] for s in range(3)]
        r2 = right(c3[2], 2)
        h[12 + m3] = r2
        r2_low = [dot(r2, low(2, s)) for s in range(2)]
        for m2 in range(2):
            c2 = [c3[s] - r2_low[s] if m2 else c3[s] for s in range(2)]
            r1 = right(c2[1], 1)
            h[8 + m2 + 2 * m3] = r1
            r1_low = dot(r1, low(1, 0))
            for m1 in range(2):
                r0 = right(c2[0] - r1_low if m1 else c2[0], 0)
                h[m1 + 2 * m2 + 4 * m3] = r0


def window_kernel(x, out):
    for k in range(NP):
        for j in range(2):
            out[k, :, j * BS : (j + 1) * BS] = x[:, k * 2 + j, :].astype(F32).T.astype(BF)


GC = 8


def update_kernel(order, mown, mpiv, a_ref, u_ref, h, delta, out):
    g = pl.program_id(0)
    rows = lax.broadcasted_iota(jnp.int32, (BS, BS), 0)
    cols = lax.broadcasted_iota(jnp.int32, (BS, BS), 1)
    perm = jnp.where((rows % GC) * SUB + rows // GC == cols, 1.0, 0.0).astype(BF)
    cols_out = []
    for col in range(GC):
        c = g * GC + col
        m1, m2, m3 = (mpiv[order[s], c] for s in range(1, NP))
        left = [h[m1 + 2 * m2 + 4 * m3], h[8 + m2 + 2 * m3], h[12 + m3], h[14]]
        p, cc = divmod(col, CPP)
        raw = []
        for s in range(NP):
            zg, core = order[s] >> 1, order[s] & 1
            z = zg if p == 0 else 3 - zg
            raw.append(u_ref[2 * z + core, cc * BS : (cc + 1) * BS])
        lu = dot(jnp.concatenate(left, axis=1), jnp.concatenate(raw, axis=0))
        parts = []
        for r in range(NR):
            parts.append(jnp.where(mown[r, c] != 0, lu[r * BS : (r + 1) * BS], 0.0).astype(BF))
        if col == 0:
            parts = [jnp.where(g == 0, delta[r * BS : (r + 1) * BS], parts[r]) for r in range(NR)]
        cols_out.append(parts)
    for r in range(NR):
        for ag in range(0, BS // SUB, 2):
            sls = [slice((ag + e) * SUB, (ag + e + 1) * SUB) for e in range(2)]
            stack = jnp.concatenate(
                [jnp.concatenate([cols_out[col][r][sl] for col in range(GC)], axis=0) for sl in sls], axis=1
            )
            change = dot(perm, stack)
            for e, sl in enumerate(sls):
                part = change[:, e * BS : (e + 1) * BS].reshape(SUB, GC, BS)
                out[r, sl] = (a_ref[r, sl].astype(F32) - part).astype(BF)


def vmem(n):
    return [pl.BlockSpec(memory_space=pltpu.VMEM)] * n


def smem(n):
    return [pl.BlockSpec(memory_space=pltpu.SMEM)] * n


def body(front, pivot_inverse, rhs, trail_sol, block_mask, panel_order):
    blocks = front.reshape(NR, BS, NC, BS)
    mask = block_mask.reshape(NR, NC)
    b = rhs.reshape(NR, BS, NRHS)
    y = trail_sol.reshape(NR, BS, NRHS)

    fixed = lambda shape: pl.BlockSpec(shape, lambda g: (0,) * len(shape))
    sent = pl.pallas_call(
        row_kernel,
        out_shape=(jax.ShapeDtypeStruct((CPP * BS + EXTRA, BS), BF),) * PIECES,
        grid=(1,),
        in_specs=[fixed((1, BS, NC, BS)), fixed((1, BS, NRHS)), fixed((NR, NC))],
        out_specs=(fixed((CPP * BS + EXTRA, BS)),) * PIECES,
        name="row",
    )(blocks, b, mask)

    pieces = []
    for p in SCATTER_ORDER:
        pieces.append(lax.ppermute(sent[p], WIDE, [(i, holder(p, i)) for i in range(NP)]))

    mine = pl.pallas_call(
        column_kernel,
        out_shape=jax.ShapeDtypeStruct((NR * BS + 8, BS), BF),
        grid=(1,),
        in_specs=[fixed((NR, BS, 8, BS)), fixed((NR, NC))],
        out_specs=fixed((NR * BS + 8, BS)),
        name="own",
    )(blocks, mask)
    others = [lax.ppermute(mine, "narrow", [(i, (i + d) % 4) for i in range(4)]) for d in (1, 2, 3)]

    piece, copies = pl.pallas_call(
        merge_kernel,
        out_shape=(
            jax.ShapeDtypeStruct((CPP * BS, BS), BF),
            jax.ShapeDtypeStruct((NW * 2, EXTRA, BS), BF),
        ),
        in_specs=vmem(PIECES),
        out_specs=tuple(vmem(2)),
        name="merge",
    )(sent[0], *pieces)

    ugath = lax.all_gather(piece, WIDE)

    near = lax.all_to_all(copies, ("chip", "narrow"), 0, 0).reshape(NW // 2, 4, EXTRA, BS)
    near, others = lax.optimization_barrier((near, others))
    far = lax.ppermute(near, "core", [(0, 1), (1, 0)])

    lown, lpiv, tpart, delta, mpiv = pl.pallas_call(
        panel_kernel,
        out_shape=(
            jax.ShapeDtypeStruct((NR * BS, NP * BS), BF),
            jax.ShapeDtypeStruct((NP, NP * BS, BS), BF),
            jax.ShapeDtypeStruct((NW, 8, BS), F32),
            jax.ShapeDtypeStruct((NR * BS, BS), BF),
            jax.ShapeDtypeStruct((NP, BS), jnp.int32),
        ),
        in_specs=smem(1) + vmem(8),
        out_specs=tuple(vmem(5)),
        scratch_shapes=[
            pltpu.VMEM((NP, (NR + NP) * BS, BS), BF),
            pltpu.VMEM((NRHS, NP * BS), F32),
            pltpu.VMEM((NP, 8, BS), F32),
            pltpu.VMEM((NP, NP, 8, BS), F32),
        ],
        name="panel",
    )(panel_order, mine, *others, near, far, pivot_inverse, y)

    zt, frhs = pl.pallas_call(
        forward_kernel,
        out_shape=(
            jax.ShapeDtypeStruct((8, BS), F32),
            jax.ShapeDtypeStruct((NR, BS, NRHS), BF),
        ),
        in_specs=smem(1) + vmem(6),
        out_specs=tuple(vmem(2)),
        scratch_shapes=[
            pltpu.VMEM((NR + NP, BS, NRHS), F32),
            pltpu.VMEM((NRHS, BS), F32),
        ],
        name="forward",
    )(panel_order, near, far, pivot_inverse, b, lown, lpiv)

    h = pl.pallas_call(
        combine_kernel,
        out_shape=jax.ShapeDtypeStruct((15, NR * BS, BS), BF),
        in_specs=smem(1) + vmem(3),
        out_specs=vmem(1)[0],
        name="combine",
    )(panel_order, lown, lpiv, pivot_inverse)

    tparts = lax.all_to_all(tpart, WIDE, 0, 0)
    xg = pl.pallas_call(
        solve_kernel,
        out_shape=jax.ShapeDtypeStruct((NW * 4, 8, BS), BF),
        in_specs=smem(1) + vmem(4) + [pl.BlockSpec(memory_space=pl.ANY)],
        out_specs=vmem(1)[0],
        scratch_shapes=[pltpu.VMEM((NP, 2, BS), F32)],
        name="solve",
    )(panel_order, tparts, zt, lpiv, pivot_inverse, h)
    xall = lax.all_to_all(xg, ("narrow", *WIDE), 0, 0)

    front_out = pl.pallas_call(
        update_kernel,
        out_shape=jax.ShapeDtypeStruct((NR, BS, NC, BS), BF),
        grid=(NC // GC,),
        in_specs=smem(3)
        + [
            pl.BlockSpec((NR, BS, GC, BS), lambda g: (0, 0, g, 0)),
            pl.BlockSpec((8, CPP * BS, BS), lambda g: (g, 0, 0)),
            fixed((15, NR * BS, BS)),
            fixed((NR * BS, BS)),
        ],
        out_specs=pl.BlockSpec((NR, BS, GC, BS), lambda g: (0, 0, g, 0)),
        name="update",
    )(panel_order, mask, mpiv, blocks, ugath.reshape(NW, CPP * BS, BS), h, delta)
    front_out, xall = lax.optimization_barrier((front_out, xall))
    window = pl.pallas_call(
        window_kernel,
        out_shape=jax.ShapeDtypeStruct((NP, BS, NRHS), BF),
        in_specs=vmem(1),
        out_specs=vmem(1)[0],
        name="window",
    )(xall)
    return front_out.reshape(front.shape), frhs.reshape(rhs.shape), window


def solution(mesh):
    in_specs = (
        P(None, WIDE, None, None, "narrow", None),
        P(),
        P(None, WIDE, None, None),
        P(None, WIDE, None, None),
        P(None, WIDE, None, "narrow"),
        P(),
    )
    out_specs = (P(None, WIDE, None, None, "narrow", None), P(None, WIDE, None, None), P())
    axes = {"chip": NW // 2, "core": 2, "narrow": 4}
    mesh = Mesh(mesh.devices.reshape(tuple(axes.values())), tuple(axes))

    def step(*args):
        return body(*args)

    step = jax.shard_map(step, mesh=mesh, in_specs=in_specs, out_specs=out_specs, check_vma=False)
    return step
```

```python
import jax
import jax.numpy as jnp
from jax import lax
from jax.experimental import pallas as pl
from jax.experimental.pallas import tpu as pltpu
from jax.sharding import Mesh
from jax.sharding import PartitionSpec as P


BF = jnp.bfloat16
F32 = jnp.float32
BS = 128
NP = 4
NR = 4
NC = 32
NRHS = 256
NW = 32
WIDE = ("chip", "core")
PIECES = 8
CPP = NC // PIECES
SCATTER_ORDER = (2, 4, 3, 5, 6, 7, 1)
SUB = 16
EXTRA = SUB + 8 + 8


def holder(p, i):
    z = i >> 1 if p % 2 == 0 else 3 - (i >> 1)
    return (p >> 1) * 8 + z * 2 + (i & 1)


def dot(a, b, ca=1, cb=0):
    return lax.dot_general(a, b, (((ca,), (cb,)), ((), ())), preferred_element_type=F32)


def ranks_of(order, w):
    rank = [sum(jnp.where(order[s] == i, s, 0) for s in range(NP)) for i in range(NP)]
    own = jnp.int32(NP)
    for i in range(NP):
        own = jnp.where(w == i, rank[i], own)
    return rank, own


def one_hot(rows, fn):
    r = lax.broadcasted_iota(jnp.int32, (rows, BS), 0)
    c = lax.broadcasted_iota(jnp.int32, (rows, BS), 1)
    return jnp.where(fn(r) == c, 1.0, 0.0).astype(BF)


def prep_kernel(row_ref, col_ref, b_ref, mask_ref, *outs):
    q = lax.axis_index("narrow")
    sent, mine = outs[:PIECES], outs[PIECES]
    gather = one_hot(BS, lambda r: (r % SUB) * 8 + r // SUB)
    for ct in range(NC // 8):
        for ag in range(BS // SUB):
            native = row_ref[0, ag * SUB : (ag + 1) * SUB, ct * 8 : (ct + 1) * 8, :]
            native = native.astype(F32).reshape(BS, BS).astype(BF)
            blocks = dot(gather, native).astype(BF)
            for e in range(8):
                p, cc = divmod(ct * 8 + e, CPP)
                sent[p][cc * BS + ag * SUB : cc * BS + (ag + 1) * SUB] = blocks[e * SUB : (e + 1) * SUB]
            if ct == 0:
                sent[ag][CPP * BS : CPP * BS + SUB] = blocks[:SUB]
    mask = mask_ref[...].astype(F32)
    widen = one_hot(NC, lambda r: r)
    line = jnp.broadcast_to(dot(mask.astype(BF), widen)[0:1], (8, BS)).astype(BF)
    for p in range(PIECES):
        rows = b_ref[0, p * SUB : (p + 1) * SUB, :].astype(F32)
        rows = jnp.where((q & 2) != 0, rows[8:], rows[:8])
        rows = jnp.where((q & 1) != 0, rows[:, BS:], rows[:, :BS])
        sent[p][CPP * BS + SUB : CPP * BS + SUB + 8] = rows.astype(BF)
        sent[p][CPP * BS + SUB + 8 :] = line
    pick = one_hot(SUB, lambda r: r * 8)
    for r in range(NR):
        for ag in range(BS // SUB):
            native = col_ref[r, ag * SUB : (ag + 1) * SUB].astype(F32).reshape(BS, BS).astype(BF)
            mine[r * BS + ag * SUB : r * BS + (ag + 1) * SUB] = dot(pick, native).astype(BF)
    first = jnp.broadcast_to(mask[:, 0:1], (NR, BS))
    mine[NR * BS :] = jnp.concatenate([first, jnp.zeros((8 - NR, BS), F32)], axis=0).astype(BF)


def merge_kernel(*refs):
    parts, (piece, copies) = refs[:PIECES], refs[PIECES:]
    first = parts[0][...]
    is_source = lax.axis_index("chip") < 2
    total = jnp.where(is_source, first, jnp.zeros_like(first))
    for part in parts[1:]:
        total = total + part[...]
    piece[...] = total[: CPP * BS]
    for d in range(NW * 2):
        copies[d] = total[CPP * BS :]


def wide_index():
    return lax.axis_index("chip") * 2 + lax.axis_index("core")


def arrivals(near, far):
    core = lax.axis_index("core")
    for ref, c in ((near, core), (far, 1 - core)):
        for zg in range(2):
            for p in range(PIECES):
                z = zg if p % 2 == 0 else 3 - zg
                yield 2 * zg + c, p, ref.at[(p >> 1) * 4 + z]


def panel_kernel(order, own, d1, d2, d3, near, far, w_ref, y_ref,
                 lown, lpiv, tpart, delta, mpiv, pan, tall, mk, mkp):
    w, q = wide_index(), lax.axis_index("narrow")
    rank, own_rank = ranks_of(order, w)
    for d, ref in enumerate((own, d1, d2, d3)):
        k = lax.rem(q - d + 4, 4)
        pan[k, 0 : NR * BS] = ref[0 : NR * BS]
        mk[k] = ref[NR * BS : NR * BS + 8].astype(F32)
    for i, p, tile in arrivals(near, far):
        row = pl.multiple_of(NR * BS + i * BS + p * SUB, SUB)
        for k in range(NP):
            pan[k, pl.ds(row, SUB), :] = tile[k, 0:SUB]
            if p == 0:
                mkp[i, k] = tile[k, SUB + 8 : SUB + 16].astype(F32)
    for i in range(NP):
        mpiv[i : i + 1] = mkp[i, q, 0:1].astype(jnp.int32)
    row_rank = [own_rank, None, None, None] + rank
    for s in range(NP):
        k = order[s]
        weight = w_ref[k]
        left = dot(pan[k], weight)
        parts = []
        for i in range(NR + NP):
            part = left[i * BS : (i + 1) * BS]
            if row_rank[i] is not None:
                part = jnp.where(row_rank[i] > s, part, 0.0)
            parts.append(part.astype(BF))
        lb = jnp.concatenate(parts, axis=0)
        lown[:, s * BS : (s + 1) * BS] = lb[: NR * BS]
        lpiv[s] = lb[NR * BS :]
        for t in range(s + 1, NP):
            j = order[t]
            akj = pan[j, pl.ds(pl.multiple_of(NR * BS + k * BS, BS), BS), :]
            prod = dot(lb, dot(weight, akj, 0, 0).astype(BF))
            for i in range(NR + NP):
                sl = slice(i * BS, (i + 1) * BS)
                m = mk[j, i : i + 1, :] if i < NR else mkp[i - NR, j, 0:1, 0:1]
                pan[j, sl] = (pan[j, sl].astype(F32) - m * prod[sl]).astype(BF)
    delta[...] = (own[0 : NR * BS].astype(F32) - pan[q, 0 : NR * BS].astype(F32)).astype(BF)
    y0 = jnp.where(w < NP, jnp.zeros_like(y_ref[0]), y_ref[0])
    y = jnp.concatenate([y0] + [y_ref[r] for r in range(1, NR)], axis=0)
    tall[...] = dot(y, lown[...], 0, 0)
    for j in range(2):
        mine_cols = tall[pl.ds(pl.multiple_of(j * BS + q * NW, NW), NW), :]
        for s in range(NP):
            tpart[:, s * 2 + j, :] = mine_cols[:, s * BS : (s + 1) * BS]


def forward_kernel(order, near, far, w_ref, b_ref, lown, lpiv, zt, frhs, bs, ztall):
    w, q = wide_index(), lax.axis_index("narrow")
    for r in range(NR):
        bs[r] = b_ref[r].astype(F32)
    for i, p, tile in arrivals(near, far):
        for n in range(4):
            r0 = p * SUB + 8 * (n >> 1)
            c0 = 128 * (n & 1)
            bs[NR + i, r0 : r0 + 8, c0 : c0 + 128] = tile[n, SUB : SUB + 8].astype(F32)
    for s in range(NP):
        k = order[s]
        weight = w_ref[k]
        bk = bs[NR + k].astype(BF)
        z = dot(weight, bk, 0, 0).astype(BF)
        ztall[...] = dot(bk, weight, 0, 0).astype(BF).astype(F32)
        for j in range(2):
            zt[s * 2 + j : s * 2 + j + 1] = ztall[pl.ds(j * BS + q * NW + w, 1), :]
        elim = dot(lown[:, s * BS : (s + 1) * BS], z)
        for i in range(NR):
            bs[i] = (bs[i] - elim[i * BS : (i + 1) * BS]).astype(BF).astype(F32)
        for t in range(s + 1, NP):
            i = order[t]
            elim = dot(lpiv[s, pl.ds(pl.multiple_of(i * BS, BS), BS), :], z)
            bs[NR + i] = (bs[NR + i] - elim).astype(BF).astype(F32)
    for r in range(NR):
        frhs[r] = bs[r].astype(BF)


def solve_kernel(order, parts, zt, lpiv, w_ref, h, out, xs):
    total = jnp.sum(parts[...], axis=0)
    for s in reversed(range(NP)):
        k = order[s]
        acc = total[s * 2 : s * 2 + 2]
        for t in range(s + 1, NP):
            i = order[t]
            acc = acc + dot(xs[i].astype(BF), lpiv[s, pl.ds(pl.multiple_of(i * BS, BS), BS), :])
        c = (zt[s * 2 : s * 2 + 2] - acc).astype(BF)
        xs[k] = dot(c, w_ref[k], 1, 1).astype(BF).astype(F32)
    x = jnp.concatenate([xs[i] for i in range(NP)], axis=0).astype(BF)
    for d in range(NW * 4):
        out[d] = x


def combine_kernel(order, lown, lpiv, w_ref, h):
    def low(t, s):
        return lpiv[s, pl.ds(pl.multiple_of(order[t] * BS, BS), BS), :]

    def right(coeff, s):
        return dot(coeff.astype(BF), w_ref[order[s]], 1, 1).astype(BF)

    base = [lown[:, s * BS : (s + 1) * BS].astype(F32) for s in range(NP)]
    r3 = right(base[3], 3)
    h[14] = r3
    r3_low = [dot(r3, low(3, s)) for s in range(3)]
    for m3 in range(2):
        c3 = [base[s] - r3_low[s] if m3 else base[s] for s in range(3)]
        r2 = right(c3[2], 2)
        h[12 + m3] = r2
        r2_low = [dot(r2, low(2, s)) for s in range(2)]
        for m2 in range(2):
            c2 = [c3[s] - r2_low[s] if m2 else c3[s] for s in range(2)]
            r1 = right(c2[1], 1)
            h[8 + m2 + 2 * m3] = r1
            r1_low = dot(r1, low(1, 0))
            for m1 in range(2):
                r0 = right(c2[0] - r1_low if m1 else c2[0], 0)
                h[m1 + 2 * m2 + 4 * m3] = r0


GC = 8


def update_kernel(order, mown, mpiv, a_ref, u_ref, h, delta, out):
    g = pl.program_id(0)
    rows = lax.broadcasted_iota(jnp.int32, (BS, BS), 0)
    cols = lax.broadcasted_iota(jnp.int32, (BS, BS), 1)
    perm = jnp.where((rows % GC) * SUB + rows // GC == cols, 1.0, 0.0).astype(BF)
    cols_out = []
    for col in range(GC):
        c = g * GC + col
        m1, m2, m3 = (mpiv[order[s], c] for s in range(1, NP))
        left = [h[m1 + 2 * m2 + 4 * m3], h[8 + m2 + 2 * m3], h[12 + m3], h[14]]
        p, cc = divmod(col, CPP)
        raw = []
        for s in range(NP):
            zg, core = order[s] >> 1, order[s] & 1
            z = zg if p == 0 else 3 - zg
            raw.append(u_ref[2 * z + core, cc * BS : (cc + 1) * BS])
        lu = dot(jnp.concatenate(left, axis=1), jnp.concatenate(raw, axis=0))
        parts = []
        for r in range(NR):
            parts.append(jnp.where(mown[r, c] != 0, lu[r * BS : (r + 1) * BS], 0.0).astype(BF))
        if col == 0:
            parts = [jnp.where(g == 0, delta[r * BS : (r + 1) * BS], parts[r]) for r in range(NR)]
        cols_out.append(parts)
    for r in range(NR):
        for ag in range(0, BS // SUB, 2):
            sls = [slice((ag + e) * SUB, (ag + e + 1) * SUB) for e in range(2)]
            stack = jnp.concatenate(
                [jnp.concatenate([cols_out[col][r][sl] for col in range(GC)], axis=0) for sl in sls], axis=1
            )
            change = dot(perm, stack)
            for e, sl in enumerate(sls):
                part = change[:, e * BS : (e + 1) * BS].reshape(SUB, GC, BS)
                out[r, sl] = (a_ref[r, sl].astype(F32) - part).astype(BF)


def vmem(n):
    return [pl.BlockSpec(memory_space=pltpu.VMEM)] * n


def smem(n):
    return [pl.BlockSpec(memory_space=pltpu.SMEM)] * n


def body(front, pivot_inverse, rhs, trail_sol, block_mask, panel_order):
    blocks = front.reshape(NR, BS, NC, BS)
    mask = block_mask.reshape(NR, NC)
    b = rhs.reshape(NR, BS, NRHS)
    y = trail_sol.reshape(NR, BS, NRHS)

    fixed = lambda shape: pl.BlockSpec(shape, lambda g: (0,) * len(shape))
    shapes = [(CPP * BS + EXTRA, BS)] * PIECES + [(NR * BS + 8, BS)]
    *sent, mine = pl.pallas_call(
        prep_kernel,
        out_shape=tuple(jax.ShapeDtypeStruct(shape, BF) for shape in shapes),
        grid=(1,),
        in_specs=[fixed((1, BS, NC, BS)), fixed((NR, BS, 8, BS)), fixed((1, BS, NRHS)), fixed((NR, NC))],
        out_specs=tuple(fixed(shape) for shape in shapes),
        name="prep",
    )(blocks, blocks, b, mask)

    pieces = []
    for p in SCATTER_ORDER:
        pieces.append(lax.ppermute(sent[p], WIDE, [(i, holder(p, i)) for i in range(NP)]))

    others = [lax.ppermute(mine, "narrow", [(i, (i + d) % 4) for i in range(4)]) for d in (1, 2, 3)]

    piece, copies = pl.pallas_call(
        merge_kernel,
        out_shape=(
            jax.ShapeDtypeStruct((CPP * BS, BS), BF),
            jax.ShapeDtypeStruct((NW * 2, EXTRA, BS), BF),
        ),
        in_specs=vmem(PIECES),
        out_specs=tuple(vmem(2)),
        name="merge",
    )(sent[0], *pieces)

    ugath = lax.all_gather(piece, WIDE)

    near = lax.all_to_all(copies, ("chip", "narrow"), 0, 0).reshape(NW // 2, 4, EXTRA, BS)
    far = lax.ppermute(near, "core", [(0, 1), (1, 0)])

    lown, lpiv, tpart, delta, mpiv = pl.pallas_call(
        panel_kernel,
        out_shape=(
            jax.ShapeDtypeStruct((NR * BS, NP * BS), BF),
            jax.ShapeDtypeStruct((NP, NP * BS, BS), BF),
            jax.ShapeDtypeStruct((NW, 8, BS), F32),
            jax.ShapeDtypeStruct((NR * BS, BS), BF),
            jax.ShapeDtypeStruct((NP, BS), jnp.int32),
        ),
        in_specs=smem(1) + vmem(8),
        out_specs=tuple(vmem(5)),
        scratch_shapes=[
            pltpu.VMEM((NP, (NR + NP) * BS, BS), BF),
            pltpu.VMEM((NRHS, NP * BS), F32),
            pltpu.VMEM((NP, 8, BS), F32),
            pltpu.VMEM((NP, NP, 8, BS), F32),
        ],
        name="panel",
    )(panel_order, mine, *others, near, far, pivot_inverse, y)

    zt, frhs = pl.pallas_call(
        forward_kernel,
        out_shape=(
            jax.ShapeDtypeStruct((8, BS), F32),
            jax.ShapeDtypeStruct((NR, BS, NRHS), BF),
        ),
        in_specs=smem(1) + vmem(6),
        out_specs=tuple(vmem(2)),
        scratch_shapes=[
            pltpu.VMEM((NR + NP, BS, NRHS), F32),
            pltpu.VMEM((NRHS, BS), F32),
        ],
        name="forward",
    )(panel_order, near, far, pivot_inverse, b, lown, lpiv)

    h = pl.pallas_call(
        combine_kernel,
        out_shape=jax.ShapeDtypeStruct((15, NR * BS, BS), BF),
        in_specs=smem(1) + vmem(3),
        out_specs=vmem(1)[0],
        name="combine",
    )(panel_order, lown, lpiv, pivot_inverse)

    tparts = lax.all_to_all(tpart, WIDE, 0, 0)
    xg = pl.pallas_call(
        solve_kernel,
        out_shape=jax.ShapeDtypeStruct((NW * 4, 8, BS), BF),
        in_specs=smem(1) + vmem(4) + [pl.BlockSpec(memory_space=pl.ANY)],
        out_specs=vmem(1)[0],
        scratch_shapes=[pltpu.VMEM((NP, 2, BS), F32)],
        name="solve",
    )(panel_order, tparts, zt, lpiv, pivot_inverse, h)
    xall = lax.all_to_all(xg, ("narrow", *WIDE), 0, 0)

    front_out = pl.pallas_call(
        update_kernel,
        out_shape=jax.ShapeDtypeStruct((NR, BS, NC, BS), BF),
        grid=(NC // GC,),
        in_specs=smem(3)
        + [
            pl.BlockSpec((NR, BS, GC, BS), lambda g: (0, 0, g, 0)),
            pl.BlockSpec((8, CPP * BS, BS), lambda g: (g, 0, 0)),
            fixed((15, NR * BS, BS)),
            fixed((NR * BS, BS)),
        ],
        out_specs=pl.BlockSpec((NR, BS, GC, BS), lambda g: (0, 0, g, 0)),
        name="update",
    )(panel_order, mask, mpiv, blocks, ugath.reshape(NW, CPP * BS, BS), h, delta)
    front_out, xall = lax.optimization_barrier((front_out, xall))
    window = xall.reshape(NW * 4, NP, 2, BS).transpose(1, 3, 2, 0).reshape(NP, BS, NRHS)
    return front_out.reshape(front.shape), frhs.reshape(rhs.shape), window


def solution(mesh):
    in_specs = (
        P(None, WIDE, None, None, "narrow", None),
        P(),
        P(None, WIDE, None, None),
        P(None, WIDE, None, None),
        P(None, WIDE, None, "narrow"),
        P(),
    )
    out_specs = (P(None, WIDE, None, None, "narrow", None), P(None, WIDE, None, None), P())
    axes = {"chip": NW // 2, "core": 2, "narrow": 4}
    mesh = Mesh(mesh.devices.reshape(tuple(axes.values())), tuple(axes))

    def step(*args):
        return body(*args)

    step = jax.shard_map(step, mesh=mesh, in_specs=in_specs, out_specs=out_specs, check_vma=False)
    return step
```

```python
import jax
import jax.numpy as jnp
from jax import lax
from jax.experimental import pallas as pl
from jax.experimental.pallas import tpu as pltpu
from jax.sharding import Mesh
from jax.sharding import PartitionSpec as P


BF = jnp.bfloat16
F32 = jnp.float32
BS = 128
NP = 4
NR = 4
NC = 32
NRHS = 256
NW = 32
WIDE = ("chip", "core")
PIECES = 8
CPP = NC // PIECES
SCATTER_ORDER = (2, 4, 3, 5, 6, 7, 1)
SUB = 16
EXTRA = SUB + 8 + 8


def holder(p, i):
    z = i >> 1 if p % 2 == 0 else 3 - (i >> 1)
    return (p >> 1) * 8 + z * 2 + (i & 1)


def dot(a, b, ca=1, cb=0):
    return lax.dot_general(a, b, (((ca,), (cb,)), ((), ())), preferred_element_type=F32)


def ranks_of(order, w):
    rank = [sum(jnp.where(order[s] == i, s, 0) for s in range(NP)) for i in range(NP)]
    own = jnp.int32(NP)
    for i in range(NP):
        own = jnp.where(w == i, rank[i], own)
    return rank, own


def one_hot(rows, fn):
    r = lax.broadcasted_iota(jnp.int32, (rows, BS), 0)
    c = lax.broadcasted_iota(jnp.int32, (rows, BS), 1)
    return jnp.where(fn(r) == c, 1.0, 0.0).astype(BF)


def prep_kernel(row_ref, col_ref, b_ref, mask_ref, *outs):
    q = lax.axis_index("narrow")
    sent, mine = outs[:PIECES], outs[PIECES]
    gather = one_hot(BS, lambda r: (r % SUB) * 8 + r // SUB)
    for ct in range(NC // 8):
        for ag in range(BS // SUB):
            native = row_ref[0, ag * SUB : (ag + 1) * SUB, ct * 8 : (ct + 1) * 8, :]
            native = native.astype(F32).reshape(BS, BS).astype(BF)
            blocks = dot(gather, native).astype(BF)
            for e in range(8):
                p, cc = divmod(ct * 8 + e, CPP)
                sent[p][cc * BS + ag * SUB : cc * BS + (ag + 1) * SUB] = blocks[e * SUB : (e + 1) * SUB]
            if ct == 0:
                sent[ag][CPP * BS : CPP * BS + SUB] = blocks[:SUB]
    mask = mask_ref[...].astype(F32)
    widen = one_hot(NC, lambda r: r)
    line = jnp.broadcast_to(dot(mask.astype(BF), widen)[0:1], (8, BS)).astype(BF)
    for p in range(PIECES):
        rows = b_ref[0, p * SUB : (p + 1) * SUB, :].astype(F32)
        rows = jnp.where((q & 2) != 0, rows[8:], rows[:8])
        rows = jnp.where((q & 1) != 0, rows[:, BS:], rows[:, :BS])
        sent[p][CPP * BS + SUB : CPP * BS + SUB + 8] = rows.astype(BF)
        sent[p][CPP * BS + SUB + 8 :] = line
    pick = one_hot(SUB, lambda r: r * 8)
    for r in range(NR):
        for ag in range(BS // SUB):
            native = col_ref[r, ag * SUB : (ag + 1) * SUB].astype(F32).reshape(BS, BS).astype(BF)
            mine[r * BS + ag * SUB : r * BS + (ag + 1) * SUB] = dot(pick, native).astype(BF)
    first = jnp.broadcast_to(mask[:, 0:1], (NR, BS))
    mine[NR * BS :] = jnp.concatenate([first, jnp.zeros((8 - NR, BS), F32)], axis=0).astype(BF)


def merge_kernel(*refs):
    parts, (piece, copies) = refs[:PIECES], refs[PIECES:]
    first = parts[0][...]
    is_source = lax.axis_index("chip") < 2
    total = parts[1][...]
    for part in parts[2:]:
        total = total + part[...]
    total = jnp.where(is_source, first, total)
    piece[...] = total[: CPP * BS]
    for d in range(NW * 2):
        copies[d] = total[CPP * BS :]


def wide_index():
    return lax.axis_index("chip") * 2 + lax.axis_index("core")


def arrivals(near, far):
    core = lax.axis_index("core")
    for ref, c in ((near, core), (far, 1 - core)):
        for zg in range(2):
            for p in range(PIECES):
                z = zg if p % 2 == 0 else 3 - zg
                yield 2 * zg + c, p, ref.at[(p >> 1) * 4 + z]


def panel_kernel(order, own, d1, d2, d3, near, far, w_ref, y_ref,
                 lown, lpiv, tpart, delta, mpiv, pan, tall, mk, mkp):
    w, q = wide_index(), lax.axis_index("narrow")
    rank, own_rank = ranks_of(order, w)
    for d, ref in enumerate((own, d1, d2, d3)):
        k = lax.rem(q - d + 4, 4)
        pan[k, 0 : NR * BS] = ref[0 : NR * BS]
        mk[k] = ref[NR * BS : NR * BS + 8].astype(F32)
    for i, p, tile in arrivals(near, far):
        row = pl.multiple_of(NR * BS + i * BS + p * SUB, SUB)
        for k in range(NP):
            pan[k, pl.ds(row, SUB), :] = tile[k, 0:SUB]
            if p == 0:
                mkp[i, k] = tile[k, SUB + 8 : SUB + 16].astype(F32)
    for i in range(NP):
        mpiv[i : i + 1] = mkp[i, q, 0:1].astype(jnp.int32)
    row_rank = [own_rank, None, None, None] + rank
    for s in range(NP):
        k = order[s]
        weight = w_ref[k]
        left = dot(pan[k], weight)
        parts = []
        for i in range(NR + NP):
            part = left[i * BS : (i + 1) * BS]
            if row_rank[i] is not None:
                part = jnp.where(row_rank[i] > s, part, 0.0)
            parts.append(part.astype(BF))
        lb = jnp.concatenate(parts, axis=0)
        lown[:, s * BS : (s + 1) * BS] = lb[: NR * BS]
        lpiv[s] = lb[NR * BS :]
        for t in range(s + 1, NP):
            j = order[t]
            akj = pan[j, pl.ds(pl.multiple_of(NR * BS + k * BS, BS), BS), :]
            prod = dot(lb, dot(weight, akj, 0, 0).astype(BF))
            for i in range(NR + NP):
                sl = slice(i * BS, (i + 1) * BS)
                m = mk[j, i : i + 1, :] if i < NR else mkp[i - NR, j, 0:1, 0:1]
                pan[j, sl] = (pan[j, sl].astype(F32) - m * prod[sl]).astype(BF)
    delta[...] = (own[0 : NR * BS].astype(F32) - pan[q, 0 : NR * BS].astype(F32)).astype(BF)
    y0 = jnp.where(w < NP, jnp.zeros_like(y_ref[0]), y_ref[0])
    y = jnp.concatenate([y0] + [y_ref[r] for r in range(1, NR)], axis=0)
    tall[...] = dot(y, lown[...], 0, 0)
    for j in range(2):
        mine_cols = tall[pl.ds(pl.multiple_of(j * BS + q * NW, NW), NW), :]
        for s in range(NP):
            tpart[:, s * 2 + j, :] = mine_cols[:, s * BS : (s + 1) * BS]


def forward_kernel(order, near, far, w_ref, b_ref, lown, lpiv, zt, frhs, bs, ztall):
    w, q = wide_index(), lax.axis_index("narrow")
    for r in range(NR):
        bs[r] = b_ref[r].astype(F32)
    for i, p, tile in arrivals(near, far):
        for n in range(4):
            r0 = p * SUB + 8 * (n >> 1)
            c0 = 128 * (n & 1)
            bs[NR + i, r0 : r0 + 8, c0 : c0 + 128] = tile[n, SUB : SUB + 8].astype(F32)
    for s in range(NP):
        k = order[s]
        weight = w_ref[k]
        bk = bs[NR + k].astype(BF)
        z = dot(weight, bk, 0, 0).astype(BF)
        ztall[...] = dot(bk, weight, 0, 0).astype(BF).astype(F32)
        for j in range(2):
            zt[s * 2 + j : s * 2 + j + 1] = ztall[pl.ds(j * BS + q * NW + w, 1), :]
        elim = dot(lown[:, s * BS : (s + 1) * BS], z)
        for i in range(NR):
            bs[i] = (bs[i] - elim[i * BS : (i + 1) * BS]).astype(BF).astype(F32)
        for t in range(s + 1, NP):
            i = order[t]
            elim = dot(lpiv[s, pl.ds(pl.multiple_of(i * BS, BS), BS), :], z)
            bs[NR + i] = (bs[NR + i] - elim).astype(BF).astype(F32)
    for r in range(NR):
        frhs[r] = bs[r].astype(BF)


def solve_kernel(order, parts, zt, lpiv, w_ref, h, out, xs):
    total = jnp.sum(parts[...], axis=0)
    for s in reversed(range(NP)):
        k = order[s]
        acc = total[s * 2 : s * 2 + 2]
        for t in range(s + 1, NP):
            i = order[t]
            acc = acc + dot(xs[i].astype(BF), lpiv[s, pl.ds(pl.multiple_of(i * BS, BS), BS), :])
        c = (zt[s * 2 : s * 2 + 2] - acc).astype(BF)
        xs[k] = dot(c, w_ref[k], 1, 1).astype(BF).astype(F32)
    x = jnp.concatenate([xs[i] for i in range(NP)], axis=0).astype(BF)
    for d in range(NW * 4):
        out[d] = x


def combine_kernel(order, lown, lpiv, w_ref, h):
    def low(t, s):
        return lpiv[s, pl.ds(pl.multiple_of(order[t] * BS, BS), BS), :]

    def right(coeff, s):
        return dot(coeff.astype(BF), w_ref[order[s]], 1, 1).astype(BF)

    base = [lown[:, s * BS : (s + 1) * BS].astype(F32) for s in range(NP)]
    r3 = right(base[3], 3)
    h[14] = r3
    r3_low = [dot(r3, low(3, s)) for s in range(3)]
    for m3 in range(2):
        c3 = [base[s] - r3_low[s] if m3 else base[s] for s in range(3)]
        r2 = right(c3[2], 2)
        h[12 + m3] = r2
        r2_low = [dot(r2, low(2, s)) for s in range(2)]
        for m2 in range(2):
            c2 = [c3[s] - r2_low[s] if m2 else c3[s] for s in range(2)]
            r1 = right(c2[1], 1)
            h[8 + m2 + 2 * m3] = r1
            r1_low = dot(r1, low(1, 0))
            for m1 in range(2):
                r0 = right(c2[0] - r1_low if m1 else c2[0], 0)
                h[m1 + 2 * m2 + 4 * m3] = r0


GC = 8


def update_kernel(order, mown, mpiv, a_ref, u_ref, h, delta, out):
    g = pl.program_id(0)
    rows = lax.broadcasted_iota(jnp.int32, (BS, BS), 0)
    cols = lax.broadcasted_iota(jnp.int32, (BS, BS), 1)
    perm = jnp.where((rows % GC) * SUB + rows // GC == cols, 1.0, 0.0).astype(BF)
    cols_out = []
    for col in range(GC):
        c = g * GC + col
        m1, m2, m3 = (mpiv[order[s], c] for s in range(1, NP))
        left = [h[m1 + 2 * m2 + 4 * m3], h[8 + m2 + 2 * m3], h[12 + m3], h[14]]
        p, cc = divmod(col, CPP)
        raw = []
        for s in range(NP):
            zg, core = order[s] >> 1, order[s] & 1
            z = zg if p == 0 else 3 - zg
            raw.append(u_ref[2 * z + core, cc * BS : (cc + 1) * BS])
        lu = dot(jnp.concatenate(left, axis=1), jnp.concatenate(raw, axis=0))
        parts = []
        for r in range(NR):
            parts.append(jnp.where(mown[r, c] != 0, lu[r * BS : (r + 1) * BS], 0.0).astype(BF))
        if col == 0:
            parts = [jnp.where(g == 0, delta[r * BS : (r + 1) * BS], parts[r]) for r in range(NR)]
        cols_out.append(parts)
    for r in range(NR):
        for ag in range(0, BS // SUB, 2):
            sls = [slice((ag + e) * SUB, (ag + e + 1) * SUB) for e in range(2)]
            stack = jnp.concatenate(
                [jnp.concatenate([cols_out[col][r][sl] for col in range(GC)], axis=0) for sl in sls], axis=1
            )
            change = dot(perm, stack)
            for e, sl in enumerate(sls):
                part = change[:, e * BS : (e + 1) * BS].reshape(SUB, GC, BS)
                out[r, sl] = (a_ref[r, sl].astype(F32) - part).astype(BF)


def vmem(n):
    return [pl.BlockSpec(memory_space=pltpu.VMEM)] * n


def smem(n):
    return [pl.BlockSpec(memory_space=pltpu.SMEM)] * n


def body(front, pivot_inverse, rhs, trail_sol, block_mask, panel_order):
    blocks = front.reshape(NR, BS, NC, BS)
    mask = block_mask.reshape(NR, NC)
    b = rhs.reshape(NR, BS, NRHS)
    y = trail_sol.reshape(NR, BS, NRHS)

    fixed = lambda shape: pl.BlockSpec(shape, lambda g: (0,) * len(shape))
    shapes = [(CPP * BS + EXTRA, BS)] * PIECES + [(NR * BS + 8, BS)]
    *sent, mine = pl.pallas_call(
        prep_kernel,
        out_shape=tuple(jax.ShapeDtypeStruct(shape, BF) for shape in shapes),
        grid=(1,),
        in_specs=[fixed((1, BS, NC, BS)), fixed((NR, BS, 8, BS)), fixed((1, BS, NRHS)), fixed((NR, NC))],
        out_specs=tuple(fixed(shape) for shape in shapes),
        name="prep",
    )(blocks, blocks, b, mask)

    pieces = []
    for p in SCATTER_ORDER:
        pairs = [(i, holder(p, i)) for i in range(NP)]
        pieces.append(lax.ppermute(sent[p], WIDE, pairs + [(b, a) for a, b in pairs]))

    others = [lax.ppermute(mine, "narrow", [(i, (i + d) % 4) for i in range(4)]) for d in (1, 2, 3)]

    piece, copies = pl.pallas_call(
        merge_kernel,
        out_shape=(
            jax.ShapeDtypeStruct((CPP * BS, BS), BF),
            jax.ShapeDtypeStruct((NW * 2, EXTRA, BS), BF),
        ),
        in_specs=vmem(PIECES),
        out_specs=tuple(vmem(2)),
        name="merge",
    )(sent[0], *pieces)

    ugath = lax.all_gather(piece, WIDE)

    near = lax.all_to_all(copies, ("chip", "narrow"), 0, 0).reshape(NW // 2, 4, EXTRA, BS)
    far = lax.ppermute(near, "core", [(0, 1), (1, 0)])

    lown, lpiv, tpart, delta, mpiv = pl.pallas_call(
        panel_kernel,
        out_shape=(
            jax.ShapeDtypeStruct((NR * BS, NP * BS), BF),
            jax.ShapeDtypeStruct((NP, NP * BS, BS), BF),
            jax.ShapeDtypeStruct((NW, 8, BS), F32),
            jax.ShapeDtypeStruct((NR * BS, BS), BF),
            jax.ShapeDtypeStruct((NP, BS), jnp.int32),
        ),
        in_specs=smem(1) + vmem(8),
        out_specs=tuple(vmem(5)),
        scratch_shapes=[
            pltpu.VMEM((NP, (NR + NP) * BS, BS), BF),
            pltpu.VMEM((NRHS, NP * BS), F32),
            pltpu.VMEM((NP, 8, BS), F32),
            pltpu.VMEM((NP, NP, 8, BS), F32),
        ],
        name="panel",
    )(panel_order, mine, *others, near, far, pivot_inverse, y)

    zt, frhs = pl.pallas_call(
        forward_kernel,
        out_shape=(
            jax.ShapeDtypeStruct((8, BS), F32),
            jax.ShapeDtypeStruct((NR, BS, NRHS), BF),
        ),
        in_specs=smem(1) + vmem(6),
        out_specs=tuple(vmem(2)),
        scratch_shapes=[
            pltpu.VMEM((NR + NP, BS, NRHS), F32),
            pltpu.VMEM((NRHS, BS), F32),
        ],
        name="forward",
    )(panel_order, near, far, pivot_inverse, b, lown, lpiv)

    h = pl.pallas_call(
        combine_kernel,
        out_shape=jax.ShapeDtypeStruct((15, NR * BS, BS), BF),
        in_specs=smem(1) + vmem(3),
        out_specs=vmem(1)[0],
        name="combine",
    )(panel_order, lown, lpiv, pivot_inverse)

    tparts = lax.all_to_all(tpart, WIDE, 0, 0)
    xg = pl.pallas_call(
        solve_kernel,
        out_shape=jax.ShapeDtypeStruct((NW * 4, 8, BS), BF),
        in_specs=smem(1) + vmem(4) + [pl.BlockSpec(memory_space=pl.ANY)],
        out_specs=vmem(1)[0],
        scratch_shapes=[pltpu.VMEM((NP, 2, BS), F32)],
        name="solve",
    )(panel_order, tparts, zt, lpiv, pivot_inverse, h)
    xall = lax.all_to_all(xg, ("narrow", *WIDE), 0, 0)

    front_out = pl.pallas_call(
        update_kernel,
        out_shape=jax.ShapeDtypeStruct((NR, BS, NC, BS), BF),
        grid=(NC // GC,),
        in_specs=smem(3)
        + [
            pl.BlockSpec((NR, BS, GC, BS), lambda g: (0, 0, g, 0)),
            pl.BlockSpec((8, CPP * BS, BS), lambda g: (g, 0, 0)),
            fixed((15, NR * BS, BS)),
            fixed((NR * BS, BS)),
        ],
        out_specs=pl.BlockSpec((NR, BS, GC, BS), lambda g: (0, 0, g, 0)),
        name="update",
    )(panel_order, mask, mpiv, blocks, ugath.reshape(NW, CPP * BS, BS), h, delta)
    front_out, xall = lax.optimization_barrier((front_out, xall))
    window = xall.reshape(NW * 4, NP, 2, BS).transpose(1, 3, 2, 0).reshape(NP, BS, NRHS)
    return front_out.reshape(front.shape), frhs.reshape(rhs.shape), window


def solution(mesh):
    in_specs = (
        P(None, WIDE, None, None, "narrow", None),
        P(),
        P(None, WIDE, None, None),
        P(None, WIDE, None, None),
        P(None, WIDE, None, "narrow"),
        P(),
    )
    out_specs = (P(None, WIDE, None, None, "narrow", None), P(None, WIDE, None, None), P())
    axes = {"chip": NW // 2, "core": 2, "narrow": 4}
    mesh = Mesh(mesh.devices.reshape(tuple(axes.values())), tuple(axes))

    def step(*args):
        return body(*args)

    step = jax.shard_map(step, mesh=mesh, in_specs=in_specs, out_specs=out_specs, check_vma=False)
    return step
```

```python
import jax
import jax.numpy as jnp
from jax import lax
from jax.experimental import pallas as pl
from jax.experimental.pallas import tpu as pltpu
from jax.sharding import Mesh
from jax.sharding import PartitionSpec as P


BF = jnp.bfloat16
F32 = jnp.float32
BS = 128
NP = 4
NR = 4
NC = 32
NRHS = 256
NW = 32
WIDE = ("chip", "core")
PIECES = 8
CPP = NC // PIECES
SCATTER_ORDER = (2, 4, 3, 5, 6, 7, 1)
SUB = 16
EXTRA = SUB + 8 + 8


def holder(p, i):
    z = i >> 1 if p % 2 == 0 else 3 - (i >> 1)
    return (p >> 1) * 8 + z * 2 + (i & 1)


def dot(a, b, ca=1, cb=0):
    return lax.dot_general(a, b, (((ca,), (cb,)), ((), ())), preferred_element_type=F32)


def ranks_of(order, w):
    rank = [sum(jnp.where(order[s] == i, s, 0) for s in range(NP)) for i in range(NP)]
    own = jnp.int32(NP)
    for i in range(NP):
        own = jnp.where(w == i, rank[i], own)
    return rank, own


def one_hot(rows, fn):
    r = lax.broadcasted_iota(jnp.int32, (rows, BS), 0)
    c = lax.broadcasted_iota(jnp.int32, (rows, BS), 1)
    return jnp.where(fn(r) == c, 1.0, 0.0).astype(BF)


def prep_kernel(row_ref, col_ref, b_ref, mask_ref, *outs):
    q = lax.axis_index("narrow")
    sent, mine = outs[:PIECES], outs[PIECES]
    g = pl.program_id(0)
    gather = one_hot(BS, lambda r: (r % SUB) * 8 + r // SUB)
    for ct in range(NC // 8):

        @pl.when(g == ct)
        def _():
            for ag in range(BS // SUB):
                native = row_ref[0, ag * SUB : (ag + 1) * SUB].astype(F32).reshape(BS, BS).astype(BF)
                blocks = dot(gather, native).astype(BF)
                for e in range(8):
                    p, cc = divmod(ct * 8 + e, CPP)
                    sent[p][cc * BS + ag * SUB : cc * BS + (ag + 1) * SUB] = blocks[e * SUB : (e + 1) * SUB]
                if ct == 0:
                    sent[ag][CPP * BS : CPP * BS + SUB] = blocks[:SUB]

    @pl.when(g == 0)
    def _():
        mask = mask_ref[...].astype(F32)
        widen = one_hot(NC, lambda r: r)
        line = jnp.broadcast_to(dot(mask.astype(BF), widen)[0:1], (8, BS)).astype(BF)
        for p in range(PIECES):
            rows = b_ref[0, p * SUB : (p + 1) * SUB, :].astype(F32)
            rows = jnp.where((q & 2) != 0, rows[8:], rows[:8])
            rows = jnp.where((q & 1) != 0, rows[:, BS:], rows[:, :BS])
            sent[p][CPP * BS + SUB : CPP * BS + SUB + 8] = rows.astype(BF)
            sent[p][CPP * BS + SUB + 8 :] = line
        first = jnp.broadcast_to(mask[:, 0:1], (NR, BS))
        mine[NR * BS :] = jnp.concatenate([first, jnp.zeros((8 - NR, BS), F32)], axis=0).astype(BF)

    pick = one_hot(SUB, lambda r: r * 8)
    for ag in range(BS // SUB):
        native = col_ref[0, ag * SUB : (ag + 1) * SUB].astype(F32).reshape(BS, BS).astype(BF)
        mine[pl.ds(pl.multiple_of(g * BS + ag * SUB, SUB), SUB), :] = dot(pick, native).astype(BF)


def merge_kernel(*refs):
    parts, (piece, copies, buf) = refs[:PIECES], refs[PIECES:]
    chip = lax.axis_index("chip")
    place = (chip >> 2) * 2 + ((chip & 3) >> 1)
    for p, part in zip((0, *SCATTER_ORDER), parts):

        @pl.when(place == p)
        def _():
            pltpu.sync_copy(part, buf)

    piece[...] = buf[: CPP * BS]
    for d in range(NW * 2):
        copies[d] = buf[CPP * BS :]


def wide_index():
    return lax.axis_index("chip") * 2 + lax.axis_index("core")


def arrivals(near, far):
    core = lax.axis_index("core")
    for ref, c in ((near, core), (far, 1 - core)):
        for zg in range(2):
            for p in range(PIECES):
                z = zg if p % 2 == 0 else 3 - zg
                yield 2 * zg + c, p, ref.at[(p >> 1) * 4 + z]


def panel_kernel(order, own, d1, d2, d3, near, far, w_ref, y_ref,
                 lown, lpiv, tpart, delta, mpiv, pan, tall, mk, mkp):
    w, q = wide_index(), lax.axis_index("narrow")
    rank, own_rank = ranks_of(order, w)
    for d, ref in enumerate((own, d1, d2, d3)):
        k = lax.rem(q - d + 4, 4)
        pan[k, 0 : NR * BS] = ref[0 : NR * BS]
        mk[k] = ref[NR * BS : NR * BS + 8].astype(F32)
    for i, p, tile in arrivals(near, far):
        row = pl.multiple_of(NR * BS + i * BS + p * SUB, SUB)
        for k in range(NP):
            pan[k, pl.ds(row, SUB), :] = tile[k, 0:SUB]
            if p == 0:
                mkp[i, k] = tile[k, SUB + 8 : SUB + 16].astype(F32)
    for i in range(NP):
        mpiv[i : i + 1] = mkp[i, q, 0:1].astype(jnp.int32)
    y0 = jnp.where(w < NP, jnp.zeros_like(y_ref[0]), y_ref[0])
    y = jnp.concatenate([y0] + [y_ref[r] for r in range(1, NR)], axis=0)
    row_rank = [own_rank, None, None, None] + rank
    for s in range(NP):
        k = order[s]
        weight = w_ref[k]
        left = dot(pan[k], weight)
        parts = []
        for i in range(NR + NP):
            part = left[i * BS : (i + 1) * BS]
            if row_rank[i] is not None:
                part = jnp.where(row_rank[i] > s, part, 0.0)
            parts.append(part.astype(BF))
        lb = jnp.concatenate(parts, axis=0)
        lown[:, s * BS : (s + 1) * BS] = lb[: NR * BS]
        lpiv[s] = lb[NR * BS :]
        tall[:, s * BS : (s + 1) * BS] = dot(y, lb[: NR * BS], 0, 0)
        for t in range(s + 1, NP):
            j = order[t]
            akj = pan[j, pl.ds(pl.multiple_of(NR * BS + k * BS, BS), BS), :]
            prod = dot(lb, dot(weight, akj, 0, 0).astype(BF))
            for i in range(NR + NP):
                sl = slice(i * BS, (i + 1) * BS)
                m = mk[j, i : i + 1, :] if i < NR else mkp[i - NR, j, 0:1, 0:1]
                pan[j, sl] = (pan[j, sl].astype(F32) - m * prod[sl]).astype(BF)
    delta[...] = (own[0 : NR * BS].astype(F32) - pan[q, 0 : NR * BS].astype(F32)).astype(BF)
    for j in range(2):
        mine_cols = tall[pl.ds(pl.multiple_of(j * BS + q * NW, NW), NW), :]
        for s in range(NP):
            tpart[:, s * 2 + j, :] = mine_cols[:, s * BS : (s + 1) * BS]


def forward_kernel(order, near, far, w_ref, b_ref, lown, lpiv, zt, frhs, bs, ztall):
    w, q = wide_index(), lax.axis_index("narrow")
    for r in range(NR):
        bs[r] = b_ref[r].astype(F32)
    for i, p, tile in arrivals(near, far):
        for n in range(4):
            r0 = p * SUB + 8 * (n >> 1)
            c0 = 128 * (n & 1)
            bs[NR + i, r0 : r0 + 8, c0 : c0 + 128] = tile[n, SUB : SUB + 8].astype(F32)
    for s in range(NP):
        k = order[s]
        weight = w_ref[k]
        bk = bs[NR + k].astype(BF)
        z = dot(weight, bk, 0, 0).astype(BF)
        ztall[...] = dot(bk, weight, 0, 0).astype(BF).astype(F32)
        for j in range(2):
            zt[s * 2 + j : s * 2 + j + 1] = ztall[pl.ds(j * BS + q * NW + w, 1), :]
        elim = dot(lown[:, s * BS : (s + 1) * BS], z)
        for i in range(NR):
            bs[i] = (bs[i] - elim[i * BS : (i + 1) * BS]).astype(BF).astype(F32)
        for t in range(s + 1, NP):
            i = order[t]
            elim = dot(lpiv[s, pl.ds(pl.multiple_of(i * BS, BS), BS), :], z)
            bs[NR + i] = (bs[NR + i] - elim).astype(BF).astype(F32)
    for r in range(NR):
        frhs[r] = bs[r].astype(BF)


def solve_kernel(order, parts, zt, lpiv, w_ref, h, out, xs):
    total = jnp.sum(parts[...], axis=0)
    for s in reversed(range(NP)):
        k = order[s]
        acc = total[s * 2 : s * 2 + 2]
        for t in range(s + 1, NP):
            i = order[t]
            acc = acc + dot(xs[i].astype(BF), lpiv[s, pl.ds(pl.multiple_of(i * BS, BS), BS), :])
        c = (zt[s * 2 : s * 2 + 2] - acc).astype(BF)
        xs[k] = dot(c, w_ref[k], 1, 1).astype(BF).astype(F32)
    x = jnp.concatenate([xs[i] for i in range(NP)], axis=0).astype(BF)
    for d in range(NW * 4):
        out[d] = x


def combine_kernel(order, lown, lpiv, w_ref, h):
    def low(t, s):
        return lpiv[s, pl.ds(pl.multiple_of(order[t] * BS, BS), BS), :]

    def right(coeff, s):
        return dot(coeff.astype(BF), w_ref[order[s]], 1, 1).astype(BF)

    base = [lown[:, s * BS : (s + 1) * BS].astype(F32) for s in range(NP)]
    r3 = right(base[3], 3)
    h[14] = r3
    r3_low = [dot(r3, low(3, s)) for s in range(3)]
    for m3 in range(2):
        c3 = [base[s] - r3_low[s] if m3 else base[s] for s in range(3)]
        r2 = right(c3[2], 2)
        h[12 + m3] = r2
        r2_low = [dot(r2, low(2, s)) for s in range(2)]
        for m2 in range(2):
            c2 = [c3[s] - r2_low[s] if m2 else c3[s] for s in range(2)]
            r1 = right(c2[1], 1)
            h[8 + m2 + 2 * m3] = r1
            r1_low = dot(r1, low(1, 0))
            for m1 in range(2):
                r0 = right(c2[0] - r1_low if m1 else c2[0], 0)
                h[m1 + 2 * m2 + 4 * m3] = r0


GC = 8


def update_kernel(order, mown, mpiv, a_ref, u_ref, h, delta, out):
    g = pl.program_id(0)
    rows = lax.broadcasted_iota(jnp.int32, (BS, BS), 0)
    cols = lax.broadcasted_iota(jnp.int32, (BS, BS), 1)
    perm = jnp.where((rows % GC) * SUB + rows // GC == cols, 1.0, 0.0).astype(BF)
    cols_out = []
    for col in range(GC):
        c = g * GC + col
        m1, m2, m3 = (mpiv[order[s], c] for s in range(1, NP))
        left = [h[m1 + 2 * m2 + 4 * m3], h[8 + m2 + 2 * m3], h[12 + m3], h[14]]
        p, cc = divmod(col, CPP)
        raw = []
        for s in range(NP):
            zg, core = order[s] >> 1, order[s] & 1
            z = zg if p == 0 else 3 - zg
            raw.append(u_ref[2 * z + core, cc * BS : (cc + 1) * BS])
        lu = dot(jnp.concatenate(left, axis=1), jnp.concatenate(raw, axis=0))
        parts = []
        for r in range(NR):
            parts.append(jnp.where(mown[r, c] != 0, lu[r * BS : (r + 1) * BS], 0.0).astype(BF))
        if col == 0:
            parts = [jnp.where(g == 0, delta[r * BS : (r + 1) * BS], parts[r]) for r in range(NR)]
        cols_out.append(parts)
    for r in range(NR):
        for ag in range(0, BS // SUB, 2):
            sls = [slice((ag + e) * SUB, (ag + e + 1) * SUB) for e in range(2)]
            stack = jnp.concatenate(
                [jnp.concatenate([cols_out[col][r][sl] for col in range(GC)], axis=0) for sl in sls], axis=1
            )
            change = dot(perm, stack)
            for e, sl in enumerate(sls):
                part = change[:, e * BS : (e + 1) * BS].reshape(SUB, GC, BS)
                out[r, sl] = (a_ref[r, sl].astype(F32) - part).astype(BF)


def vmem(n):
    return [pl.BlockSpec(memory_space=pltpu.VMEM)] * n


def smem(n):
    return [pl.BlockSpec(memory_space=pltpu.SMEM)] * n


def body(front, pivot_inverse, rhs, trail_sol, block_mask, panel_order):
    blocks = front.reshape(NR, BS, NC, BS)
    mask = block_mask.reshape(NR, NC)
    b = rhs.reshape(NR, BS, NRHS)
    y = trail_sol.reshape(NR, BS, NRHS)

    fixed = lambda shape: pl.BlockSpec(shape, lambda g: (0,) * len(shape))
    shapes = [(CPP * BS + EXTRA, BS)] * PIECES + [(NR * BS + 8, BS)]
    *sent, mine = pl.pallas_call(
        prep_kernel,
        out_shape=tuple(jax.ShapeDtypeStruct(shape, BF) for shape in shapes),
        grid=(NC // 8,),
        in_specs=[
            pl.BlockSpec((1, BS, 8, BS), lambda g: (0, 0, g, 0)),
            pl.BlockSpec((1, BS, 8, BS), lambda g: (g, 0, 0, 0)),
            fixed((1, BS, NRHS)),
            fixed((NR, NC)),
        ],
        out_specs=tuple(fixed(shape) for shape in shapes),
        name="prep",
    )(blocks, blocks, b, mask)

    pieces = []
    for p in SCATTER_ORDER:
        pieces.append(lax.ppermute(sent[p], WIDE, [(i, holder(p, i)) for i in range(NP)]))

    others = [lax.ppermute(mine, "narrow", [(i, (i + d) % 4) for i in range(4)]) for d in (1, 2, 3)]

    piece, copies = pl.pallas_call(
        merge_kernel,
        out_shape=(
            jax.ShapeDtypeStruct((CPP * BS, BS), BF),
            jax.ShapeDtypeStruct((NW * 2, EXTRA, BS), BF),
        ),
        in_specs=[pl.BlockSpec(memory_space=pl.ANY)] * PIECES,
        out_specs=tuple(vmem(2)),
        scratch_shapes=[pltpu.VMEM((CPP * BS + EXTRA, BS), BF)],
        name="merge",
    )(sent[0], *pieces)

    ugath = lax.all_gather(piece, WIDE)

    near = lax.all_to_all(copies, ("chip", "narrow"), 0, 0).reshape(NW // 2, 4, EXTRA, BS)
    far = lax.ppermute(near, "core", [(0, 1), (1, 0)])

    lown, lpiv, tpart, delta, mpiv = pl.pallas_call(
        panel_kernel,
        out_shape=(
            jax.ShapeDtypeStruct((NR * BS, NP * BS), BF),
            jax.ShapeDtypeStruct((NP, NP * BS, BS), BF),
            jax.ShapeDtypeStruct((NW, 8, BS), F32),
            jax.ShapeDtypeStruct((NR * BS, BS), BF),
            jax.ShapeDtypeStruct((NP, BS), jnp.int32),
        ),
        in_specs=smem(1) + vmem(8),
        out_specs=tuple(vmem(5)),
        scratch_shapes=[
            pltpu.VMEM((NP, (NR + NP) * BS, BS), BF),
            pltpu.VMEM((NRHS, NP * BS), F32),
            pltpu.VMEM((NP, 8, BS), F32),
            pltpu.VMEM((NP, NP, 8, BS), F32),
        ],
        name="panel",
    )(panel_order, mine, *others, near, far, pivot_inverse, y)

    zt, frhs = pl.pallas_call(
        forward_kernel,
        out_shape=(
            jax.ShapeDtypeStruct((8, BS), F32),
            jax.ShapeDtypeStruct((NR, BS, NRHS), BF),
        ),
        in_specs=smem(1) + vmem(6),
        out_specs=tuple(vmem(2)),
        scratch_shapes=[
            pltpu.VMEM((NR + NP, BS, NRHS), F32),
            pltpu.VMEM((NRHS, BS), F32),
        ],
        name="forward",
    )(panel_order, near, far, pivot_inverse, b, lown, lpiv)

    h = pl.pallas_call(
        combine_kernel,
        out_shape=jax.ShapeDtypeStruct((15, NR * BS, BS), BF),
        in_specs=smem(1) + vmem(3),
        out_specs=vmem(1)[0],
        name="combine",
    )(panel_order, lown, lpiv, pivot_inverse)

    tparts = lax.all_to_all(tpart, WIDE, 0, 0)
    xg = pl.pallas_call(
        solve_kernel,
        out_shape=jax.ShapeDtypeStruct((NW * 4, 8, BS), BF),
        in_specs=smem(1) + vmem(4) + [pl.BlockSpec(memory_space=pl.ANY)],
        out_specs=vmem(1)[0],
        scratch_shapes=[pltpu.VMEM((NP, 2, BS), F32)],
        name="solve",
    )(panel_order, tparts, zt, lpiv, pivot_inverse, h)
    xall = lax.all_to_all(xg, ("narrow", *WIDE), 0, 0)

    front_out = pl.pallas_call(
        update_kernel,
        out_shape=jax.ShapeDtypeStruct((NR, BS, NC, BS), BF),
        grid=(NC // GC,),
        in_specs=smem(3)
        + [
            pl.BlockSpec((NR, BS, GC, BS), lambda g: (0, 0, g, 0)),
            pl.BlockSpec((8, CPP * BS, BS), lambda g: (g, 0, 0)),
            fixed((15, NR * BS, BS)),
            fixed((NR * BS, BS)),
        ],
        out_specs=pl.BlockSpec((NR, BS, GC, BS), lambda g: (0, 0, g, 0)),
        name="update",
    )(panel_order, mask, mpiv, blocks, ugath.reshape(NW, CPP * BS, BS), h, delta)
    front_out, xall = lax.optimization_barrier((front_out, xall))
    window = xall.reshape(NW * 4, NP, 2, BS).transpose(1, 3, 2, 0).reshape(NP, BS, NRHS)
    return front_out.reshape(front.shape), frhs.reshape(rhs.shape), window


def solution(mesh):
    in_specs = (
        P(None, WIDE, None, None, "narrow", None),
        P(),
        P(None, WIDE, None, None),
        P(None, WIDE, None, None),
        P(None, WIDE, None, "narrow"),
        P(),
    )
    out_specs = (P(None, WIDE, None, None, "narrow", None), P(None, WIDE, None, None), P())
    axes = {"chip": NW // 2, "core": 2, "narrow": 4}
    mesh = Mesh(mesh.devices.reshape(tuple(axes.values())), tuple(axes))

    def step(*args):
        return body(*args)

    step = jax.shard_map(step, mesh=mesh, in_specs=in_specs, out_specs=out_specs, check_vma=False)
    return step
```

```python
import jax
import jax.numpy as jnp
from jax import lax
from jax.experimental import pallas as pl
from jax.experimental.pallas import tpu as pltpu
from jax.sharding import Mesh
from jax.sharding import PartitionSpec as P


BF = jnp.bfloat16
F32 = jnp.float32
BS = 128
NP = 4
NR = 4
NC = 32
NRHS = 256
NW = 32
WIDE = ("chip", "core")
PIECES = 8
CPP = NC // PIECES
SCATTER_ORDER = (2, 6, 4, 1, 3, 7, 5)
SUB = 16
EXTRA = SUB + 8 + 8


def holder(p, i):
    z = i >> 1 if p % 2 == 0 else 3 - (i >> 1)
    return (p >> 1) * 8 + z * 2 + (i & 1)


def dot(a, b, ca=1, cb=0):
    return lax.dot_general(a, b, (((ca,), (cb,)), ((), ())), preferred_element_type=F32)


def ranks_of(order, w):
    rank = [sum(jnp.where(order[s] == i, s, 0) for s in range(NP)) for i in range(NP)]
    own = jnp.int32(NP)
    for i in range(NP):
        own = jnp.where(w == i, rank[i], own)
    return rank, own


def one_hot(rows, fn):
    r = lax.broadcasted_iota(jnp.int32, (rows, BS), 0)
    c = lax.broadcasted_iota(jnp.int32, (rows, BS), 1)
    return jnp.where(fn(r) == c, 1.0, 0.0).astype(BF)


def prep_kernel(row_ref, col_ref, b_ref, mask_ref, *outs):
    q = lax.axis_index("narrow")
    sent, mine = outs[:PIECES], outs[PIECES]
    gather = one_hot(BS, lambda r: (r % SUB) * 8 + r // SUB)
    for ct in range(NC // 8):
        for ag in range(BS // SUB):
            native = row_ref[0, ag * SUB : (ag + 1) * SUB, ct * 8 : (ct + 1) * 8, :]
            native = native.astype(F32).reshape(BS, BS).astype(BF)
            blocks = dot(gather, native).astype(BF)
            for e in range(8):
                p, cc = divmod(ct * 8 + e, CPP)
                sent[p][cc * BS + ag * SUB : cc * BS + (ag + 1) * SUB] = blocks[e * SUB : (e + 1) * SUB]
            if ct == 0:
                sent[ag][CPP * BS : CPP * BS + SUB] = blocks[:SUB]
    mask = mask_ref[...].astype(F32)
    widen = one_hot(NC, lambda r: r)
    line = jnp.broadcast_to(dot(mask.astype(BF), widen)[0:1], (8, BS)).astype(BF)
    for p in range(PIECES):
        rows = b_ref[0, p * SUB : (p + 1) * SUB, :].astype(F32)
        rows = jnp.where((q & 2) != 0, rows[8:], rows[:8])
        rows = jnp.where((q & 1) != 0, rows[:, BS:], rows[:, :BS])
        sent[p][CPP * BS + SUB : CPP * BS + SUB + 8] = rows.astype(BF)
        sent[p][CPP * BS + SUB + 8 :] = line
    pick = one_hot(SUB, lambda r: r * 8)
    for r in range(NR):
        for ag in range(BS // SUB):
            native = col_ref[r, ag * SUB : (ag + 1) * SUB].astype(F32).reshape(BS, BS).astype(BF)
            mine[r * BS + ag * SUB : r * BS + (ag + 1) * SUB] = dot(pick, native).astype(BF)
    first = jnp.broadcast_to(mask[:, 0:1], (NR, BS))
    mine[NR * BS :] = jnp.concatenate([first, jnp.zeros((8 - NR, BS), F32)], axis=0).astype(BF)


def merge_kernel(*refs):
    parts, (piece, copies, buf) = refs[:PIECES], refs[PIECES:]
    chip = lax.axis_index("chip")
    place = (chip >> 2) * 2 + ((chip & 3) >> 1)
    for p, part in zip((0, *SCATTER_ORDER), parts):

        @pl.when(place == p)
        def _():
            pltpu.sync_copy(part, buf)

    piece[...] = buf[: CPP * BS]
    for d in range(NW * 2):
        copies[d] = buf[CPP * BS :]


def wide_index():
    return lax.axis_index("chip") * 2 + lax.axis_index("core")


def arrivals(near, far):
    core = lax.axis_index("core")
    for ref, c in ((near, core), (far, 1 - core)):
        for zg in range(2):
            for p in range(PIECES):
                z = zg if p % 2 == 0 else 3 - zg
                yield 2 * zg + c, p, ref.at[(p >> 1) * 4 + z]


def panel_kernel(order, own, d1, d2, d3, near, far, w_ref, y_ref,
                 lown, lpiv, tpart, delta, mpiv, pan, tall, mk, mkp):
    w, q = wide_index(), lax.axis_index("narrow")
    rank, own_rank = ranks_of(order, w)
    for d, ref in enumerate((own, d1, d2, d3)):
        k = lax.rem(q - d + 4, 4)
        pan[k, 0 : NR * BS] = ref[0 : NR * BS]
        mk[k] = ref[NR * BS : NR * BS + 8].astype(F32)
    for i, p, tile in arrivals(near, far):
        row = pl.multiple_of(NR * BS + i * BS + p * SUB, SUB)
        for k in range(NP):
            pan[k, pl.ds(row, SUB), :] = tile[k, 0:SUB]
            if p == 0:
                mkp[i, k] = tile[k, SUB + 8 : SUB + 16].astype(F32)
    for i in range(NP):
        mpiv[i : i + 1] = mkp[i, q, 0:1].astype(jnp.int32)
    row_rank = [own_rank, None, None, None] + rank
    for s in range(NP):
        k = order[s]
        weight = w_ref[k]
        left = dot(pan[k], weight)
        parts = []
        for i in range(NR + NP):
            part = left[i * BS : (i + 1) * BS]
            if row_rank[i] is not None:
                part = jnp.where(row_rank[i] > s, part, 0.0)
            parts.append(part.astype(BF))
        lb = jnp.concatenate(parts, axis=0)
        lown[:, s * BS : (s + 1) * BS] = lb[: NR * BS]
        lpiv[s] = lb[NR * BS :]
        for t in range(s + 1, NP):
            j = order[t]
            akj = pan[j, pl.ds(pl.multiple_of(NR * BS + k * BS, BS), BS), :]
            prod = dot(lb, dot(weight, akj, 0, 0).astype(BF))
            for i in range(NR + NP):
                sl = slice(i * BS, (i + 1) * BS)
                m = mk[j, i : i + 1, :] if i < NR else mkp[i - NR, j, 0:1, 0:1]
                pan[j, sl] = (pan[j, sl].astype(F32) - m * prod[sl]).astype(BF)
    delta[...] = (own[0 : NR * BS].astype(F32) - pan[q, 0 : NR * BS].astype(F32)).astype(BF)
    y0 = jnp.where(w < NP, jnp.zeros_like(y_ref[0]), y_ref[0])
    y = jnp.concatenate([y0] + [y_ref[r] for r in range(1, NR)], axis=0)
    tall[...] = dot(y, lown[...], 0, 0)
    for j in range(2):
        mine_cols = tall[pl.ds(pl.multiple_of(j * BS + q * NW, NW), NW), :]
        for s in range(NP):
            tpart[:, s * 2 + j, :] = mine_cols[:, s * BS : (s + 1) * BS]


def forward_kernel(order, near, far, w_ref, b_ref, lown, lpiv, zt, frhs, bs, ztall):
    w, q = wide_index(), lax.axis_index("narrow")
    for r in range(NR):
        bs[r] = b_ref[r].astype(F32)
    for i, p, tile in arrivals(near, far):
        for n in range(4):
            r0 = p * SUB + 8 * (n >> 1)
            c0 = 128 * (n & 1)
            bs[NR + i, r0 : r0 + 8, c0 : c0 + 128] = tile[n, SUB : SUB + 8].astype(F32)
    for s in range(NP):
        k = order[s]
        weight = w_ref[k]
        bk = bs[NR + k].astype(BF)
        z = dot(weight, bk, 0, 0).astype(BF)
        ztall[...] = dot(bk, weight, 0, 0).astype(BF).astype(F32)
        for j in range(2):
            zt[s * 2 + j : s * 2 + j + 1] = ztall[pl.ds(j * BS + q * NW + w, 1), :]
        elim = dot(lown[:, s * BS : (s + 1) * BS], z)
        for i in range(NR):
            bs[i] = (bs[i] - elim[i * BS : (i + 1) * BS]).astype(BF).astype(F32)
        for t in range(s + 1, NP):
            i = order[t]
            elim = dot(lpiv[s, pl.ds(pl.multiple_of(i * BS, BS), BS), :], z)
            bs[NR + i] = (bs[NR + i] - elim).astype(BF).astype(F32)
    for r in range(NR):
        frhs[r] = bs[r].astype(BF)


def solve_kernel(order, parts, zt, lpiv, w_ref, h, out, xs):
    total = jnp.sum(parts[...], axis=0)
    for s in reversed(range(NP)):
        k = order[s]
        acc = total[s * 2 : s * 2 + 2]
        for t in range(s + 1, NP):
            i = order[t]
            acc = acc + dot(xs[i].astype(BF), lpiv[s, pl.ds(pl.multiple_of(i * BS, BS), BS), :])
        c = (zt[s * 2 : s * 2 + 2] - acc).astype(BF)
        xs[k] = dot(c, w_ref[k], 1, 1).astype(BF).astype(F32)
    x = jnp.concatenate([xs[i] for i in range(NP)], axis=0).astype(BF)
    for d in range(NW * 4):
        out[d] = x


def combine_kernel(order, lown, lpiv, w_ref, h):
    def low(t, s):
        return lpiv[s, pl.ds(pl.multiple_of(order[t] * BS, BS), BS), :]

    def right(coeff, s):
        return dot(coeff.astype(BF), w_ref[order[s]], 1, 1).astype(BF)

    base = [lown[:, s * BS : (s + 1) * BS].astype(F32) for s in range(NP)]
    r3 = right(base[3], 3)
    h[14] = r3
    r3_low = [dot(r3, low(3, s)) for s in range(3)]
    for m3 in range(2):
        c3 = [base[s] - r3_low[s] if m3 else base[s] for s in range(3)]
        r2 = right(c3[2], 2)
        h[12 + m3] = r2
        r2_low = [dot(r2, low(2, s)) for s in range(2)]
        for m2 in range(2):
            c2 = [c3[s] - r2_low[s] if m2 else c3[s] for s in range(2)]
            r1 = right(c2[1], 1)
            h[8 + m2 + 2 * m3] = r1
            r1_low = dot(r1, low(1, 0))
            for m1 in range(2):
                r0 = right(c2[0] - r1_low if m1 else c2[0], 0)
                h[m1 + 2 * m2 + 4 * m3] = r0


GC = 8


def update_kernel(order, mown, mpiv, a_ref, u_ref, h, delta, out):
    g = pl.program_id(0)
    rows = lax.broadcasted_iota(jnp.int32, (BS, BS), 0)
    cols = lax.broadcasted_iota(jnp.int32, (BS, BS), 1)
    perm = jnp.where((rows % GC) * SUB + rows // GC == cols, 1.0, 0.0).astype(BF)
    cols_out = []
    for col in range(GC):
        c = g * GC + col
        m1, m2, m3 = (mpiv[order[s], c] for s in range(1, NP))
        left = [h[m1 + 2 * m2 + 4 * m3], h[8 + m2 + 2 * m3], h[12 + m3], h[14]]
        p, cc = divmod(col, CPP)
        raw = []
        for s in range(NP):
            zg, core = order[s] >> 1, order[s] & 1
            z = zg if p == 0 else 3 - zg
            raw.append(u_ref[2 * z + core, cc * BS : (cc + 1) * BS])
        lu = dot(jnp.concatenate(left, axis=1), jnp.concatenate(raw, axis=0))
        parts = []
        for r in range(NR):
            parts.append(jnp.where(mown[r, c] != 0, lu[r * BS : (r + 1) * BS], 0.0).astype(BF))
        if col == 0:
            parts = [jnp.where(g == 0, delta[r * BS : (r + 1) * BS], parts[r]) for r in range(NR)]
        cols_out.append(parts)
    for r in range(NR):
        for ag in range(0, BS // SUB, 2):
            sls = [slice((ag + e) * SUB, (ag + e + 1) * SUB) for e in range(2)]
            stack = jnp.concatenate(
                [jnp.concatenate([cols_out[col][r][sl] for col in range(GC)], axis=0) for sl in sls], axis=1
            )
            change = dot(perm, stack)
            for e, sl in enumerate(sls):
                part = change[:, e * BS : (e + 1) * BS].reshape(SUB, GC, BS)
                out[r, sl] = (a_ref[r, sl].astype(F32) - part).astype(BF)


def vmem(n):
    return [pl.BlockSpec(memory_space=pltpu.VMEM)] * n


def smem(n):
    return [pl.BlockSpec(memory_space=pltpu.SMEM)] * n


def body(front, pivot_inverse, rhs, trail_sol, block_mask, panel_order):
    blocks = front.reshape(NR, BS, NC, BS)
    mask = block_mask.reshape(NR, NC)
    b = rhs.reshape(NR, BS, NRHS)
    y = trail_sol.reshape(NR, BS, NRHS)

    fixed = lambda shape: pl.BlockSpec(shape, lambda g: (0,) * len(shape))
    shapes = [(CPP * BS + EXTRA, BS)] * PIECES + [(NR * BS + 8, BS)]
    *sent, mine = pl.pallas_call(
        prep_kernel,
        out_shape=tuple(jax.ShapeDtypeStruct(shape, BF) for shape in shapes),
        grid=(1,),
        in_specs=[fixed((1, BS, NC, BS)), fixed((NR, BS, 8, BS)), fixed((1, BS, NRHS)), fixed((NR, NC))],
        out_specs=tuple(fixed(shape) for shape in shapes),
        name="prep",
    )(blocks, blocks, b, mask)

    pieces = []
    for p in SCATTER_ORDER:
        pieces.append(lax.ppermute(sent[p], WIDE, [(i, holder(p, i)) for i in range(NP)]))

    others = [lax.ppermute(mine, "narrow", [(i, (i + d) % 4) for i in range(4)]) for d in (1, 2, 3)]

    piece, copies = pl.pallas_call(
        merge_kernel,
        out_shape=(
            jax.ShapeDtypeStruct((CPP * BS, BS), BF),
            jax.ShapeDtypeStruct((NW * 2, EXTRA, BS), BF),
        ),
        in_specs=[pl.BlockSpec(memory_space=pl.ANY)] * PIECES,
        out_specs=tuple(vmem(2)),
        scratch_shapes=[pltpu.VMEM((CPP * BS + EXTRA, BS), BF)],
        name="merge",
    )(sent[0], *pieces)

    ugath = lax.all_gather(piece, WIDE)

    near = lax.all_to_all(copies, ("chip", "narrow"), 0, 0).reshape(NW // 2, 4, EXTRA, BS)
    far = lax.ppermute(near, "core", [(0, 1), (1, 0)])

    lown, lpiv, tpart, delta, mpiv = pl.pallas_call(
        panel_kernel,
        out_shape=(
            jax.ShapeDtypeStruct((NR * BS, NP * BS), BF),
            jax.ShapeDtypeStruct((NP, NP * BS, BS), BF),
            jax.ShapeDtypeStruct((NW, 8, BS), F32),
            jax.ShapeDtypeStruct((NR * BS, BS), BF),
            jax.ShapeDtypeStruct((NP, BS), jnp.int32),
        ),
        in_specs=smem(1) + vmem(8),
        out_specs=tuple(vmem(5)),
        scratch_shapes=[
            pltpu.VMEM((NP, (NR + NP) * BS, BS), BF),
            pltpu.VMEM((NRHS, NP * BS), F32),
            pltpu.VMEM((NP, 8, BS), F32),
            pltpu.VMEM((NP, NP, 8, BS), F32),
        ],
        name="panel",
    )(panel_order, mine, *others, near, far, pivot_inverse, y)

    zt, frhs = pl.pallas_call(
        forward_kernel,
        out_shape=(
            jax.ShapeDtypeStruct((8, BS), F32),
            jax.ShapeDtypeStruct((NR, BS, NRHS), BF),
        ),
        in_specs=smem(1) + vmem(6),
        out_specs=tuple(vmem(2)),
        scratch_shapes=[
            pltpu.VMEM((NR + NP, BS, NRHS), F32),
            pltpu.VMEM((NRHS, BS), F32),
        ],
        name="forward",
    )(panel_order, near, far, pivot_inverse, b, lown, lpiv)

    h = pl.pallas_call(
        combine_kernel,
        out_shape=jax.ShapeDtypeStruct((15, NR * BS, BS), BF),
        in_specs=smem(1) + vmem(3),
        out_specs=vmem(1)[0],
        name="combine",
    )(panel_order, lown, lpiv, pivot_inverse)

    tparts = lax.all_to_all(tpart, WIDE, 0, 0)
    xg = pl.pallas_call(
        solve_kernel,
        out_shape=jax.ShapeDtypeStruct((NW * 4, 8, BS), BF),
        in_specs=smem(1) + vmem(4) + [pl.BlockSpec(memory_space=pl.ANY)],
        out_specs=vmem(1)[0],
        scratch_shapes=[pltpu.VMEM((NP, 2, BS), F32)],
        name="solve",
    )(panel_order, tparts, zt, lpiv, pivot_inverse, h)
    xall = lax.all_to_all(xg, ("narrow", *WIDE), 0, 0)

    front_out = pl.pallas_call(
        update_kernel,
        out_shape=jax.ShapeDtypeStruct((NR, BS, NC, BS), BF),
        grid=(NC // GC,),
        in_specs=smem(3)
        + [
            pl.BlockSpec((NR, BS, GC, BS), lambda g: (0, 0, g, 0)),
            pl.BlockSpec((8, CPP * BS, BS), lambda g: (g, 0, 0)),
            fixed((15, NR * BS, BS)),
            fixed((NR * BS, BS)),
        ],
        out_specs=pl.BlockSpec((NR, BS, GC, BS), lambda g: (0, 0, g, 0)),
        name="update",
    )(panel_order, mask, mpiv, blocks, ugath.reshape(NW, CPP * BS, BS), h, delta)
    front_out, xall = lax.optimization_barrier((front_out, xall))
    window = xall.reshape(NW * 4, NP, 2, BS).transpose(1, 3, 2, 0).reshape(NP, BS, NRHS)
    return front_out.reshape(front.shape), frhs.reshape(rhs.shape), window


def solution(mesh):
    in_specs = (
        P(None, WIDE, None, None, "narrow", None),
        P(),
        P(None, WIDE, None, None),
        P(None, WIDE, None, None),
        P(None, WIDE, None, "narrow"),
        P(),
    )
    out_specs = (P(None, WIDE, None, None, "narrow", None), P(None, WIDE, None, None), P())
    axes = {"chip": NW // 2, "core": 2, "narrow": 4}
    mesh = Mesh(mesh.devices.reshape(tuple(axes.values())), tuple(axes))

    def step(*args):
        return body(*args)

    step = jax.shard_map(step, mesh=mesh, in_specs=in_specs, out_specs=out_specs, check_vma=False)
    return step
```

```python
import jax
import jax.numpy as jnp
from jax import lax
from jax.experimental import pallas as pl
from jax.experimental.pallas import tpu as pltpu
from jax.sharding import Mesh
from jax.sharding import PartitionSpec as P


BF = jnp.bfloat16
F32 = jnp.float32
BS = 128
NP = 4
NR = 4
NC = 32
NRHS = 256
NW = 32
WIDE = ("chip", "core")
PIECES = 8
CPP = NC // PIECES
SCATTER_ORDER = (2, 6, 4, 1, 3, 7, 5)
SUB = 16
EXTRA = SUB + 8 + 8


def holder(p, i):
    z = i >> 1 if p % 2 == 0 else 3 - (i >> 1)
    return (p >> 1) * 8 + z * 2 + (i & 1)


def dot(a, b, ca=1, cb=0):
    return lax.dot_general(a, b, (((ca,), (cb,)), ((), ())), preferred_element_type=F32)


def ranks_of(order, w):
    rank = [sum(jnp.where(order[s] == i, s, 0) for s in range(NP)) for i in range(NP)]
    own = jnp.int32(NP)
    for i in range(NP):
        own = jnp.where(w == i, rank[i], own)
    return rank, own


def one_hot(rows, fn):
    r = lax.broadcasted_iota(jnp.int32, (rows, BS), 0)
    c = lax.broadcasted_iota(jnp.int32, (rows, BS), 1)
    return jnp.where(fn(r) == c, 1.0, 0.0).astype(BF)


def prep_kernel(row_ref, col_ref, b_ref, mask_ref, *outs):
    q = lax.axis_index("narrow")
    sent, mine = outs[:PIECES], outs[PIECES]
    gather = one_hot(BS, lambda r: (r % SUB) * 8 + r // SUB)
    for ct in range(NC // 8):
        for ag in range(BS // SUB):
            native = row_ref[0, ag * SUB : (ag + 1) * SUB, ct * 8 : (ct + 1) * 8, :]
            native = native.astype(F32).reshape(BS, BS).astype(BF)
            blocks = dot(gather, native).astype(BF)
            for e in range(8):
                p, cc = divmod(ct * 8 + e, CPP)
                sent[p][cc * BS + ag * SUB : cc * BS + (ag + 1) * SUB] = blocks[e * SUB : (e + 1) * SUB]
            if ct == 0:
                sent[ag][CPP * BS : CPP * BS + SUB] = blocks[:SUB]
    mask = mask_ref[...].astype(F32)
    widen = one_hot(NC, lambda r: r)
    line = jnp.broadcast_to(dot(mask.astype(BF), widen)[0:1], (8, BS)).astype(BF)
    for p in range(PIECES):
        rows = b_ref[0, p * SUB : (p + 1) * SUB, :].astype(F32)
        rows = jnp.where((q & 2) != 0, rows[8:], rows[:8])
        rows = jnp.where((q & 1) != 0, rows[:, BS:], rows[:, :BS])
        sent[p][CPP * BS + SUB : CPP * BS + SUB + 8] = rows.astype(BF)
        sent[p][CPP * BS + SUB + 8 :] = line
    pick = one_hot(SUB, lambda r: r * 8)
    for r in range(NR):
        for ag in range(BS // SUB):
            native = col_ref[r, ag * SUB : (ag + 1) * SUB].astype(F32).reshape(BS, BS).astype(BF)
            mine[r * BS + ag * SUB : r * BS + (ag + 1) * SUB] = dot(pick, native).astype(BF)
    first = jnp.broadcast_to(mask[:, 0:1], (NR, BS))
    mine[NR * BS :] = jnp.concatenate([first, jnp.zeros((8 - NR, BS), F32)], axis=0).astype(BF)


def merge_kernel(*refs):
    parts, (piece, copies, buf) = refs[:PIECES], refs[PIECES:]
    chip = lax.axis_index("chip")
    place = (chip >> 2) * 2 + ((chip & 3) >> 1)
    for p, part in zip((0, *SCATTER_ORDER), parts):

        @pl.when(place == p)
        def _():
            pltpu.sync_copy(part, buf)

    piece[...] = buf[: CPP * BS]
    for d in range(NW * 2):
        copies[d] = buf[CPP * BS :]


def wide_index():
    return lax.axis_index("chip") * 2 + lax.axis_index("core")


def arrivals(near, far):
    core = lax.axis_index("core")
    for ref, c in ((near, core), (far, 1 - core)):
        for zg in range(2):
            for p in range(PIECES):
                z = zg if p % 2 == 0 else 3 - zg
                yield 2 * zg + c, p, ref.at[(p >> 1) * 4 + z]


def panel_kernel(order, own, d1, d2, d3, near, far, w_ref, y_ref,
                 lown, lpiv, tpart, delta, mpiv, pan, tall, mk, mkp):
    w, q = wide_index(), lax.axis_index("narrow")
    rank, own_rank = ranks_of(order, w)
    for d, ref in enumerate((own, d1, d2, d3)):
        k = lax.rem(q - d + 4, 4)
        pan[k, 0 : NR * BS] = ref[0 : NR * BS]
        mk[k] = ref[NR * BS : NR * BS + 8].astype(F32)
    for i, p, tile in arrivals(near, far):
        row = pl.multiple_of(NR * BS + i * BS + p * SUB, SUB)
        for k in range(NP):
            pan[k, pl.ds(row, SUB), :] = tile[k, 0:SUB]
            if p == 0:
                mkp[i, k] = tile[k, SUB + 8 : SUB + 16].astype(F32)
    for i in range(NP):
        mpiv[i : i + 1] = mkp[i, q, 0:1].astype(jnp.int32)
    row_rank = [own_rank, None, None, None] + rank
    for s in range(NP):
        k = order[s]
        weight = w_ref[k]
        left = dot(pan[k], weight)
        parts = []
        for i in range(NR + NP):
            part = left[i * BS : (i + 1) * BS]
            if row_rank[i] is not None:
                part = jnp.where(row_rank[i] > s, part, 0.0)
            parts.append(part.astype(BF))
        lb = jnp.concatenate(parts, axis=0)
        lown[:, s * BS : (s + 1) * BS] = lb[: NR * BS]
        lpiv[s] = lb[NR * BS :]
        for t in range(s + 1, NP):
            j = order[t]
            akj = pan[j, pl.ds(pl.multiple_of(NR * BS + k * BS, BS), BS), :]
            prod = dot(lb, dot(weight, akj, 0, 0).astype(BF))
            for i in range(NR + NP):
                sl = slice(i * BS, (i + 1) * BS)
                m = mk[j, i : i + 1, :] if i < NR else mkp[i - NR, j, 0:1, 0:1]
                pan[j, sl] = (pan[j, sl].astype(F32) - m * prod[sl]).astype(BF)
    delta[...] = (own[0 : NR * BS].astype(F32) - pan[q, 0 : NR * BS].astype(F32)).astype(BF)
    y0 = jnp.where(w < NP, jnp.zeros_like(y_ref[0]), y_ref[0])
    y = jnp.concatenate([y0] + [y_ref[r] for r in range(1, NR)], axis=0)
    tall[...] = dot(y, lown[...], 0, 0)
    for j in range(2):
        mine_cols = tall[pl.ds(pl.multiple_of(j * BS + q * NW, NW), NW), :]
        for s in range(NP):
            tpart[:, s * 2 + j, :] = mine_cols[:, s * BS : (s + 1) * BS]


PAIRS = [(t, s) for s in range(NP) for t in range(s + 1, NP)]


def forward_kernel(order, near, far, w_ref, b_ref, lown, lpiv, zt, frhs, wl, bs, ztall):
    w, q = wide_index(), lax.axis_index("narrow")
    for r in range(NR):
        bs[r] = b_ref[r].astype(F32)
    for i, p, tile in arrivals(near, far):
        for n in range(4):
            r0 = p * SUB + 8 * (n >> 1)
            c0 = 128 * (n & 1)
            bs[NR + i, r0 : r0 + 8, c0 : c0 + 128] = tile[n, SUB : SUB + 8].astype(F32)
    for s in range(NP):
        k = order[s]
        weight = w_ref[k]
        bk = bs[NR + k].astype(BF)
        z = dot(weight, bk, 0, 0).astype(BF)
        ztall[...] = dot(bk, weight, 0, 0).astype(BF).astype(F32)
        for j in range(2):
            zt[s * 2 + j : s * 2 + j + 1] = ztall[pl.ds(j * BS + q * NW + w, 1), :]
        elim = dot(lown[:, s * BS : (s + 1) * BS], z)
        for i in range(NR):
            bs[i] = (bs[i] - elim[i * BS : (i + 1) * BS]).astype(BF).astype(F32)
        for t in range(s + 1, NP):
            i = order[t]
            low = lpiv[s, pl.ds(pl.multiple_of(i * BS, BS), BS), :]
            wl[PAIRS.index((t, s))] = dot(w_ref[i], low, 0, 0).astype(BF)
            elim = dot(low, z)
            bs[NR + i] = (bs[NR + i] - elim).astype(BF).astype(F32)
    for r in range(NR):
        frhs[r] = bs[r].astype(BF)


def solve_kernel(order, parts, zt, wl, w_ref, h, out, xs):
    total = jnp.sum(parts[...], axis=0)
    c = {}
    for s in reversed(range(NP)):
        acc = total[s * 2 : s * 2 + 2]
        for t in range(s + 1, NP):
            acc = acc + dot(c[t], wl[PAIRS.index((t, s))])
        c[s] = (zt[s * 2 : s * 2 + 2] - acc).astype(BF)
    for s in range(NP):
        k = order[s]
        xs[k] = dot(c[s], w_ref[k], 1, 1).astype(BF).astype(F32)
    x = jnp.concatenate([xs[i] for i in range(NP)], axis=0).astype(BF)
    for d in range(NW * 4):
        out[d] = x


def combine_kernel(order, lown, lpiv, w_ref, h):
    def low(t, s):
        return lpiv[s, pl.ds(pl.multiple_of(order[t] * BS, BS), BS), :]

    def right(coeff, s):
        return dot(coeff.astype(BF), w_ref[order[s]], 1, 1).astype(BF)

    base = [lown[:, s * BS : (s + 1) * BS].astype(F32) for s in range(NP)]
    r3 = right(base[3], 3)
    h[14] = r3
    r3_low = [dot(r3, low(3, s)) for s in range(3)]
    for m3 in range(2):
        c3 = [base[s] - r3_low[s] if m3 else base[s] for s in range(3)]
        r2 = right(c3[2], 2)
        h[12 + m3] = r2
        r2_low = [dot(r2, low(2, s)) for s in range(2)]
        for m2 in range(2):
            c2 = [c3[s] - r2_low[s] if m2 else c3[s] for s in range(2)]
            r1 = right(c2[1], 1)
            h[8 + m2 + 2 * m3] = r1
            r1_low = dot(r1, low(1, 0))
            for m1 in range(2):
                r0 = right(c2[0] - r1_low if m1 else c2[0], 0)
                h[m1 + 2 * m2 + 4 * m3] = r0


GC = 8


def update_kernel(order, mown, mpiv, a_ref, u_ref, h, delta, out):
    g = pl.program_id(0)
    rows = lax.broadcasted_iota(jnp.int32, (BS, BS), 0)
    cols = lax.broadcasted_iota(jnp.int32, (BS, BS), 1)
    perm = jnp.where((rows % GC) * SUB + rows // GC == cols, 1.0, 0.0).astype(BF)
    cols_out = []
    for col in range(GC):
        c = g * GC + col
        m1, m2, m3 = (mpiv[order[s], c] for s in range(1, NP))
        left = [h[m1 + 2 * m2 + 4 * m3], h[8 + m2 + 2 * m3], h[12 + m3], h[14]]
        p, cc = divmod(col, CPP)
        raw = []
        for s in range(NP):
            zg, core = order[s] >> 1, order[s] & 1
            z = zg if p == 0 else 3 - zg
            raw.append(u_ref[2 * z + core, cc * BS : (cc + 1) * BS])
        lu = dot(jnp.concatenate(left, axis=1), jnp.concatenate(raw, axis=0))
        parts = []
        for r in range(NR):
            parts.append(jnp.where(mown[r, c] != 0, lu[r * BS : (r + 1) * BS], 0.0).astype(BF))
        if col == 0:
            parts = [jnp.where(g == 0, delta[r * BS : (r + 1) * BS], parts[r]) for r in range(NR)]
        cols_out.append(parts)
    for r in range(NR):
        for ag in range(0, BS // SUB, 2):
            sls = [slice((ag + e) * SUB, (ag + e + 1) * SUB) for e in range(2)]
            stack = jnp.concatenate(
                [jnp.concatenate([cols_out[col][r][sl] for col in range(GC)], axis=0) for sl in sls], axis=1
            )
            change = dot(perm, stack)
            for e, sl in enumerate(sls):
                part = change[:, e * BS : (e + 1) * BS].reshape(SUB, GC, BS)
                out[r, sl] = (a_ref[r, sl].astype(F32) - part).astype(BF)


def vmem(n):
    return [pl.BlockSpec(memory_space=pltpu.VMEM)] * n


def smem(n):
    return [pl.BlockSpec(memory_space=pltpu.SMEM)] * n


def body(front, pivot_inverse, rhs, trail_sol, block_mask, panel_order):
    blocks = front.reshape(NR, BS, NC, BS)
    mask = block_mask.reshape(NR, NC)
    b = rhs.reshape(NR, BS, NRHS)
    y = trail_sol.reshape(NR, BS, NRHS)

    fixed = lambda shape: pl.BlockSpec(shape, lambda g: (0,) * len(shape))
    shapes = [(CPP * BS + EXTRA, BS)] * PIECES + [(NR * BS + 8, BS)]
    *sent, mine = pl.pallas_call(
        prep_kernel,
        out_shape=tuple(jax.ShapeDtypeStruct(shape, BF) for shape in shapes),
        grid=(1,),
        in_specs=[fixed((1, BS, NC, BS)), fixed((NR, BS, 8, BS)), fixed((1, BS, NRHS)), fixed((NR, NC))],
        out_specs=tuple(fixed(shape) for shape in shapes),
        name="prep",
    )(blocks, blocks, b, mask)

    pieces = []
    for p in SCATTER_ORDER:
        pieces.append(lax.ppermute(sent[p], WIDE, [(i, holder(p, i)) for i in range(NP)]))

    others = [lax.ppermute(mine, "narrow", [(i, (i + d) % 4) for i in range(4)]) for d in (1, 2, 3)]

    piece, copies = pl.pallas_call(
        merge_kernel,
        out_shape=(
            jax.ShapeDtypeStruct((CPP * BS, BS), BF),
            jax.ShapeDtypeStruct((NW * 2, EXTRA, BS), BF),
        ),
        in_specs=[pl.BlockSpec(memory_space=pl.ANY)] * PIECES,
        out_specs=tuple(vmem(2)),
        scratch_shapes=[pltpu.VMEM((CPP * BS + EXTRA, BS), BF)],
        name="merge",
    )(sent[0], *pieces)

    ugath = lax.all_gather(piece, WIDE)

    near = lax.all_to_all(copies, ("chip", "narrow"), 0, 0).reshape(NW // 2, 4, EXTRA, BS)
    far = lax.ppermute(near, "core", [(0, 1), (1, 0)])

    lown, lpiv, tpart, delta, mpiv = pl.pallas_call(
        panel_kernel,
        out_shape=(
            jax.ShapeDtypeStruct((NR * BS, NP * BS), BF),
            jax.ShapeDtypeStruct((NP, NP * BS, BS), BF),
            jax.ShapeDtypeStruct((NW, 8, BS), F32),
            jax.ShapeDtypeStruct((NR * BS, BS), BF),
            jax.ShapeDtypeStruct((NP, BS), jnp.int32),
        ),
        in_specs=smem(1) + vmem(8),
        out_specs=tuple(vmem(5)),
        scratch_shapes=[
            pltpu.VMEM((NP, (NR + NP) * BS, BS), BF),
            pltpu.VMEM((NRHS, NP * BS), F32),
            pltpu.VMEM((NP, 8, BS), F32),
            pltpu.VMEM((NP, NP, 8, BS), F32),
        ],
        name="panel",
    )(panel_order, mine, *others, near, far, pivot_inverse, y)

    zt, frhs, wl = pl.pallas_call(
        forward_kernel,
        out_shape=(
            jax.ShapeDtypeStruct((8, BS), F32),
            jax.ShapeDtypeStruct((NR, BS, NRHS), BF),
            jax.ShapeDtypeStruct((len(PAIRS), BS, BS), BF),
        ),
        in_specs=smem(1) + vmem(6),
        out_specs=tuple(vmem(3)),
        scratch_shapes=[
            pltpu.VMEM((NR + NP, BS, NRHS), F32),
            pltpu.VMEM((NRHS, BS), F32),
        ],
        name="forward",
    )(panel_order, near, far, pivot_inverse, b, lown, lpiv)

    h = pl.pallas_call(
        combine_kernel,
        out_shape=jax.ShapeDtypeStruct((15, NR * BS, BS), BF),
        in_specs=smem(1) + vmem(3),
        out_specs=vmem(1)[0],
        name="combine",
    )(panel_order, lown, lpiv, pivot_inverse)

    tparts = lax.all_to_all(tpart, WIDE, 0, 0)
    xg = pl.pallas_call(
        solve_kernel,
        out_shape=jax.ShapeDtypeStruct((NW * 4, 8, BS), BF),
        in_specs=smem(1) + vmem(4) + [pl.BlockSpec(memory_space=pl.ANY)],
        out_specs=vmem(1)[0],
        scratch_shapes=[pltpu.VMEM((NP, 2, BS), F32)],
        name="solve",
    )(panel_order, tparts, zt, wl, pivot_inverse, h)
    xall = lax.all_to_all(xg, ("narrow", *WIDE), 0, 0)

    front_out = pl.pallas_call(
        update_kernel,
        out_shape=jax.ShapeDtypeStruct((NR, BS, NC, BS), BF),
        grid=(NC // GC,),
        in_specs=smem(3)
        + [
            pl.BlockSpec((NR, BS, GC, BS), lambda g: (0, 0, g, 0)),
            pl.BlockSpec((8, CPP * BS, BS), lambda g: (g, 0, 0)),
            fixed((15, NR * BS, BS)),
            fixed((NR * BS, BS)),
        ],
        out_specs=pl.BlockSpec((NR, BS, GC, BS), lambda g: (0, 0, g, 0)),
        name="update",
    )(panel_order, mask, mpiv, blocks, ugath.reshape(NW, CPP * BS, BS), h, delta)
    front_out, xall = lax.optimization_barrier((front_out, xall))
    halves = xall.reshape(NW * 4, NP, 2, BS)
    window = jnp.concatenate([halves[:, :, j].transpose(1, 2, 0) for j in range(2)], axis=2)
    return front_out.reshape(front.shape), frhs.reshape(rhs.shape), window


def solution(mesh):
    in_specs = (
        P(None, WIDE, None, None, "narrow", None),
        P(),
        P(None, WIDE, None, None),
        P(None, WIDE, None, None),
        P(None, WIDE, None, "narrow"),
        P(),
    )
    out_specs = (P(None, WIDE, None, None, "narrow", None), P(None, WIDE, None, None), P())
    axes = {"chip": NW // 2, "core": 2, "narrow": 4}
    mesh = Mesh(mesh.devices.reshape(tuple(axes.values())), tuple(axes))

    def step(*args):
        return body(*args)

    step = jax.shard_map(step, mesh=mesh, in_specs=in_specs, out_specs=out_specs, check_vma=False)
    return step
```
